32 devices in a mesh: tok: 8 (over z, y), grp: 4 (over x, core).
Axes of the slice: x: 2, y: 2, z: 4, core: 2. Of those that a mesh axis runs over, the one named last changes fastest.
Arguments:
- tokens: bfloat16 [4, 8192, 768], P('grp', 'tok'), may hold values from -6 to 6
- upstream: bfloat16 [4, 8192, 768], P('grp', 'tok'), may hold values from -6 to 6
- cluster_pos: int32 [4, 12, 8192], P('grp', None, 'tok'), may hold values from 0 to 8191, as said below
- project_in: bfloat16 [768, 2304], P(('tok', 'grp')), may hold values from -0.21875 to 0.21875
- query_bias: bfloat16 [768], P(('tok', 'grp')), may hold values from -3 to 3
- value_bias: bfloat16 [768], P(('tok', 'grp')), may hold values from -3 to 3
- project_out: bfloat16 [768, 768], P(('tok', 'grp')), may hold values from -1.25 to 1.25
- output_bias: bfloat16 [768], P(('tok', 'grp')), may hold values from -2 to 2
- first_gain: bfloat16 [768], P(('tok', 'grp')), may hold values from 0.5 to 1.5
- first_shift: bfloat16 [768], P(('tok', 'grp')), may hold values from -2 to 2
- expand: bfloat16 [768, 3072], P(('tok', 'grp')), may hold values from -0.21875 to 0.21875
- expand_bias: bfloat16 [3072], P(('tok', 'grp')), may hold values from -2 to 2
- contract: bfloat16 [3072, 768], P(('tok', 'grp')), may hold values from -0.109375 to 0.109375
- contract_bias: bfloat16 [768], P(('tok', 'grp')), may hold values from -2 to 2
- second_gain: bfloat16 [768], P(('tok', 'grp')), may hold values from 0.5 to 1.5
- second_shift: bfloat16 [768], P(('tok', 'grp')), may hold values from -2 to 2
Outputs:
- activations: bfloat16 [4, 8192, 768], P('grp', 'tok')
- token_grad: float32 [4, 8192, 768], P('grp', 'tok')
- project_in_grad: float32 [768, 2304], P(('tok', 'grp'))
- query_bias_grad: float32 [768], P(('tok', 'grp'))
- value_bias_grad: float32 [768], P(('tok', 'grp'))
- project_out_grad: float32 [768, 768], P(('tok', 'grp'))
- output_bias_grad: float32 [768], P(('tok', 'grp'))
- first_gain_grad: float32 [768], P(('tok', 'grp'))
- first_shift_grad: float32 [768], P(('tok', 'grp'))
- expand_grad: float32 [768, 3072], P(('tok', 'grp'))
- expand_bias_grad: float32 [3072], P(('tok', 'grp'))
- contract_grad: float32 [3072, 768], P(('tok', 'grp'))
- contract_bias_grad: float32 [768], P(('tok', 'grp'))
- second_gain_grad: float32 [768], P(('tok', 'grp'))
- second_shift_grad: float32 [768], P(('tok', 'grp'))
The draws below stay inside these ranges and needn't reach their ends.
Inputs may be any that keep to these rules, and one draw needn't show every extreme that they name: `cluster_pos`: positions of one group and head form a permutation of the group's rows that maps each aligned block of 4096 rows onto itself. A block is either one sequence of 4096 tokens, in which every device of the block sends exactly 256 of its rows to every device of the block, itself included, or 8 sequences of 512 tokens, each permuted within itself. Each group has 2 blocks; on this slice both are of the first kind. Every cluster holds tokens of one sequence.
All inputs are finite; a program needn't handle non-finite values.
Results may differ from the reference program's by a relative error of at most 0.013.
Values may be sent and summed in bfloat16 or wider, within the bound.
A program may use at most 192 MiB of HBM per device.

```python
import jax
import jax.numpy as jnp
from jax import lax

D = 768
HEADS = 12
FF = 3072
CL = 128
LONG = 4096
SHORT = 512
TOK_DEV = 1024
TOK_GROUP = 8192
N_GRP = 4


def draw_cluster_pos(key, part):
    span = LONG // TOK_DEV
    share = TOK_DEV // span
    blocks = TOK_GROUP // LONG
    pieces = LONG // SHORT
    kind_key, source_key, target_key, short_key = jax.random.split(key, 4)
    tossed = jax.random.randint(kind_key, (N_GRP, blocks), 0, 2, dtype=jnp.int32)
    block_index = jnp.arange(blocks, dtype=jnp.int32)[None, :]
    kinds = jnp.where(block_index < blocks - blocks // 4, 1, tossed)
    count = N_GRP * HEADS * blocks * span
    source_perm = jax.vmap(lambda sub: jax.random.permutation(sub, TOK_DEV))(jax.random.split(source_key, count))
    source_perm = source_perm.astype(jnp.int32).reshape(N_GRP, HEADS, blocks, span, TOK_DEV)
    target_perm = jax.vmap(lambda sub: jax.random.permutation(sub, TOK_DEV))(jax.random.split(target_key, count))
    target_flat = target_perm.astype(jnp.int32).reshape(N_GRP, HEADS, blocks, span * TOK_DEV)
    target_dev = source_perm // share
    inbound = source_perm % share
    sender = jnp.arange(span, dtype=jnp.int32)[:, None]
    lookup = target_dev * TOK_DEV + sender * share + inbound
    slot = jnp.take_along_axis(target_flat, lookup.reshape(N_GRP, HEADS, blocks, span * TOK_DEV), axis=3)
    long_pos = target_dev.reshape(N_GRP, HEADS, blocks, LONG) * TOK_DEV + slot
    short_count = N_GRP * HEADS * blocks * pieces
    short_perm = jax.vmap(lambda sub: jax.random.permutation(sub, SHORT))(jax.random.split(short_key, short_count))
    short_perm = short_perm.astype(jnp.int32).reshape(N_GRP, HEADS, blocks, pieces, SHORT)
    short_pos = (short_perm + jnp.arange(pieces, dtype=jnp.int32)[:, None] * SHORT).reshape(N_GRP, HEADS, blocks, LONG)
    chosen = jnp.where((kinds > 0)[:, None, :, None], long_pos, short_pos)
    chosen = chosen + (jnp.arange(blocks, dtype=jnp.int32) * LONG)[None, None, :, None]
    return chosen.reshape(N_GRP, HEADS, TOK_GROUP).astype(jnp.int32)


def block_levels(key, shape, cuts, low, largest):
    factor_of = 1.0
    for position, parts in cuts:
        steps = jax.random.uniform(jax.random.fold_in(jax.random.fold_in(key, 6), position), (parts,), jnp.float32, low / len(cuts), largest / len(cuts))
        factor_of = factor_of * jnp.repeat(jnp.exp(steps), shape[position] // parts).reshape((-1,) + (1,) * (len(shape) - 1 - position))
    return factor_of


def noise(rng, dims, scale, bound, cuts=(), kind=jnp.bfloat16):
    level = block_levels(rng, dims, cuts, -0.22, 0.18) if cuts else 1.0
    values = jax.random.normal(rng, dims, jnp.float32) * scale * level
    return jnp.minimum(jnp.maximum(values, -bound), bound).astype(kind)


def setup_inputs(seed: int = 0) -> dict:
    arg_keys = jax.random.split(jax.random.key(seed), 17)
    return {
        "tokens": noise(arg_keys[0], (N_GRP, TOK_GROUP, D), 1.0, 6.0, ((0, 4), (1, 8))),
        "upstream": noise(arg_keys[1], (N_GRP, TOK_GROUP, D), 1.0, 6.0, ((0, 4), (1, 8))),
        "cluster_pos": draw_cluster_pos(jax.random.fold_in(arg_keys[16], 71), 0),
        "project_in": noise(arg_keys[3], (D, 3 * D), D ** -0.5, 0.21875, ((0, 32),)),
        "query_bias": noise(arg_keys[4], (D,), 0.5, 3.0, ((0, 32),)),
        "value_bias": noise(arg_keys[5], (D,), 0.5, 3.0, ((0, 32),)),
        "project_out": noise(arg_keys[6], (D, D), (D // 32) ** -0.5, 1.25, ((0, 32),)),
        "output_bias": noise(arg_keys[7], (D,), 0.3, 2.0, ((0, 32),)),
        "first_gain": jnp.clip(1.0 + 0.1 * jax.random.normal(arg_keys[8], (D,), jnp.float32), 0.5, 1.5).astype(jnp.bfloat16),
        "first_shift": noise(arg_keys[9], (D,), 0.3, 2.0, ((0, 32),)),
        "expand": noise(arg_keys[10], (D, FF), D ** -0.5, 0.21875, ((0, 32),)),
        "expand_bias": noise(arg_keys[11], (FF,), 0.3, 2.0, ((0, 32),)),
        "contract": noise(arg_keys[12], (FF, D), FF ** -0.5, 0.109375, ((0, 32),)),
        "contract_bias": noise(arg_keys[13], (D,), 0.3, 2.0, ((0, 32),)),
        "second_gain": jnp.clip(1.0 + 0.1 * jax.random.normal(arg_keys[14], (D,), jnp.float32), 0.5, 1.5).astype(jnp.bfloat16),
        "second_shift": noise(arg_keys[15], (D,), 0.3, 2.0, ((0, 32),)),
    }


@jax.custom_vjp
def low(v):
    return lax.optimization_barrier(v.astype(jnp.bfloat16)).astype(jnp.float32)

@jax.custom_vjp
def low_back(v):
    return v

def low_keep(v):
    return (low(v), None)

def low_pass(kept, grad):
    return (grad,)

def back_keep(v):
    return (v, None)

def back_low(kept, grad):
    return (low(grad),)
low.defvjp(low_keep, low_pass)
low_back.defvjp(back_keep, back_low)
epsilon = 1e-05
highest = lax.Precision.HIGHEST

def product(left, right):
    return jnp.dot(left, right, preferred_element_type=jnp.float32, precision=highest)

def normalize(hidden, gain, shift):
    centred = hidden - lax.optimization_barrier(jnp.mean(hidden, axis=1, keepdims=True))
    inverse_std = lax.rsqrt(lax.optimization_barrier(jnp.mean(centred * centred, axis=1, keepdims=True)) + epsilon)
    return centred * inverse_std * gain + shift

def layer(params, inputs, placed):
    project_in, query_bias, value_bias, project_out, output_bias, first_gain, first_shift, expand, expand_bias, contract, contract_bias, second_gain, second_shift = params
    heads = placed.shape[0]
    count, width = inputs.shape
    head_dim = width // heads
    scale = head_dim ** (-0.5)
    bias_all = jnp.concatenate([query_bias, jnp.zeros_like(query_bias), value_bias])
    joined = low_back(low(product(inputs, project_in) + bias_all))
    per_head = joined.reshape(count, 3, heads, head_dim).transpose(2, 0, 1, 3).reshape(heads, count, 3 * head_dim)
    lanes = jnp.arange(heads, dtype=jnp.int32)[:, None]
    inverse = jnp.zeros((heads, count), jnp.int32).at[lanes, placed].set(jnp.broadcast_to(jnp.arange(count, dtype=jnp.int32)[None, :], (heads, count)))
    ordered = jnp.take_along_axis(per_head, inverse[:, :, None], axis=1)
    grouped = ordered.reshape(heads, count // CL, CL, 3 * head_dim)
    query = grouped[..., :head_dim]
    keys = grouped[..., head_dim:2 * head_dim]
    values = grouped[..., 2 * head_dim:]
    scores = low_back(jnp.einsum('hcqd,hckd->hcqk', query, keys, precision=highest) * scale)
    probs = jax.nn.softmax(scores, axis=-1)
    attended = jnp.einsum('hcqk,hckd->hcqd', low(probs), values, precision=highest).reshape(heads, count, head_dim)
    returned = jnp.take_along_axis(attended, placed[:, :, None], axis=1)
    merged = low_back(low(returned.transpose(1, 0, 2).reshape(count, width)))
    branch = low_back(product(merged, project_out) + output_bias)
    normed_one = normalize(inputs + branch, first_gain, first_shift)
    inner = low_back(product(low(normed_one), expand) + expand_bias)
    lifted = low(jax.nn.gelu(inner, approximate=False))
    second = low_back(product(lifted, contract) + contract_bias)
    return normalize(normed_one + second, second_gain, second_shift)

def reference(tokens, upstream, cluster_pos, project_in, query_bias, value_bias, project_out, output_bias, first_gain, first_shift, expand, expand_bias, contract, contract_bias, second_gain, second_shift):
    params = tuple((item.astype(jnp.float32) for item in (project_in, query_bias, value_bias, project_out, output_bias, first_gain, first_shift, expand, expand_bias, contract, contract_bias, second_gain, second_shift)))
    groups, group_rows, width = tokens.shape
    heads = cluster_pos.shape[1]
    blocks = group_rows // LONG
    inputs_all = tokens.astype(jnp.float32).reshape(groups * blocks, LONG, width)
    upstream_all = upstream.astype(jnp.float32).reshape(groups * blocks, LONG, width)
    placed_all = cluster_pos.reshape(groups, heads, blocks, LONG).transpose(0, 2, 1, 3).reshape(groups * blocks, heads, LONG)
    starts = jnp.tile(jnp.arange(blocks, dtype=jnp.int32) * LONG, groups)
    placed_all = placed_all - starts[:, None, None]

    def visit(totals, item):
        inputs, cotangent, placed = item
        result, pullback = jax.vjp(lambda weights, rows_in: layer(weights, rows_in, placed), params, inputs)
        grad_params, grad_inputs = pullback(cotangent)
        totals = tuple((total + grad for total, grad in zip(totals, grad_params)))
        return (totals, (result, grad_inputs))
    zeros = tuple((jnp.zeros(item.shape, jnp.float32) for item in params))
    totals, (results, grads) = lax.scan(visit, zeros, (inputs_all, upstream_all, placed_all))
    activations = results.reshape(groups, group_rows, width).astype(jnp.bfloat16)
    token_grad = grads.reshape(groups, group_rows, width)
    return (activations, token_grad, totals[0], totals[1], totals[2], totals[3], totals[4], totals[5], totals[6], totals[7], totals[8], totals[9], totals[10], totals[11], totals[12])
```

```python
import jax
import jax.numpy as jnp
from jax import lax
from jax.experimental import pallas as pl
from jax.experimental.pallas import tpu as pltpu
from jax.sharding import PartitionSpec as P

CL = 128
LONG = 4096
F32 = jnp.float32
BF = jnp.bfloat16
VMEM_ALL = 64 * 1024 * 1024 - 65536

epsilon = 1e-05
root_half = 0.7071067811865476
density_norm = 0.3989422804014327

def normalize(hidden, gain, shift):
    centred = hidden - jnp.mean(hidden, axis=1, keepdims=True)
    inverse_std = lax.rsqrt(jnp.mean(centred * centred, axis=1, keepdims=True) + epsilon)
    unit = centred * inverse_std
    return (unit * gain + shift, unit, inverse_std)


def normalize_back(grad_out, gain, unit, inverse_std):
    scaled = grad_out * gain
    return inverse_std * (
        scaled
        - jnp.mean(scaled, axis=1, keepdims=True)
        - unit * jnp.mean(scaled * unit, axis=1, keepdims=True)
    )


def nt(a,b): return lax.dot_general(a,b,(((1,),(1,)),((),())),preferred_element_type=F32)
def nn(a,b): return lax.dot_general(a,b,(((1,),(0,)),((),())),preferred_element_type=F32)
def tn(a,b): return lax.dot_general(a,b,(((0,),(0,)),((),())),preferred_element_type=F32)

def fwd_kernel(pos, tok, w, bias, att, left, right, src, ord_, oc):
    h=pl.program_id(0)
    n=tok.shape[0]
    ch=512
    def proj(i,_):
        r=pl.multiple_of(i*ch,ch)
        acc=nn(tok[pl.ds(r,ch),:],w[...])+bias[0]
        src[pl.ds(2*r,ch,stride=2),:]=acc[:,:128]
        src[pl.ds(2*r+1,ch,stride=2),:]=acc[:,128:]
        return 0
    lax.fori_loop(0,n//ch,proj,0)
    U=64
    def scat(i,_):
        for u in range(U):
            t=i*U+u
            ord_[pl.ds(2*pos[h*n+t],2),:]=src[pl.ds(2*t,2),:]
        return 0
    lax.fori_loop(0,n//U,scat,0)
    CB=4
    def clus(i,_):
        for u in range(CB):
            r=pl.multiple_of((i*CB+u)*CL,CL)
            l=ord_[pl.ds(2*r,CL,stride=2),:].astype(BF)
            rr=ord_[pl.ds(2*r+1,CL,stride=2),:].astype(BF)
            left[0,pl.ds(r,CL),:]=l
            right[0,pl.ds(r,CL),:]=rr
            s=nt(rr,l)
            m=jnp.max(s,axis=0,keepdims=True)
            e=jnp.exp((s-m)*0.125)
            p=(e*(1.0/jnp.sum(e,axis=0,keepdims=True))).astype(BF)
            oc[pl.ds(r,CL),:]=tn(p,rr)
        return 0
    lax.fori_loop(0,n//CL//CB,clus,0)
    def gath(i,_):
        for u in range(U):
            t=i*U+u
            src[pl.ds(t,1),:]=oc[pl.ds(pos[h*n+t],1),:]
        return 0
    lax.fori_loop(0,n//U,gath,0)
    att[0]=src[pl.ds(0,n),:].astype(BF)

def fwd(pos,tok,w,bias):
    n=tok.shape[0]; H=pos.shape[0]//n
    return pl.pallas_call(fwd_kernel,grid=(H,),
      out_shape=(jax.ShapeDtypeStruct((H,n,128),BF),)*3,
      in_specs=[pl.BlockSpec(memory_space=pltpu.SMEM),
                pl.BlockSpec((n,tok.shape[1]),lambda h:(0,0)),
                pl.BlockSpec((tok.shape[1],256),lambda h:(0,h)),
                pl.BlockSpec((1,1,256),lambda h: (h, 0, 0))],
      out_specs=(pl.BlockSpec((1,n,128),lambda h: (h, 0, 0)),)*3,
      scratch_shapes=[pltpu.VMEM((2*n,128),F32),pltpu.VMEM((2*n,128),F32),pltpu.VMEM((n,128),F32)],
      compiler_params=pltpu.CompilerParams(vmem_limit_bytes=VMEM_ALL),name="att_fwd")(pos,tok,w,bias)

def bwd_kernel(pos, left, right, g, gj, src, ord_, dc):
    h=pl.program_id(0)
    n=g.shape[1]
    U=64
    src[pl.ds(0,n),:]=g[0].astype(F32)
    def scat(i,_):
        for u in range(U):
            t=i*U+u
            ord_[pl.ds(pos[h*n+t],1),:]=src[pl.ds(t,1),:]
        return 0
    lax.fori_loop(0,n//U,scat,0)
    lane=lax.broadcasted_iota(jnp.int32,(CL,128),1)
    mask=(lane<64)==(h==0)
    CB=4
    def clus(i,_):
        for u in range(CB):
            r=pl.multiple_of((i*CB+u)*CL,CL)
            l=left[0,pl.ds(r,CL),:]
            rr=right[0,pl.ds(r,CL),:]
            d=jnp.where(mask,ord_[pl.ds(r,CL),:],0.0).astype(BF)
            s=nt(rr,l)
            m=jnp.max(s,axis=0,keepdims=True)
            e=jnp.exp((s-m)*0.125)
            p=e*(1.0/jnp.sum(e,axis=0,keepdims=True))
            dp=nt(rr,d)
            rd=jnp.sum(dp*p,axis=0,keepdims=True)
            ds=(p*(dp-rd)).astype(BF)
            dl=tn(ds,rr)*0.125
            dr=nn(ds,l)*0.125+nn(p.astype(BF),d)
            dc[pl.ds(2*r,CL,stride=2),:]=dl
            dc[pl.ds(2*r+1,CL,stride=2),:]=dr
        return 0
    lax.fori_loop(0,n//CL//CB,clus,0)
    def gath(i,_):
        for u in range(U):
            t=i*U+u
            src[pl.ds(2*t,2),:]=dc[pl.ds(2*pos[h*n+t],2),:]
        return 0
    lax.fori_loop(0,n//U,gath,0)
    ch=512
    def out(i,_):
        r=pl.multiple_of(i*ch,ch)
        gj[0,pl.ds(r,ch),:128]=src[pl.ds(2*r,ch,stride=2),:].astype(BF)
        gj[0,pl.ds(r,ch),128:]=src[pl.ds(2*r+1,ch,stride=2),:].astype(BF)
        return 0
    lax.fori_loop(0,n//ch,out,0)

def bwd(pos,left,right,g):
    n=g.shape[1]; H=left.shape[0]
    blk=lambda: pl.BlockSpec((1,n,128),lambda h: (h, 0, 0))
    return pl.pallas_call(bwd_kernel,grid=(H,),
      out_shape=jax.ShapeDtypeStruct((H,n,256),BF),
      in_specs=[pl.BlockSpec(memory_space=pltpu.SMEM),blk(),blk(),pl.BlockSpec((1,n,128),lambda h: (h // 2, 0, 0))],
      out_specs=pl.BlockSpec((1,n,256),lambda h: (h, 0, 0)),
      scratch_shapes=[pltpu.VMEM((2*n,128),F32),pltpu.VMEM((n,128),F32),pltpu.VMEM((2*n,128),F32)],
      compiler_params=pltpu.CompilerParams(vmem_limit_bytes=VMEM_ALL),name="att_bwd")(pos,left,right,g)

def flip(block, mask):
    count = lax.axis_size("tok")
    return lax.ppermute(block, "tok", [(i, i ^ mask) for i in range(count)])


def gather_all(item):
    return lax.all_gather(item, ("tok", "grp"), axis=0, tiled=True)


def scatter_sum(item):
    return lax.psum_scatter(item, ("tok", "grp"), scatter_dimension=0, tiled=True)


def shards(
    tokens,
    upstream,
    cluster_pos,
    project_in,
    query_bias,
    value_bias,
    project_out,
    output_bias,
    first_gain,
    first_shift,
    expand,
    expand_bias,
    contract,
    contract_bias,
    second_gain,
    second_shift,
):
    inputs = tokens[0]
    count, width = inputs.shape
    positions = cluster_pos[0] % LONG
    heads = positions.shape[0]
    head_dim = width // heads
    span = LONG // count
    mine = heads // span
    offset = lax.axis_index("tok") % span
    total = span * count

    near = flip(inputs, 1)
    far = flip(jnp.stack([inputs, near]), 2)
    block = jnp.concatenate([inputs[None], near[None], far]).reshape(total, width)
    near_at = flip(positions, 1)
    far_at = flip(jnp.stack([positions, near_at]), 2)
    block_at = jnp.concatenate([positions[None], near_at[None], far_at])
    own_at = lax.dynamic_slice_in_dim(block_at, offset * mine, mine, axis=1)
    own_at = own_at.transpose(1, 0, 2).reshape(-1)

    project_in = gather_all(project_in)
    project_out = gather_all(project_out)
    expand = gather_all(expand)
    contract = gather_all(contract)
    packed = jnp.concatenate(
        [
            query_bias, value_bias, output_bias, first_gain, first_shift,
            contract_bias, second_gain, second_shift, expand_bias,
        ]
    )
    few = query_bias.shape[0]
    packed = gather_all(packed[None].astype(F32))
    vectors = [packed[:, i * few : (i + 1) * few].reshape(-1) for i in range(8)]
    query_bias, value_bias, output_bias, gain_one, shift_one, contract_bias, gain_two, shift_two = vectors
    expand_bias = packed[:, 8 * few :].reshape(-1)

    pieces = lax.dynamic_slice_in_dim(
        project_in.reshape(width, 3, heads, head_dim), offset * mine, mine, axis=2
    )
    hollow = jnp.zeros((width, head_dim), BF)
    columns = []
    for h in range(mine):
        query, key, value = pieces[:, 0, h], pieces[:, 1, h], pieces[:, 2, h]
        columns += [hollow, query, value, key] if h == 0 else [query, hollow, key, value]
    arranged = jnp.concatenate(columns, axis=1)
    own_query = lax.dynamic_slice_in_dim(query_bias.reshape(heads, head_dim), offset * mine, mine)
    own_value = lax.dynamic_slice_in_dim(value_bias.reshape(heads, head_dim), offset * mine, mine)
    blank = jnp.zeros((head_dim,), F32)
    rows = []
    for h in range(mine):
        parts = [blank, own_query[h], own_value[h], blank] if h == 0 else [own_query[h], blank, blank, own_value[h]]
        rows.append(jnp.concatenate(parts))
    bias_rows = jnp.stack(rows)[:, None]

    att, left, right = fwd(own_at, block, arranged, bias_rows)
    lane = jnp.arange(2 * head_dim) < head_dim
    pair = jnp.where(lane, att[0], att[1]).reshape(span, count, 2 * head_dim)
    single = att[2, :, head_dim:].reshape(span, 2, count // 2, head_dim)
    single = single.transpose(0, 2, 1, 3).reshape(span, count // 2, 2 * head_dim)
    leaving = jnp.concatenate([pair, single], axis=1)
    came = [leaving[0]] + [flip(leaving[k], k) for k in range(1, span)]

    def open_single(item):
        return jnp.concatenate([item[:, :head_dim], item[:, head_dim:]], axis=0)

    merged = jnp.concatenate(
        [item[:count] for item in came] + [open_single(item[count:]) for item in came], axis=1
    )
    by_owner = project_out.reshape(span, mine * head_dim, width)
    turned = [lax.dynamic_index_in_dim(by_owner, offset ^ k, 0, False) for k in range(span)]
    project_turned = jnp.concatenate(
        [item[: 2 * head_dim] for item in turned] + [item[2 * head_dim :] for item in turned], axis=0
    )

    branch = jnp.dot(merged, project_turned, preferred_element_type=F32) + output_bias
    normed_one, unit_one, inverse_one = normalize(inputs.astype(F32) + branch, gain_one, shift_one)
    normed_low = normed_one.astype(BF)
    inner = jnp.dot(normed_low, expand, preferred_element_type=F32) + expand_bias
    lifted = jax.nn.gelu(inner, approximate=False).astype(BF)
    second_sum = normed_one + jnp.dot(lifted, contract, preferred_element_type=F32) + contract_bias
    result, unit_two, inverse_two = normalize(second_sum, gain_two, shift_two)
    cotangent = upstream[0].astype(F32)
    second_gain_grad = jnp.sum(cotangent * unit_two, axis=0)
    second_shift_grad = jnp.sum(cotangent, axis=0)
    grad_second = normalize_back(cotangent, gain_two, unit_two, inverse_two)
    grad_mid = grad_second.astype(BF)
    contract_bias_grad = jnp.sum(grad_mid.astype(F32), axis=0)
    contract_grad = jnp.einsum("rf,rd->fd", lifted, grad_mid, preferred_element_type=F32)
    grad_lifted = jnp.einsum("rd,fd->rf", grad_mid, contract, preferred_element_type=F32)
    slope = (
        0.5 * (1.0 + lax.erf(inner * root_half))
        + inner * jnp.exp(-0.5 * inner * inner) * density_norm
    )
    grad_inner = (grad_lifted * slope).astype(BF)
    expand_bias_grad = jnp.sum(grad_inner.astype(F32), axis=0)
    expand_grad = jnp.einsum("rd,rf->df", normed_low, grad_inner, preferred_element_type=F32)
    grad_normed = grad_second + jnp.einsum(
        "rf,df->rd", grad_inner, expand, preferred_element_type=F32
    )
    first_gain_grad = jnp.sum(grad_normed * unit_one, axis=0)
    first_shift_grad = jnp.sum(grad_normed, axis=0)
    grad_first = normalize_back(grad_normed, gain_one, unit_one, inverse_one)
    grad_branch = grad_first.astype(BF)
    output_bias_grad = jnp.sum(grad_branch.astype(F32), axis=0)
    turned_grad = jnp.einsum("rd,re->de", merged, grad_branch, preferred_element_type=F32)
    grad_merged = jnp.einsum(
        "re,de->rd", grad_branch, project_turned, preferred_element_type=F32
    ).astype(BF)

    pair_cols = span * 2 * head_dim
    sending = []
    for k in range(span):
        two = grad_merged[:, k * 2 * head_dim : (k + 1) * 2 * head_dim]
        one = grad_merged[:, pair_cols + k * head_dim : pair_cols + (k + 1) * head_dim]
        one = jnp.concatenate([one[: count // 2], one[count // 2 :]], axis=1)
        sending.append(jnp.concatenate([two, one], axis=0))
    landed = [sending[0]] + [flip(sending[k], k) for k in range(1, span)]
    grad_pair = jnp.concatenate([item[:count] for item in landed], axis=0)
    grad_single = jnp.concatenate([open_single(item[count:]) for item in landed], axis=0)
    grad_att = jnp.stack([grad_pair, jnp.concatenate([grad_single, grad_single], axis=1)])
    grad_rows = bwd(own_at, left, right, grad_att)

    arranged_grad = jnp.concatenate(
        [jnp.einsum("rd,re->de", block, grad_rows[h], preferred_element_type=F32) for h in range(mine)],
        axis=1,
    ).reshape(width, mine, 4, head_dim)
    sums = jnp.sum(grad_rows.astype(F32), axis=1).reshape(mine, 4, head_dim)
    query_at = [1] + [0] * (mine - 1)
    key_at = [3] + [2] * (mine - 1)
    value_at = [2] + [3] * (mine - 1)

    def spread(take, at):
        return jnp.stack([take(h, at[h]) for h in range(mine)], axis=-2)

    own_grad = jnp.stack(
        [spread(lambda h, s: arranged_grad[:, h, s], at) for at in (query_at, key_at, value_at)], axis=1
    )
    project_in_grad = lax.dynamic_update_slice_in_dim(
        jnp.zeros((width, 3, heads, head_dim), F32), own_grad, offset * mine, axis=2
    ).reshape(width, 3 * width)
    own_sums = jnp.stack([spread(lambda h, s: sums[h, s], at) for at in (query_at, value_at)])
    bias_grads = lax.dynamic_update_slice_in_dim(
        jnp.zeros((2, heads, head_dim), F32), own_sums, offset * mine, axis=1
    ).reshape(2, width)
    partial = sum(
        jnp.einsum(
            "re,de->rd", grad_rows[h], arranged[:, 256 * h : 256 * h + 256], preferred_element_type=F32
        )
        for h in range(mine)
    ).reshape(span, count, width)
    token_grad = grad_first + partial[0]
    for k in range(1, span):
        token_grad = token_grad + flip(partial[k].astype(BF), k).astype(F32)

    by_owner = jnp.concatenate(
        [
            turned_grad[:pair_cols].reshape(span, 2 * head_dim, width),
            turned_grad[pair_cols:].reshape(span, head_dim, width),
        ],
        axis=1,
    )
    project_out_grad = jnp.concatenate(
        [lax.dynamic_index_in_dim(by_owner, offset ^ k, 0, False) for k in range(span)], axis=0
    )
    project_in_grad = scatter_sum(project_in_grad.astype(BF)).astype(F32)
    project_out_grad = scatter_sum(project_out_grad.astype(BF)).astype(F32)
    expand_grad = scatter_sum(expand_grad.astype(BF)).astype(F32)
    contract_grad = scatter_sum(contract_grad.astype(BF)).astype(F32)
    devices = lax.axis_size("tok") * lax.axis_size("grp")
    small = jnp.concatenate(
        [
            item.reshape(devices, -1)
            for item in (
                bias_grads[0], bias_grads[1], output_bias_grad, first_gain_grad, first_shift_grad,
                contract_bias_grad, second_gain_grad, second_shift_grad, expand_bias_grad,
            )
        ],
        axis=1,
    )
    small = scatter_sum(small)[0]
    each = [small[i * few : (i + 1) * few] for i in range(8)] + [small[8 * few :]]
    return (
        result.astype(BF)[None],
        token_grad[None],
        project_in_grad,
        each[0],
        each[1],
        project_out_grad,
        each[2],
        each[3],
        each[4],
        expand_grad,
        each[8],
        contract_grad,
        each[5],
        each[6],
        each[7],
    )


def solution(mesh):
    placed = (
        P("grp", "tok", None),
        P("grp", "tok", None),
        P("grp", None, "tok"),
        P(("tok", "grp"), None),
        P(("tok", "grp")),
        P(("tok", "grp")),
        P(("tok", "grp"), None),
        P(("tok", "grp")),
        P(("tok", "grp")),
        P(("tok", "grp")),
        P(("tok", "grp"), None),
        P(("tok", "grp")),
        P(("tok", "grp"), None),
        P(("tok", "grp")),
        P(("tok", "grp")),
        P(("tok", "grp")),
    )
    return jax.shard_map(
        shards,
        mesh=mesh,
        in_specs=placed,
        out_specs=(
            P("grp", "tok", None),
            P("grp", "tok", None),
            P(("tok", "grp"), None),
            P(("tok", "grp")),
            P(("tok", "grp")),
            P(("tok", "grp"), None),
            P(("tok", "grp")),
            P(("tok", "grp")),
            P(("tok", "grp")),
            P(("tok", "grp"), None),
            P(("tok", "grp")),
            P(("tok", "grp"), None),
            P(("tok", "grp")),
            P(("tok", "grp")),
            P(("tok", "grp")),
        ),
        check_vma=False,
    )
```

```python
import functools
import jax
import jax.numpy as jnp
from jax import lax
from jax.experimental import pallas as pl
from jax.experimental.pallas import tpu as pltpu
from jax.sharding import PartitionSpec as P

CL = 128
LONG = 4096
F32 = jnp.float32
BF = jnp.bfloat16
VMEM_ALL = 64 * 1024 * 1024 - 65536

epsilon = 1e-05
root_half = 0.7071067811865476
density_norm = 0.3989422804014327

def normalize(hidden, gain, shift):
    centred = hidden - jnp.mean(hidden, axis=1, keepdims=True)
    inverse_std = lax.rsqrt(jnp.mean(centred * centred, axis=1, keepdims=True) + epsilon)
    unit = centred * inverse_std
    return (unit * gain + shift, unit, inverse_std)


def normalize_back(grad_out, gain, unit, inverse_std):
    scaled = grad_out * gain
    return inverse_std * (
        scaled
        - jnp.mean(scaled, axis=1, keepdims=True)
        - unit * jnp.mean(scaled * unit, axis=1, keepdims=True)
    )


def nt(a,b): return lax.dot_general(a,b,(((1,),(1,)),((),())),preferred_element_type=F32)
def nn(a,b): return lax.dot_general(a,b,(((1,),(0,)),((),())),preferred_element_type=F32)
def tn(a,b): return lax.dot_general(a,b,(((0,),(0,)),((),())),preferred_element_type=F32)

def fwd_kernel(pos, tok, w, bias, att, left, right, src, ord_, oc):
    h=pl.program_id(0)
    n=tok.shape[0]
    ch=512
    def proj(i,_):
        r=pl.multiple_of(i*ch,ch)
        acc=nn(tok[pl.ds(r,ch),:],w[...])+bias[0]
        src[pl.ds(2*r,ch,stride=2),:]=acc[:,:128]
        src[pl.ds(2*r+1,ch,stride=2),:]=acc[:,128:]
        return 0
    lax.fori_loop(0,n//ch,proj,0)
    U=64
    def scat(i,_):
        for u in range(U):
            t=i*U+u
            ord_[pl.ds(2*pos[h*n+t],2),:]=src[pl.ds(2*t,2),:]
        return 0
    lax.fori_loop(0,n//U,scat,0)
    CB=4
    def clus(i,_):
        for u in range(CB):
            r=pl.multiple_of((i*CB+u)*CL,CL)
            l=ord_[pl.ds(2*r,CL,stride=2),:].astype(BF)
            rr=ord_[pl.ds(2*r+1,CL,stride=2),:].astype(BF)
            left[0,pl.ds(r,CL),:]=l
            right[0,pl.ds(r,CL),:]=rr
            s=nt(rr,l)
            m=jnp.max(s,axis=0,keepdims=True)
            e=jnp.exp((s-m)*0.125)
            p=(e*(1.0/jnp.sum(e,axis=0,keepdims=True))).astype(BF)
            oc[pl.ds(r,CL),:]=tn(p,rr)
        return 0
    lax.fori_loop(0,n//CL//CB,clus,0)
    def gath(i,_):
        for u in range(U):
            t=i*U+u
            src[pl.ds(t,1),:]=oc[pl.ds(pos[h*n+t],1),:]
        return 0
    lax.fori_loop(0,n//U,gath,0)
    att[0]=src[pl.ds(0,n),:].astype(BF)

def fwd(pos,tok,w,bias):
    n=tok.shape[0]; H=pos.shape[0]//n
    return pl.pallas_call(fwd_kernel,grid=(H,),
      out_shape=(jax.ShapeDtypeStruct((H,n,128),BF),)*3,
      in_specs=[pl.BlockSpec(memory_space=pltpu.SMEM),
                pl.BlockSpec((n,tok.shape[1]),lambda h:(0,0)),
                pl.BlockSpec((tok.shape[1],256),lambda h:(0,h)),
                pl.BlockSpec((1,1,256),lambda h: (h, 0, 0))],
      out_specs=(pl.BlockSpec((1,n,128),lambda h: (h, 0, 0)),)*3,
      scratch_shapes=[pltpu.VMEM((2*n,128),F32),pltpu.VMEM((2*n,128),F32),pltpu.VMEM((n,128),F32)],
      compiler_params=pltpu.CompilerParams(vmem_limit_bytes=VMEM_ALL),name="att_fwd")(pos,tok,w,bias)

def bwd_kernel(pos, left, right, g, gj, src, ord_, dc):
    h=pl.program_id(0)
    n=g.shape[1]
    U=64
    src[pl.ds(0,n),:]=g[0].astype(F32)
    def scat(i,_):
        for u in range(U):
            t=i*U+u
            ord_[pl.ds(pos[h*n+t],1),:]=src[pl.ds(t,1),:]
        return 0
    lax.fori_loop(0,n//U,scat,0)
    lane=lax.broadcasted_iota(jnp.int32,(CL,128),1)
    mask=(lane<64)==(h==0)
    CB=4
    def clus(i,_):
        for u in range(CB):
            r=pl.multiple_of((i*CB+u)*CL,CL)
            l=left[0,pl.ds(r,CL),:]
            rr=right[0,pl.ds(r,CL),:]
            d=jnp.where(mask,ord_[pl.ds(r,CL),:],0.0).astype(BF)
            s=nt(rr,l)
            m=jnp.max(s,axis=0,keepdims=True)
            e=jnp.exp((s-m)*0.125)
            p=e*(1.0/jnp.sum(e,axis=0,keepdims=True))
            dp=nt(rr,d)
            rd=jnp.sum(dp*p,axis=0,keepdims=True)
            ds=(p*(dp-rd)).astype(BF)
            dl=tn(ds,rr)*0.125
            dr=nn(ds,l)*0.125+nn(p.astype(BF),d)
            dc[pl.ds(2*r,CL,stride=2),:]=dl
            dc[pl.ds(2*r+1,CL,stride=2),:]=dr
        return 0
    lax.fori_loop(0,n//CL//CB,clus,0)
    def gath(i,_):
        for u in range(U):
            t=i*U+u
            src[pl.ds(2*t,2),:]=dc[pl.ds(2*pos[h*n+t],2),:]
        return 0
    lax.fori_loop(0,n//U,gath,0)
    ch=512
    def out(i,_):
        r=pl.multiple_of(i*ch,ch)
        gj[0,pl.ds(r,ch),:128]=src[pl.ds(2*r,ch,stride=2),:].astype(BF)
        gj[0,pl.ds(r,ch),128:]=src[pl.ds(2*r+1,ch,stride=2),:].astype(BF)
        return 0
    lax.fori_loop(0,n//ch,out,0)

def bwd(pos,left,right,g):
    n=g.shape[1]; H=left.shape[0]
    blk=lambda: pl.BlockSpec((1,n,128),lambda h: (h, 0, 0))
    return pl.pallas_call(bwd_kernel,grid=(H,),
      out_shape=jax.ShapeDtypeStruct((H,n,256),BF),
      in_specs=[pl.BlockSpec(memory_space=pltpu.SMEM),blk(),blk(),pl.BlockSpec((1,n,128),lambda h: (h // 2, 0, 0))],
      out_specs=pl.BlockSpec((1,n,256),lambda h: (h, 0, 0)),
      scratch_shapes=[pltpu.VMEM((2*n,128),F32),pltpu.VMEM((n,128),F32),pltpu.VMEM((2*n,128),F32)],
      compiler_params=pltpu.CompilerParams(vmem_limit_bytes=VMEM_ALL),name="att_bwd")(pos,left,right,g)

MESH = pl.DeviceIdType.MESH


def bits_of(size):
    return size.bit_length() - 1


def steps_of(nt, ng):
    return [("tok", b) for b in reversed(range(bits_of(nt)))] + [
        ("grp", b) for b in reversed(range(bits_of(ng)))
    ]


def greet(peers):
    barrier = pltpu.get_barrier_semaphore()
    for peer in peers:
        pl.semaphore_signal(barrier, inc=1, device_id=peer, device_id_type=MESH)
    pl.semaphore_wait(barrier, len(peers))


def collect_kernel(nt, ng, parts, *refs):
    tok_in, pos_in, pin_in = refs[:3]
    nf = (len(refs) - 13) // 2
    full_in = refs[3:3 + nf]
    tok_out, pos_out, pin_out = refs[3 + nf:6 + nf]
    full_out = refs[6 + nf:6 + 2 * nf]
    lsem, tsend, trecv, psend, precv, wsend, wrecv = refs[6 + 2 * nf:]
    t = lax.axis_index("tok")
    g = lax.axis_index("grp")
    steps = steps_of(nt, ng)
    nb = len(steps)
    me = t * ng + g
    digits = [(me // (1 << (nb - 1 - j))) % 2 for j in range(nb)]

    def held_at(s):
        return (slice(None),) * s + tuple(digits[s:])

    def peer(axis, mask):
        return {"tok": t ^ mask, "grp": g} if axis == "tok" else {"tok": t, "grp": g ^ mask}

    count = tok_in.shape[0]
    own = [pltpu.make_async_copy(tok_in, tok_out.at[0], lsem.at[0]),
           pltpu.make_async_copy(pos_in.at[t % 4], pos_out.at[0], lsem.at[1])]
    for i, (a, b) in enumerate(zip(full_in, full_out)):
        own.append(pltpu.make_async_copy(a, b.at[held_at(0)], lsem.at[2 + i]))
    greet([peer(axis, 1 << b) for axis, b in steps] + [peer("tok", 3)])
    for copy in own:
        copy.start()

    flights = {}

    def send(name, src, dst, sems, to):
        copy = pltpu.make_async_remote_copy(
            src_ref=src, dst_ref=dst, send_sem=sems[0], recv_sem=sems[1],
            device_id=to, device_id_type=MESH)
        copy.start()
        flights[name] = copy

    arrived = set()

    def wait(name):
        if name not in arrived:
            arrived.add(name)
            flights[name].wait_recv()

    chunk = count // parts

    def rows(c):
        return pl.ds(c * chunk, chunk)

    def token(c, mask):
        i = (mask - 1) * parts + c
        send(("t", mask, c), tok_in.at[rows(c)], tok_out.at[mask, rows(c)],
             (tsend.at[i], trecv.at[i]), peer("tok", mask))

    def relay(c):
        i = 2 * parts + c
        mask = 2 if c >= parts // 2 else 1
        wait(("t", 3 - mask, c))
        send(("r", c), tok_out.at[3 - mask, rows(c)], tok_out.at[3, rows(c)],
             (tsend.at[i], trecv.at[i]), peer("tok", mask))

    def position(mask):
        i = mask - 1
        send(("p", mask), pos_in.at[(t ^ mask) % 4], pos_out.at[mask],
             (psend.at[i], precv.at[i]), peer("tok", mask))

    def full(w, s):
        axis, b = steps[s]
        i = w * nb + s
        to = peer(axis, 1 << b)
        out = full_out[w]
        if s == 0:
            src, dst = full_in[w], out.at[held_at(0)]
        else:
            wait(("w", w, s - 1))
            if s == 1:
                own[2 + w].wait()
            src = out.at[held_at(s)]
            dst = src
        send(("w", w, s), src, dst, (wsend.at[i], wrecv.at[i]), to)

    def slices(s):
        axis, b = steps[s]
        i = nf * nb + s
        to = peer(axis, 1 << b)
        tb = bits_of(nt)
        if s > 0:
            wait(("w", nf, s - 1))
        high = tb - 2
        theirs = (t ^ (1 << b)) if axis == "tok" else t
        if s < high:
            place = (slice(None), slice(None))
        elif s == high:
            place = ((theirs // 2) % 2, slice(None))
        else:
            place = ((theirs // 2) % 2, theirs % 2)
        src = pin_out.at[place + held_at(s)]
        send(("w", nf, s), src, src, (wsend.at[i], wrecv.at[i]), to)

    pin_own = pltpu.make_async_copy(pin_in, pin_out.at[(slice(None), slice(None)) + held_at(0)], lsem.at[2 + nf])
    pin_own.start()
    order = list(range(nf))
    half = parts // 2
    for c in range(half):
        token(c, 1)
    for w in order:
        full(w, 0)
    pin_own.wait()
    slices(0)
    for mask in (1, 2, 3):
        position(mask)
    token(0, 2)
    done_y, done_z = half, 1
    for s in range(1, nb):
        for w in order:
            full(w, s)
            if w >= 0:
                if done_z < parts:
                    token(done_z, 2)
                    done_z += 1
                if done_y < parts and s >= 2:
                    token(done_y, 1)
                    done_y += 1
        slices(s)
        if s == nb - 2:
            for c in range(done_z, parts):
                token(c, 2)
            for c in range(done_y, parts):
                token(c, 1)
            for c in range(parts):
                relay(c)
    own[0].wait()
    own[1].wait()
    if nb == 1:
        for w in range(nf):
            own[2 + w].wait()
    for name in flights:
        wait(name)
    for copy in flights.values():
        copy.wait_send()


def collect(nt, ng, tokens, pos, pin, fulls, parts=4):
    n = nt * ng
    nb = bits_of(nt) + bits_of(ng)
    hbm = pl.BlockSpec(memory_space=pl.ANY)
    vm = pl.BlockSpec(memory_space=pltpu.VMEM)
    S = jax.ShapeDtypeStruct
    block, at, own, *wide = pl.pallas_call(
        functools.partial(collect_kernel, nt, ng, parts),
        out_shape=[S((4,) + tokens.shape, tokens.dtype), S((4,) + pos.shape[1:], pos.dtype),
                   S((2, 2) + (2,) * nb + pin.shape[1:], pin.dtype)] + [S((2,) * nb + f.shape, f.dtype) for f in fulls],
        in_specs=[vm] * (3 + len(fulls)),
        out_specs=[hbm] * (3 + len(fulls)),
        scratch_shapes=[
            pltpu.SemaphoreType.DMA((3 + len(fulls),)),
            pltpu.SemaphoreType.DMA((3 * parts,)), pltpu.SemaphoreType.DMA((3 * parts,)),
            pltpu.SemaphoreType.DMA((3,)), pltpu.SemaphoreType.DMA((3,)),
            pltpu.SemaphoreType.DMA(((len(fulls) + 1) * nb,)), pltpu.SemaphoreType.DMA(((len(fulls) + 1) * nb,)),
        ],
        compiler_params=pltpu.CompilerParams(collective_id=0, has_side_effects=True),
        name="collect",
    )(tokens, pos, pin.reshape((2, 2) + pin.shape[1:]), *fulls)
    return [block, at, own.reshape((4, n) + pin.shape[1:])] + [
        w.reshape((n,) + f.shape) for w, f in zip(wide, fulls)]


def reduce_kernel(nt, ng, *refs):
    pin_in, pout_in, small_in, pin_out, pout_out, small_out = refs[:6]
    nb = bits_of(nt) + bits_of(ng)
    tb = bits_of(nt)
    pin_a, pout_a, small_a, quad = refs[6:10]
    landing = refs[10:10 + 3 * nb]
    ssem, rsem = refs[10 + 3 * nb:]
    t = lax.axis_index("tok")
    g = lax.axis_index("grp")
    steps = steps_of(nt, ng)
    me = t * ng + g
    digits = [(me // (1 << (nb - 1 - j))) % 2 for j in range(nb)]

    def peer(s):
        axis, b = steps[s]
        mask = 1 << b
        return {"tok": t ^ mask, "grp": g} if axis == "tok" else {"tok": t, "grp": g ^ mask}

    greet([peer(s) for s in range(nb)])
    p1, p0 = (t // 2) % 2, t % 2
    flying = []

    def launch(i, src, dst, s):
        copy = pltpu.make_async_remote_copy(
            src_ref=src, dst_ref=dst, send_sem=ssem.at[i], recv_sem=rsem.at[i],
            device_id=peer(s), device_id_type=MESH)
        copy.start()
        flying.append(copy)
        return copy

    def away(s):
        return (slice(None),) * s + (1 - digits[s],) + tuple(digits[s + 1:])

    def kept(s):
        return (slice(None),) * s + tuple(digits[s:])

    def add(ref, at, other, dst, to):
        value = ref[at].astype(F32) + other[...].astype(F32)
        dst[to] = value.astype(dst.dtype)

    for s in reversed(range(nb)):
        first = s == nb - 1
        outer = s >= tb
        sources = [pin_in if first else pin_a, pout_in if first else pout_a, small_in if first else small_a]
        copies = []
        for w in range(3):
            land = landing[w * nb + s]
            i = w * nb + s
            if w == 0 and not outer:
                place = {tb - 1: (p1, p0), tb - 2: (p1, slice(None))}.get(s, (slice(None), slice(None)))
                cut = (slice(None),) * s + (1 - digits[s],) + tuple(digits[s + 1:tb])
                src = quad.at[place + cut]
                copies.append(launch(i, src, src if s >= tb - 2 else land, s))
            else:
                copies.append(launch(i, sources[w].at[away(s)], land, s))
        for w in range(3):
            copies[w].wait_recv()
            land = landing[w * nb + s]
            if w == 0 and not outer:
                if s < tb - 2:
                    at = (slice(None), slice(None)) + (slice(None),) * s + tuple(digits[s:tb])
                    add(quad, at, land, quad, at)
            elif w == 0 and s == tb:
                add(sources[0], kept(s), land, quad, (p1, p0))
            else:
                dst = (pin_a, pout_a, small_a)[w]
                add(sources[w], kept(s), land, dst, kept(s))
    for copy in flying:
        copy.wait_send()
    pin_out[...] = quad[(slice(None), slice(None)) + tuple(digits[:tb])]
    pout_out[...] = pout_a[tuple(digits)]
    small_out[...] = small_a[tuple(digits)]


def reduce_small(nt, ng, pin, pout, small):
    nb = bits_of(nt) + bits_of(ng)
    tb = bits_of(nt)
    two = (2,) * nb
    r, c = pin.shape[1:]
    rp = pout.shape[1:]
    rs = small.shape[1:]
    S = jax.ShapeDtypeStruct
    vm = pl.BlockSpec(memory_space=pltpu.VMEM)
    landing = []
    for w, (shape, dt) in enumerate((((r, c), BF), (rp, BF), (rs, F32))):
        for s in range(nb):
            lead = (2,) * s
            if w == 0 and s < tb:
                lead = ((2, 2) + lead) if s < tb - 2 else (1,)
                landing.append(pltpu.VMEM(lead + (shape if s < tb - 2 else (8, 128)), dt))
            else:
                landing.append(pltpu.VMEM(lead + shape, dt))
    return pl.pallas_call(
        functools.partial(reduce_kernel, nt, ng),
        out_shape=[S((2, 2, r, c), BF), S(rp, BF), S(rs, F32)],
        in_specs=[vm] * 3,
        out_specs=[vm] * 3,
        scratch_shapes=[
            pltpu.VMEM(two + (r, c), BF), pltpu.VMEM(two + rp, BF), pltpu.VMEM(two + rs, F32),
            pltpu.VMEM((2, 2) + (2,) * tb + (r, c), BF),
        ] + landing + [pltpu.SemaphoreType.DMA((3 * nb,)), pltpu.SemaphoreType.DMA((3 * nb,))],
        compiler_params=pltpu.CompilerParams(collective_id=1, has_side_effects=True, vmem_limit_bytes=VMEM_ALL),
        name="reduce_small",
    )(pin.reshape(two + (r, c)), pout.reshape(two + rp), small.reshape(two + rs))


def flip(block, mask):
    count = lax.axis_size("tok")
    return lax.ppermute(block, "tok", [(i, i ^ mask) for i in range(count)])


def gather_all(item):
    return lax.all_gather(item, ("tok", "grp"), axis=0, tiled=True)


def scatter_sum(item):
    return lax.psum_scatter(item, ("tok", "grp"), scatter_dimension=0, tiled=True)


def shards(
    tokens,
    upstream,
    cluster_pos,
    project_in,
    query_bias,
    value_bias,
    project_out,
    output_bias,
    first_gain,
    first_shift,
    expand,
    expand_bias,
    contract,
    contract_bias,
    second_gain,
    second_shift,
):
    inputs = tokens[0]
    count, width = inputs.shape
    positions = cluster_pos[0] % LONG
    heads = positions.shape[0]
    head_dim = width // heads
    span = LONG // count
    mine = heads // span
    offset = lax.axis_index("tok") % span
    total = span * count

    nt = lax.axis_size("tok")
    ng = lax.axis_size("grp")
    devices = nt * ng
    few = query_bias.shape[0]
    strips = expand.shape[1] // width

    wide = jnp.concatenate(
        [expand.reshape(few, strips, width).transpose(1, 0, 2).reshape(-1, width), contract], axis=0
    )
    wide = gather_all(wide[None])
    expand = wide[:, : strips * few].reshape(devices, strips, few, width)
    expand = expand.transpose(0, 2, 1, 3).reshape(width, strips * width)
    contract = wide[:, strips * few :].reshape(strips * width, width)

    pieces = project_in.reshape(few, 3, span, mine, head_dim)
    hollow = jnp.zeros((few, head_dim), BF)
    arranged = []
    for place in range(span):
        columns = []
        for h in range(mine):
            query, key, value = (pieces[:, i, place, h] for i in range(3))
            columns += [hollow, query, value, key] if h == 0 else [query, hollow, key, value]
        arranged.append(jnp.concatenate(columns, axis=1))
    packed = jnp.concatenate(
        [
            query_bias, value_bias, output_bias, first_gain, first_shift,
            contract_bias, second_gain, second_shift, expand_bias,
        ]
    ).astype(F32)
    packed = jnp.pad(packed, (0, 1024 - packed.shape[0])).reshape(8, 128)
    block, own_at, arranged, packed, project_out = collect(
        nt, ng, inputs, positions.reshape(span, mine, count), jnp.stack(arranged), [packed, project_out]
    )
    block = block.reshape(total, width)
    own_at = own_at.transpose(1, 0, 2).reshape(-1)
    arranged = lax.dynamic_index_in_dim(arranged, offset, 0, False).reshape(width, -1)
    project_out = project_out.reshape(width, width)
    packed = packed.reshape(devices, -1)
    vectors = [packed[:, i * few : (i + 1) * few].reshape(-1) for i in range(8)]
    query_bias, value_bias, output_bias, gain_one, shift_one, contract_bias, gain_two, shift_two = vectors
    expand_bias = packed[:, 8 * few : (8 + strips) * few].reshape(-1)

    own_query = lax.dynamic_slice_in_dim(query_bias.reshape(heads, head_dim), offset * mine, mine)
    own_value = lax.dynamic_slice_in_dim(value_bias.reshape(heads, head_dim), offset * mine, mine)
    blank = jnp.zeros((head_dim,), F32)
    rows = []
    for h in range(mine):
        parts = [blank, own_query[h], own_value[h], blank] if h == 0 else [own_query[h], blank, blank, own_value[h]]
        rows.append(jnp.concatenate(parts))
    bias_rows = jnp.stack(rows)[:, None]

    att, left, right = fwd(own_at, block, arranged, bias_rows)
    lane = jnp.arange(2 * head_dim) < head_dim
    pair = jnp.where(lane, att[0], att[1]).reshape(span, count, 2 * head_dim)
    single = att[2, :, head_dim:].reshape(span, 2, count // 2, head_dim)
    single = single.transpose(0, 2, 1, 3).reshape(span, count // 2, 2 * head_dim)
    leaving = jnp.concatenate([pair, single], axis=1)
    came = [leaving[0]] + [flip(leaving[k], k) for k in range(1, span)]

    def open_single(item):
        return jnp.concatenate([item[:, :head_dim], item[:, head_dim:]], axis=0)

    merged = jnp.concatenate(
        [item[:count] for item in came] + [open_single(item[count:]) for item in came], axis=1
    )
    by_owner = project_out.reshape(span, mine * head_dim, width)
    turned = [lax.dynamic_index_in_dim(by_owner, offset ^ k, 0, False) for k in range(span)]
    project_turned = jnp.concatenate(
        [item[: 2 * head_dim] for item in turned] + [item[2 * head_dim :] for item in turned], axis=0
    )

    branch = jnp.dot(merged, project_turned, preferred_element_type=F32) + output_bias
    normed_one, unit_one, inverse_one = normalize(inputs.astype(F32) + branch, gain_one, shift_one)
    normed_low = normed_one.astype(BF)
    inner = jnp.dot(normed_low, expand, preferred_element_type=F32) + expand_bias
    lifted = jax.nn.gelu(inner, approximate=False).astype(BF)
    second_sum = normed_one + jnp.dot(lifted, contract, preferred_element_type=F32) + contract_bias
    result, unit_two, inverse_two = normalize(second_sum, gain_two, shift_two)
    cotangent = upstream[0].astype(F32)
    second_gain_grad = jnp.sum(cotangent * unit_two, axis=0)
    second_shift_grad = jnp.sum(cotangent, axis=0)
    grad_second = normalize_back(cotangent, gain_two, unit_two, inverse_two)
    grad_mid = grad_second.astype(BF)
    contract_bias_grad = jnp.sum(grad_mid.astype(F32), axis=0)
    contract_grad = jnp.einsum("rf,rd->fd", lifted, grad_mid, preferred_element_type=F32)
    grad_lifted = jnp.einsum("rd,fd->rf", grad_mid, contract, preferred_element_type=F32)
    slope = (
        0.5 * (1.0 + lax.erf(inner * root_half))
        + inner * jnp.exp(-0.5 * inner * inner) * density_norm
    )
    grad_inner = (grad_lifted * slope).astype(BF)
    expand_bias_grad = jnp.sum(grad_inner.astype(F32), axis=0)
    expand_grad = jnp.einsum("rd,rf->df", normed_low, grad_inner, preferred_element_type=F32)
    grad_normed = grad_second + jnp.einsum(
        "rf,df->rd", grad_inner, expand, preferred_element_type=F32
    )
    first_gain_grad = jnp.sum(grad_normed * unit_one, axis=0)
    first_shift_grad = jnp.sum(grad_normed, axis=0)
    grad_first = normalize_back(grad_normed, gain_one, unit_one, inverse_one)
    grad_branch = grad_first.astype(BF)
    output_bias_grad = jnp.sum(grad_branch.astype(F32), axis=0)
    turned_grad = jnp.einsum("rd,re->de", merged, grad_branch, preferred_element_type=F32)
    grad_merged = jnp.einsum(
        "re,de->rd", grad_branch, project_turned, preferred_element_type=F32
    ).astype(BF)

    pair_cols = span * 2 * head_dim
    sending = []
    for k in range(span):
        two = grad_merged[:, k * 2 * head_dim : (k + 1) * 2 * head_dim]
        one = grad_merged[:, pair_cols + k * head_dim : pair_cols + (k + 1) * head_dim]
        one = jnp.concatenate([one[: count // 2], one[count // 2 :]], axis=1)
        sending.append(jnp.concatenate([two, one], axis=0))
    landed = [sending[0]] + [flip(sending[k], k) for k in range(1, span)]
    expand_grad = expand_grad.astype(BF)
    contract_grad = contract_grad.astype(BF)
    landed, expand_grad, contract_grad = lax.optimization_barrier((landed, expand_grad, contract_grad))
    wide_grad = jnp.concatenate(
        [expand_grad[:, i * width : (i + 1) * width].reshape(devices, few, width) for i in range(strips)]
        + [contract_grad.reshape(devices, strips * few, width)],
        axis=1,
    )
    wide_grad = scatter_sum(wide_grad)[0].astype(F32)
    expand_grad = wide_grad[: strips * few].reshape(strips, few, width).transpose(1, 0, 2).reshape(few, -1)
    contract_grad = wide_grad[strips * few :]
    grad_pair = jnp.concatenate([item[:count] for item in landed], axis=0)
    grad_single = jnp.concatenate([open_single(item[count:]) for item in landed], axis=0)
    grad_att = jnp.stack([grad_pair, jnp.concatenate([grad_single, grad_single], axis=1)])
    grad_rows = bwd(own_at, left, right, grad_att)

    arranged_grad = jnp.concatenate(
        [jnp.einsum("rd,re->de", block, grad_rows[h], preferred_element_type=F32) for h in range(mine)],
        axis=1,
    ).astype(BF)
    sums = jnp.sum(grad_rows.astype(F32), axis=1).reshape(mine, 4, head_dim)
    query_at = [1] + [0] * (mine - 1)
    key_at = [3] + [2] * (mine - 1)
    value_at = [2] + [3] * (mine - 1)

    def spread(take, at):
        return jnp.stack([take(h, at[h]) for h in range(mine)], axis=-2)

    own_sums = jnp.stack([spread(lambda h, s: sums[h, s], at) for at in (query_at, value_at)])
    bias_grads = lax.dynamic_update_slice_in_dim(
        jnp.zeros((2, heads, head_dim), F32), own_sums, offset * mine, axis=1
    ).reshape(2, width)
    partial = sum(
        jnp.einsum(
            "re,de->rd", grad_rows[h], arranged[:, 256 * h : 256 * h + 256], preferred_element_type=F32
        )
        for h in range(mine)
    ).reshape(span, count, width)
    token_grad = grad_first + partial[0]
    for k in range(1, span):
        token_grad = token_grad + flip(partial[k].astype(BF), k).astype(F32)

    by_owner = jnp.concatenate(
        [
            turned_grad[:pair_cols].reshape(span, 2 * head_dim, width),
            turned_grad[pair_cols:].reshape(span, head_dim, width),
        ],
        axis=1,
    )
    project_out_grad = jnp.concatenate(
        [lax.dynamic_index_in_dim(by_owner, offset ^ k, 0, False) for k in range(span)], axis=0
    )
    small = jnp.concatenate(
        [
            item.reshape(devices, -1)
            for item in (
                bias_grads[0], bias_grads[1], output_bias_grad, first_gain_grad, first_shift_grad,
                contract_bias_grad, second_gain_grad, second_shift_grad, expand_bias_grad,
            )
        ],
        axis=1,
    )
    small = jnp.pad(small, ((0, 0), (0, 1024 - small.shape[1]))).reshape(devices, 8, 128)
    project_in_grad, project_out_grad, small = reduce_small(
        nt, ng, arranged_grad.reshape(devices, few, -1),
        project_out_grad.astype(BF).reshape(devices, few, width), small,
    )
    project_in_grad = project_in_grad.astype(F32).reshape(span, few, mine, 4, head_dim)
    project_in_grad = jnp.concatenate(
        [
            project_in_grad[place, :, h, at[h]]
            for at in (query_at, key_at, value_at)
            for place in range(span)
            for h in range(mine)
        ],
        axis=1,
    )
    project_out_grad = project_out_grad.astype(F32)
    small = small.reshape(-1)
    each = [small[i * few : (i + 1) * few] for i in range(8)] + [small[8 * few : (8 + strips) * few]]
    return (
        result.astype(BF)[None],
        token_grad[None],
        project_in_grad,
        each[0],
        each[1],
        project_out_grad,
        each[2],
        each[3],
        each[4],
        expand_grad,
        each[8],
        contract_grad,
        each[5],
        each[6],
        each[7],
    )


def solution(mesh):
    placed = (
        P("grp", "tok", None),
        P("grp", "tok", None),
        P("grp", None, "tok"),
        P(("tok", "grp"), None),
        P(("tok", "grp")),
        P(("tok", "grp")),
        P(("tok", "grp"), None),
        P(("tok", "grp")),
        P(("tok", "grp")),
        P(("tok", "grp")),
        P(("tok", "grp"), None),
        P(("tok", "grp")),
        P(("tok", "grp"), None),
        P(("tok", "grp")),
        P(("tok", "grp")),
        P(("tok", "grp")),
    )
    return jax.shard_map(
        shards,
        mesh=mesh,
        in_specs=placed,
        out_specs=(
            P("grp", "tok", None),
            P("grp", "tok", None),
            P(("tok", "grp"), None),
            P(("tok", "grp")),
            P(("tok", "grp")),
            P(("tok", "grp"), None),
            P(("tok", "grp")),
            P(("tok", "grp")),
            P(("tok", "grp")),
            P(("tok", "grp"), None),
            P(("tok", "grp")),
            P(("tok", "grp"), None),
            P(("tok", "grp")),
            P(("tok", "grp")),
            P(("tok", "grp")),
        ),
        check_vma=False,
    )
```

```python
import functools
import jax
import jax.numpy as jnp
from jax import lax
from jax.experimental import pallas as pl
from jax.experimental.pallas import tpu as pltpu
from jax.sharding import PartitionSpec as P

CL = 128
LONG = 4096
F32 = jnp.float32
BF = jnp.bfloat16
VMEM_ALL = 64 * 1024 * 1024 - 65536

epsilon = 1e-05
root_half = 0.7071067811865476
density_norm = 0.3989422804014327

def normalize(hidden, gain, shift):
    centred = hidden - jnp.mean(hidden, axis=1, keepdims=True)
    inverse_std = lax.rsqrt(jnp.mean(centred * centred, axis=1, keepdims=True) + epsilon)
    unit = centred * inverse_std
    return (unit * gain + shift, unit, inverse_std)


def normalize_back(grad_out, gain, unit, inverse_std):
    scaled = grad_out * gain
    return inverse_std * (
        scaled
        - jnp.mean(scaled, axis=1, keepdims=True)
        - unit * jnp.mean(scaled * unit, axis=1, keepdims=True)
    )


def nt(a,b): return lax.dot_general(a,b,(((1,),(1,)),((),())),preferred_element_type=F32)
def nn(a,b): return lax.dot_general(a,b,(((1,),(0,)),((),())),preferred_element_type=F32)
def tn(a,b): return lax.dot_general(a,b,(((0,),(0,)),((),())),preferred_element_type=F32)

def fwd_kernel(span, pos, tok, w, bias, *refs):
    leave = refs[:span]
    left, right, src, ord_, oc = refs[span:]
    h=pl.program_id(0)
    n=tok.shape[0]
    ch=512
    def proj(i,_):
        r=pl.multiple_of(i*ch,ch)
        acc=nn(tok[pl.ds(r,ch),:],w[...])+bias[0]
        src[pl.ds(2*r,ch,stride=2),:]=acc[:,:128]
        src[pl.ds(2*r+1,ch,stride=2),:]=acc[:,128:]
        return 0
    lax.fori_loop(0,n//ch,proj,0)
    U=64
    def scat(i,_):
        for u in range(U):
            t=i*U+u
            ord_[pl.ds(2*pos[h*n+t],2),:]=src[pl.ds(2*t,2),:]
        return 0
    lax.fori_loop(0,n//U,scat,0)
    CB=4
    def clus(i,_):
        for u in range(CB):
            r=pl.multiple_of((i*CB+u)*CL,CL)
            l=ord_[pl.ds(2*r,CL,stride=2),:].astype(BF)
            rr=ord_[pl.ds(2*r+1,CL,stride=2),:].astype(BF)
            left[0,pl.ds(r,CL),:]=l
            right[0,pl.ds(r,CL),:]=rr
            s=nt(rr,l)
            m=jnp.max(s,axis=0,keepdims=True)
            e=jnp.exp((s-m)*0.125)
            p=(e*(1.0/jnp.sum(e,axis=0,keepdims=True))).astype(BF)
            oc[pl.ds(r,CL),:]=tn(p,rr)
        return 0
    lax.fori_loop(0,n//CL//CB,clus,0)
    def gath(i,_):
        for u in range(U):
            t=i*U+u
            src[pl.ds(t,1),:]=oc[pl.ds(pos[h*n+t],1),:]
        return 0
    lax.fori_loop(0,n//U,gath,0)
    count=n//span
    @pl.when(h==0)
    def _():
        for k in range(span):
            leave[k][:count,:64]=src[k*count:(k+1)*count,:64].astype(BF)
    @pl.when(h==1)
    def _():
        for k in range(span):
            leave[k][:count,64:]=src[k*count:(k+1)*count,64:].astype(BF)
    @pl.when(h==2)
    def _():
        for k in range(span):
            mid_row=k*count+count//2
            leave[k][count:,:64]=src[k*count:mid_row,64:].astype(BF)
            leave[k][count:,64:]=src[mid_row:(k+1)*count,64:].astype(BF)

def fwd(pos,tok,w,bias,span):
    rows=tok.shape[0]//span*3//2
    n=tok.shape[0]; H=pos.shape[0]//n
    return pl.pallas_call(functools.partial(fwd_kernel,span),grid=(H,),
      out_shape=(jax.ShapeDtypeStruct((rows,128),BF),)*span+(jax.ShapeDtypeStruct((H,n,128),BF),)*2,
      in_specs=[pl.BlockSpec(memory_space=pltpu.SMEM),
                pl.BlockSpec((n,tok.shape[1]),lambda h:(0,0)),
                pl.BlockSpec((tok.shape[1],256),lambda h:(0,h)),
                pl.BlockSpec((1,1,256),lambda h: (h, 0, 0))],
      out_specs=(pl.BlockSpec((rows,128),lambda h: (0, 0)),)*span+(pl.BlockSpec((1,n,128),lambda h: (h, 0, 0)),)*2,
      scratch_shapes=[pltpu.VMEM((2*n,128),F32),pltpu.VMEM((2*n,128),F32),pltpu.VMEM((n,128),F32)],
      compiler_params=pltpu.CompilerParams(vmem_limit_bytes=VMEM_ALL),name="att_fwd")(pos,tok,w,bias)

def bwd_kernel(span, pos, left, right, *refs):
    landed = refs[:span]
    gj, total, src, ord_, dc = refs[span:]
    h=pl.program_id(0)
    n=left.shape[1]
    U=64
    count=n//span
    @pl.when(h<2)
    def _():
        for k in range(span):
            src[k*count:(k+1)*count,:]=landed[k][:count,:].astype(F32)
    @pl.when(h==2)
    def _():
        for k in range(span):
            x=landed[k][count:,:].astype(F32)
            mid_row=k*count+count//2
            src[k*count:mid_row,:]=jnp.concatenate([x[:,64:],x[:,:64]],axis=1)
            src[mid_row:(k+1)*count,:]=x
    def scat(i,_):
        for u in range(U):
            t=i*U+u
            ord_[pl.ds(pos[h*n+t],1),:]=src[pl.ds(t,1),:]
        return 0
    lax.fori_loop(0,n//U,scat,0)
    lane=lax.broadcasted_iota(jnp.int32,(CL,128),1)
    mask=(lane<64)==(h==0)
    CB=4
    def clus(i,_):
        for u in range(CB):
            r=pl.multiple_of((i*CB+u)*CL,CL)
            l=left[0,pl.ds(r,CL),:]
            rr=right[0,pl.ds(r,CL),:]
            d=jnp.where(mask,ord_[pl.ds(r,CL),:],0.0).astype(BF)
            s=nt(rr,l)
            m=jnp.max(s,axis=0,keepdims=True)
            e=jnp.exp((s-m)*0.125)
            p=e*(1.0/jnp.sum(e,axis=0,keepdims=True))
            dp=nt(rr,d)
            rd=jnp.sum(dp*p,axis=0,keepdims=True)
            ds=(p*(dp-rd)).astype(BF)
            dl=tn(ds,rr)*0.125
            dr=nn(ds,l)*0.125+nn(p.astype(BF),d)
            dc[pl.ds(2*r,CL,stride=2),:]=dl
            dc[pl.ds(2*r+1,CL,stride=2),:]=dr
        return 0
    lax.fori_loop(0,n//CL//CB,clus,0)
    def gath(i,_):
        for u in range(U):
            t=i*U+u
            src[pl.ds(2*t,2),:]=dc[pl.ds(2*pos[h*n+t],2),:]
        return 0
    lax.fori_loop(0,n//U,gath,0)
    ch=512
    def out(i,sums):
        r=pl.multiple_of(i*ch,ch)
        one=src[pl.ds(2*r,ch,stride=2),:].astype(BF)
        two=src[pl.ds(2*r+1,ch,stride=2),:].astype(BF)
        gj[pl.ds(r,ch),:128]=one
        gj[pl.ds(r,ch),128:]=two
        fold=lambda x: jnp.sum(x.astype(F32).reshape(ch//8,8,128),axis=0)
        return (sums[0]+fold(one),sums[1]+fold(two))
    zero=jnp.zeros((8,128),F32)
    one,two=lax.fori_loop(0,n//ch,out,(zero,zero))
    total[:,:128]=one
    total[:,128:]=two

def bwd(pos,left,right,landed):
    H,n=left.shape[:2]
    span=len(landed)
    rows=landed[0].shape[0]
    blk=lambda: pl.BlockSpec((1,n,128),lambda h: (h, 0, 0))
    return pl.pallas_call(functools.partial(bwd_kernel,span),grid=(H,),
      out_shape=(jax.ShapeDtypeStruct((n,H*256),BF),jax.ShapeDtypeStruct((8,H*256),F32)),
      in_specs=[pl.BlockSpec(memory_space=pltpu.SMEM),blk(),blk()]+[pl.BlockSpec((rows,128),lambda h: (0, 0))]*span,
      out_specs=(pl.BlockSpec((n,256),lambda h: (0, h)),pl.BlockSpec((8,256),lambda h: (0, h))),
      scratch_shapes=[pltpu.VMEM((2*n,128),F32),pltpu.VMEM((n,128),F32),pltpu.VMEM((2*n,128),F32)],
      compiler_params=pltpu.CompilerParams(vmem_limit_bytes=VMEM_ALL),name="att_bwd")(pos,left,right,*landed)

def mid_kernel(span, *refs):
    came = refs[:span]
    at, tok, up, wo, we, wc, vec, ebias = refs[span:span + 8]
    result, gfirst = refs[span + 8:span + 10]
    leave = refs[span + 10:2 * span + 10]
    merged_o, gbranch_o, nlow_o, gmid_o, lifted_o, ginner_o, sums, esum = refs[2 * span + 10:2 * span + 18]
    wop, slope = refs[2 * span + 18:]
    i = pl.program_id(0)
    rows, width = tok.shape
    half = rows * pl.num_programs(0) // 2
    strips = we.shape[0]
    own = width // span
    pair = 128
    single = own - pair

    @pl.when(i == 0)
    def _():
        for k in range(span):
            p = pl.multiple_of((at[0] ^ k) * own, 64)
            wop[k * pair:(k + 1) * pair, :] = wo[pl.ds(p, pair), :]
            wop[span * pair + k * single:span * pair + (k + 1) * single, :] = wo[pl.ds(p + pair, single), :]
        sums[...] = jnp.zeros_like(sums)
        esum[...] = jnp.zeros_like(esum)

    def total(at_row, value):
        sums[at_row:at_row + 1, :] += jnp.sum(value, axis=0, keepdims=True)

    low = i * rows < half
    start = pl.multiple_of(2 * half + lax.rem(i * rows, half), rows)
    pairs = [c[pl.ds(pl.multiple_of(i * rows, rows), rows), :] for c in came]
    both = [c[pl.ds(start, rows), :] for c in came]
    singles = [jnp.where(low, x[:, :single], x[:, single:]) for x in both]
    merged = jnp.concatenate(pairs + singles, axis=1)
    merged_o[...] = merged
    hidden = tok[...].astype(F32) + nn(merged, wop[...]) + vec[0:1, :]
    normed_one, unit_one, inverse_one = normalize(hidden, vec[1:2, :], vec[2:3, :])
    normed_low = normed_one.astype(BF)
    nlow_o[...] = normed_low
    second = normed_one + vec[3:4, :]
    for k in range(strips):
        cols = slice(k * width, (k + 1) * width)
        inner = nn(normed_low, we[k]) + ebias[k:k + 1, :]
        cdf = 0.5 * (1.0 + lax.erf(inner * root_half))
        lifted = (inner * cdf).astype(BF)
        slope[:, cols] = cdf + inner * jnp.exp(-0.5 * inner * inner) * density_norm
        lifted_o[:, cols] = lifted
        second += nn(lifted, wc[cols, :])
    out, unit_two, inverse_two = normalize(second, vec[4:5, :], vec[5:6, :])
    result[...] = out.astype(BF)
    cotangent = up[...].astype(F32)
    total(0, cotangent * unit_two)
    total(1, cotangent)
    grad_second = normalize_back(cotangent, vec[4:5, :], unit_two, inverse_two)
    grad_mid = grad_second.astype(BF)
    gmid_o[...] = grad_mid
    total(2, grad_mid.astype(F32))
    grad_normed = grad_second
    for k in range(strips):
        cols = slice(k * width, (k + 1) * width)
        grad_inner = (nt(grad_mid, wc[cols, :]) * slope[:, cols]).astype(BF)
        ginner_o[:, cols] = grad_inner
        esum[k:k + 1, :] += jnp.sum(grad_inner.astype(F32), axis=0, keepdims=True)
        grad_normed += nt(grad_inner, we[k])
    total(3, grad_normed * unit_one)
    total(4, grad_normed)
    grad_first = normalize_back(grad_normed, vec[1:2, :], unit_one, inverse_one)
    gfirst[...] = grad_first
    grad_branch = grad_first.astype(BF)
    gbranch_o[...] = grad_branch
    total(5, grad_branch.astype(F32))
    grad_merged = nt(grad_branch, wop[...]).astype(BF)
    for k in range(span):
        leave[k][pl.ds(pl.multiple_of(i * rows, rows), rows), :] = grad_merged[:, k * pair:(k + 1) * pair]
        one = grad_merged[:, span * pair + k * single:span * pair + (k + 1) * single]

        @pl.when(low)
        def _():
            leave[k][pl.ds(start, rows), :single] = one

        @pl.when(jnp.logical_not(low))
        def _():
            leave[k][pl.ds(start, rows), single:] = one


def mid(came, at, tok, up, wo, we, wc, vec, ebias, rows=256):
    span = len(came)
    count, width = tok.shape
    strips = we.shape[0]
    S = jax.ShapeDtypeStruct
    vm = pl.BlockSpec(memory_space=pltpu.VMEM)
    tile = lambda w: pl.BlockSpec((rows, w), lambda i: (i, 0))
    fixed = lambda shape: pl.BlockSpec(shape, lambda i: (0, 0))
    deep = strips * width
    outs = (
        [(S((count, width), BF), tile(width)), (S((count, width), F32), tile(width))]
        + [(S(came[0].shape, BF), fixed(came[0].shape))] * span
        + [(S((count, width), BF), tile(width))] * 4
        + [(S((count, deep), BF), tile(deep))] * 2
        + [(S((8, width), F32), fixed((8, width))), (S((strips, width), F32), fixed((strips, width)))]
    )
    return pl.pallas_call(
        functools.partial(mid_kernel, span),
        grid=(count // rows,),
        out_shape=[o for o, _ in outs],
        in_specs=[vm] * span + [pl.BlockSpec(memory_space=pltpu.SMEM), tile(width), tile(width)] + [vm] * 5,
        out_specs=[b for _, b in outs],
        scratch_shapes=[pltpu.VMEM((width, width), BF), pltpu.VMEM((rows, deep), F32)],
        compiler_params=pltpu.CompilerParams(vmem_limit_bytes=VMEM_ALL),
        name="mid",
    )(*came, at, tok, up, wo, we, wc, vec, ebias)

MESH = pl.DeviceIdType.MESH


def bits_of(size):
    return size.bit_length() - 1


def steps_of(nt, ng):
    return [("tok", b) for b in reversed(range(bits_of(nt)))] + [
        ("grp", b) for b in reversed(range(bits_of(ng)))
    ]


def greet(peers):
    barrier = pltpu.get_barrier_semaphore()
    for peer in peers:
        pl.semaphore_signal(barrier, inc=1, device_id=peer, device_id_type=MESH)
    pl.semaphore_wait(barrier, len(peers))


def collect_kernel(nt, ng, parts, *refs):
    tok_in, pos_in, pin_in = refs[:3]
    nf = (len(refs) - 13) // 2
    full_in = refs[3:3 + nf]
    tok_out, pos_out, pin_out = refs[3 + nf:6 + nf]
    full_out = refs[6 + nf:6 + 2 * nf]
    lsem, tsend, trecv, psend, precv, wsend, wrecv = refs[6 + 2 * nf:]
    t = lax.axis_index("tok")
    g = lax.axis_index("grp")
    steps = steps_of(nt, ng)
    nb = len(steps)
    me = t * ng + g
    digits = [(me // (1 << (nb - 1 - j))) % 2 for j in range(nb)]

    def held_at(s):
        return (slice(None),) * s + tuple(digits[s:])

    def peer(axis, mask):
        return {"tok": t ^ mask, "grp": g} if axis == "tok" else {"tok": t, "grp": g ^ mask}

    count = tok_in.shape[0]
    own = [pltpu.make_async_copy(tok_in, tok_out.at[0], lsem.at[0]),
           pltpu.make_async_copy(pos_in.at[t % 4], pos_out.at[0], lsem.at[1])]
    for i, (a, b) in enumerate(zip(full_in, full_out)):
        own.append(pltpu.make_async_copy(a, b.at[held_at(0)], lsem.at[2 + i]))
    greet([peer(axis, 1 << b) for axis, b in steps] + [peer("tok", 3)])
    for copy in own:
        copy.start()

    flights = {}

    def send(name, src, dst, sems, to):
        copy = pltpu.make_async_remote_copy(
            src_ref=src, dst_ref=dst, send_sem=sems[0], recv_sem=sems[1],
            device_id=to, device_id_type=MESH)
        copy.start()
        flights[name] = copy

    arrived = set()

    def wait(name):
        if name not in arrived:
            arrived.add(name)
            flights[name].wait_recv()

    chunk = count // parts

    def rows(c):
        return pl.ds(c * chunk, chunk)

    def token(c, mask):
        i = (mask - 1) * parts + c
        send(("t", mask, c), tok_in.at[rows(c)], tok_out.at[mask, rows(c)],
             (tsend.at[i], trecv.at[i]), peer("tok", mask))

    def relay(c):
        i = 2 * parts + c
        mask = 2 if c >= parts // 2 else 1
        wait(("t", 3 - mask, c))
        send(("r", c), tok_out.at[3 - mask, rows(c)], tok_out.at[3, rows(c)],
             (tsend.at[i], trecv.at[i]), peer("tok", mask))

    def position(mask):
        i = mask - 1
        send(("p", mask), pos_in.at[(t ^ mask) % 4], pos_out.at[mask],
             (psend.at[i], precv.at[i]), peer("tok", mask))

    def full(w, s):
        axis, b = steps[s]
        i = w * nb + s
        to = peer(axis, 1 << b)
        out = full_out[w]
        if s == 0:
            src, dst = full_in[w], out.at[held_at(0)]
        else:
            wait(("w", w, s - 1))
            if s == 1:
                own[2 + w].wait()
            src = out.at[held_at(s)]
            dst = src
        send(("w", w, s), src, dst, (wsend.at[i], wrecv.at[i]), to)

    def slices(s):
        axis, b = steps[s]
        i = nf * nb + s
        to = peer(axis, 1 << b)
        tb = bits_of(nt)
        if s > 0:
            wait(("w", nf, s - 1))
        high = tb - 2
        theirs = (t ^ (1 << b)) if axis == "tok" else t
        if s < high:
            place = (slice(None), slice(None))
        elif s == high:
            place = ((theirs // 2) % 2, slice(None))
        else:
            place = ((theirs // 2) % 2, theirs % 2)
        src = pin_out.at[place + held_at(s)]
        send(("w", nf, s), src, src, (wsend.at[i], wrecv.at[i]), to)

    pin_own = pltpu.make_async_copy(pin_in, pin_out.at[(slice(None), slice(None)) + held_at(0)], lsem.at[2 + nf])
    pin_own.start()
    order = list(range(nf))
    half = parts // 2
    for c in range(half):
        token(c, 1)
    for w in order:
        full(w, 0)
    pin_own.wait()
    slices(0)
    for mask in (1, 2, 3):
        position(mask)
    token(0, 2)
    done_y, done_z = half, 1
    for s in range(1, nb):
        for w in order:
            full(w, s)
            if w >= 0:
                if done_z < parts:
                    token(done_z, 2)
                    done_z += 1
                if done_y < parts and s >= 2:
                    token(done_y, 1)
                    done_y += 1
        slices(s)
        if s == nb - 2:
            for c in range(done_z, parts):
                token(c, 2)
            for c in range(done_y, parts):
                token(c, 1)
            for c in range(parts):
                relay(c)
    own[0].wait()
    own[1].wait()
    if nb == 1:
        for w in range(nf):
            own[2 + w].wait()
    for name in flights:
        wait(name)
    for copy in flights.values():
        copy.wait_send()


def collect(nt, ng, tokens, pos, pin, fulls, parts=4):
    n = nt * ng
    nb = bits_of(nt) + bits_of(ng)
    hbm = pl.BlockSpec(memory_space=pl.ANY)
    vm = pl.BlockSpec(memory_space=pltpu.VMEM)
    S = jax.ShapeDtypeStruct
    block, at, own, *wide = pl.pallas_call(
        functools.partial(collect_kernel, nt, ng, parts),
        out_shape=[S((4,) + tokens.shape, tokens.dtype), S((4,) + pos.shape[1:], pos.dtype),
                   S((2, 2) + (2,) * nb + pin.shape[1:], pin.dtype)] + [S((2,) * nb + f.shape, f.dtype) for f in fulls],
        in_specs=[vm] * (3 + len(fulls)),
        out_specs=[hbm] * (3 + len(fulls)),
        scratch_shapes=[
            pltpu.SemaphoreType.DMA((3 + len(fulls),)),
            pltpu.SemaphoreType.DMA((3 * parts,)), pltpu.SemaphoreType.DMA((3 * parts,)),
            pltpu.SemaphoreType.DMA((3,)), pltpu.SemaphoreType.DMA((3,)),
            pltpu.SemaphoreType.DMA(((len(fulls) + 1) * nb,)), pltpu.SemaphoreType.DMA(((len(fulls) + 1) * nb,)),
        ],
        compiler_params=pltpu.CompilerParams(collective_id=0, has_side_effects=True),
        name="collect",
    )(tokens, pos, pin.reshape((2, 2) + pin.shape[1:]), *fulls)
    return [block, at, own.reshape((4, n) + pin.shape[1:])] + [
        w.reshape((n,) + f.shape) for w, f in zip(wide, fulls)]


def reduce_kernel(nt, ng, *refs):
    pin_in, small_in, pin_out, small_out = refs[:4]
    nb = bits_of(nt) + bits_of(ng)
    tb = bits_of(nt)
    pin_a, small_a, quad = refs[4:7]
    landing = refs[7:7 + 2 * nb]
    ssem, rsem = refs[7 + 2 * nb:]
    t = lax.axis_index("tok")
    g = lax.axis_index("grp")
    steps = steps_of(nt, ng)
    me = t * ng + g
    digits = [(me // (1 << (nb - 1 - j))) % 2 for j in range(nb)]

    def peer(s):
        axis, b = steps[s]
        mask = 1 << b
        return {"tok": t ^ mask, "grp": g} if axis == "tok" else {"tok": t, "grp": g ^ mask}

    greet([peer(s) for s in range(nb)])
    p1, p0 = (t // 2) % 2, t % 2
    flying = []

    def launch(i, src, dst, s):
        copy = pltpu.make_async_remote_copy(
            src_ref=src, dst_ref=dst, send_sem=ssem.at[i], recv_sem=rsem.at[i],
            device_id=peer(s), device_id_type=MESH)
        copy.start()
        flying.append(copy)
        return copy

    def away(s):
        return (slice(None),) * s + (1 - digits[s],) + tuple(digits[s + 1:])

    def kept(s):
        return (slice(None),) * s + tuple(digits[s:])

    def add(ref, at, other, dst, to):
        value = ref[at].astype(F32) + other[...].astype(F32)
        dst[to] = value.astype(dst.dtype)

    for s in reversed(range(nb)):
        first = s == nb - 1
        outer = s >= tb
        sources = [pin_in if first else pin_a, small_in if first else small_a]
        copies = []
        for w in range(2):
            land = landing[w * nb + s]
            i = w * nb + s
            if w == 0 and not outer:
                place = {tb - 1: (p1, p0), tb - 2: (p1, slice(None))}.get(s, (slice(None), slice(None)))
                cut = (slice(None),) * s + (1 - digits[s],) + tuple(digits[s + 1:tb])
                src = quad.at[place + cut]
                copies.append(launch(i, src, src if s >= tb - 2 else land, s))
            else:
                copies.append(launch(i, sources[w].at[away(s)], land, s))
        for w in range(2):
            copies[w].wait_recv()
            land = landing[w * nb + s]
            if w == 0 and not outer:
                if s < tb - 2:
                    at = (slice(None), slice(None)) + (slice(None),) * s + tuple(digits[s:tb])
                    add(quad, at, land, quad, at)
            elif w == 0 and s == tb:
                add(sources[0], kept(s), land, quad, (p1, p0))
            else:
                dst = (pin_a, small_a)[w]
                add(sources[w], kept(s), land, dst, kept(s))
    for copy in flying:
        copy.wait_send()
    pin_out[...] = quad[(slice(None), slice(None)) + tuple(digits[:tb])]
    small_out[...] = small_a[tuple(digits)]


def reduce_small(nt, ng, pin, small):
    nb = bits_of(nt) + bits_of(ng)
    tb = bits_of(nt)
    two = (2,) * nb
    r, c = pin.shape[1:]
    rs = small.shape[1:]
    S = jax.ShapeDtypeStruct
    vm = pl.BlockSpec(memory_space=pltpu.VMEM)
    landing = []
    for w, (shape, dt) in enumerate((((r, c), BF), (rs, F32))):
        for s in range(nb):
            lead = (2,) * s
            if w == 0 and s < tb:
                lead = ((2, 2) + lead) if s < tb - 2 else (1,)
                landing.append(pltpu.VMEM(lead + (shape if s < tb - 2 else (8, 128)), dt))
            else:
                landing.append(pltpu.VMEM(lead + shape, dt))
    return pl.pallas_call(
        functools.partial(reduce_kernel, nt, ng),
        out_shape=[S((2, 2, r, c), BF), S(rs, F32)],
        in_specs=[vm] * 2,
        out_specs=[vm] * 2,
        scratch_shapes=[
            pltpu.VMEM(two + (r, c), BF), pltpu.VMEM(two + rs, F32),
            pltpu.VMEM((2, 2) + (2,) * tb + (r, c), BF),
        ] + landing + [pltpu.SemaphoreType.DMA((2 * nb,)), pltpu.SemaphoreType.DMA((2 * nb,))],
        compiler_params=pltpu.CompilerParams(collective_id=1, has_side_effects=True, vmem_limit_bytes=VMEM_ALL),
        name="reduce_small",
    )(pin.reshape(two + (r, c)), small.reshape(two + rs))


def flip(block, mask):
    count = lax.axis_size("tok")
    return lax.ppermute(block, "tok", [(i, i ^ mask) for i in range(count)])


def gather_all(item):
    return lax.all_gather(item, ("tok", "grp"), axis=0, tiled=True)


def scatter_sum(item):
    return lax.psum_scatter(item, ("tok", "grp"), scatter_dimension=0, tiled=True)


def shards(
    tokens,
    upstream,
    cluster_pos,
    project_in,
    query_bias,
    value_bias,
    project_out,
    output_bias,
    first_gain,
    first_shift,
    expand,
    expand_bias,
    contract,
    contract_bias,
    second_gain,
    second_shift,
):
    inputs = tokens[0]
    count, width = inputs.shape
    positions = cluster_pos[0] % LONG
    heads = positions.shape[0]
    head_dim = width // heads
    span = LONG // count
    mine = heads // span
    offset = lax.axis_index("tok") % span
    total = span * count

    nt = lax.axis_size("tok")
    ng = lax.axis_size("grp")
    devices = nt * ng
    few = query_bias.shape[0]
    strips = expand.shape[1] // width

    pieces = project_in.reshape(few, 3, span, mine, head_dim)
    hollow = jnp.zeros((few, head_dim), BF)
    arranged = []
    for place in range(span):
        columns = []
        for h in range(mine):
            query, key, value = (pieces[:, i, place, h] for i in range(3))
            columns += [hollow, query, value, key] if h == 0 else [query, hollow, key, value]
        arranged.append(jnp.concatenate(columns, axis=1))
    packed = jnp.concatenate(
        [
            query_bias, value_bias, output_bias, first_gain, first_shift,
            contract_bias, second_gain, second_shift, expand_bias,
        ]
    ).astype(F32)
    packed = jnp.pad(packed, (0, 1024 - packed.shape[0])).reshape(8, 128)
    block, own_at, arranged, packed = collect(
        nt, ng, inputs, positions.reshape(span, mine, count), jnp.stack(arranged), [packed]
    )
    wide = jnp.concatenate(
        [project_out, expand.reshape(few, strips, width).transpose(1, 0, 2).reshape(-1, width), contract],
        axis=0,
    )
    wide, packed = lax.optimization_barrier((wide, packed))
    wide = gather_all(wide[None])
    project_out = wide[:, :few]
    expand = wide[:, few : (1 + strips) * few].reshape(devices, strips, few, width)
    expand = expand.transpose(1, 0, 2, 3).reshape(strips, width, width)
    contract = wide[:, (1 + strips) * few :].reshape(strips * width, width)
    block = block.reshape(total, width)
    own_at = own_at.transpose(1, 0, 2).reshape(-1)
    arranged = lax.dynamic_index_in_dim(arranged, offset, 0, False).reshape(width, -1)
    packed = packed.reshape(devices, -1)
    vectors = packed[:, : 8 * few].reshape(devices, 8, few).transpose(1, 0, 2).reshape(8, width)
    expand_bias = packed[:, 8 * few : (8 + strips) * few].reshape(strips, width)
    query_bias, value_bias = vectors[0], vectors[1]
    vectors = jnp.concatenate([vectors[2:], vectors[:2]], axis=0)

    own_query = lax.dynamic_slice_in_dim(query_bias.reshape(heads, head_dim), offset * mine, mine)
    own_value = lax.dynamic_slice_in_dim(value_bias.reshape(heads, head_dim), offset * mine, mine)
    blank = jnp.zeros((head_dim,), F32)
    rows = []
    for h in range(mine):
        parts = [blank, own_query[h], own_value[h], blank] if h == 0 else [own_query[h], blank, blank, own_value[h]]
        rows.append(jnp.concatenate(parts))
    bias_rows = jnp.stack(rows)[:, None]

    *leaving, left, right = fwd(own_at, block, arranged, bias_rows, span)
    came = [leaving[0]] + [flip(leaving[k], k) for k in range(1, span)]
    project_out = project_out.reshape(width, width)
    result, grad_first, *rest = mid(
        came, offset[None].astype(jnp.int32), inputs, upstream[0], project_out, expand, contract,
        vectors, expand_bias,
    )
    sending = rest[:span]
    merged, grad_branch, normed_low, grad_mid, lifted, grad_inner, row_sums, expand_sums = rest[span:]
    landed = [sending[0]] + [flip(sending[k], k) for k in range(1, span)]

    def turn(item):
        item = item.reshape(2, 2, mine * head_dim, width)
        item = jnp.where(offset % 2 == 1, item[:, ::-1], item)
        return jnp.where(offset // 2 == 1, item[::-1], item).reshape(width, width)

    contract_grad = jnp.einsum("rf,rd->fd", lifted, grad_mid, preferred_element_type=F32)
    expand_grad = jnp.einsum("rd,rf->df", normed_low, grad_inner, preferred_element_type=F32)
    turned_grad = jnp.einsum("rd,re->de", merged, grad_branch, preferred_element_type=F32).astype(BF)
    split = span * 2 * head_dim
    project_out_grad = turn(
        jnp.concatenate(
            [
                turned_grad[:split].reshape(span, 2 * head_dim, width),
                turned_grad[split:].reshape(span, head_dim, width),
            ],
            axis=1,
        )
    )
    expand_grad = expand_grad.astype(BF)
    contract_grad = contract_grad.astype(BF)
    wide_grad = jnp.concatenate(
        [project_out_grad.reshape(devices, few, width)]
        + [expand_grad[:, i * width : (i + 1) * width].reshape(devices, few, width) for i in range(strips)]
        + [contract_grad.reshape(devices, strips * few, width)],
        axis=1,
    )
    landed, wide_grad = lax.optimization_barrier((landed, wide_grad))
    wide_grad = scatter_sum(wide_grad)[0].astype(F32)
    project_out_grad = wide_grad[:few]
    expand_grad = wide_grad[few : (1 + strips) * few].reshape(strips, few, width).transpose(1, 0, 2).reshape(few, -1)
    contract_grad = wide_grad[(1 + strips) * few :]
    grad_rows, grad_sums = bwd(own_at, left, right, landed)
    partial = [
        jnp.einsum(
            "re,de->rd", grad_rows[k * count : (k + 1) * count], arranged, preferred_element_type=F32
        )
        for k in range(span)
    ]
    returned = [flip(partial[k].astype(BF), k) for k in range(1, span)]
    arranged_grad = jnp.einsum("rd,re->de", block, grad_rows, preferred_element_type=F32).astype(BF)
    sums = jnp.sum(grad_sums, axis=0).reshape(mine, 4, head_dim)
    query_at = [1] + [0] * (mine - 1)
    key_at = [3] + [2] * (mine - 1)
    value_at = [2] + [3] * (mine - 1)

    def spread(take, at):
        return jnp.stack([take(h, at[h]) for h in range(mine)], axis=-2)

    own_sums = jnp.stack([spread(lambda h, s: sums[h, s], at) for at in (query_at, value_at)])
    bias_grads = lax.dynamic_update_slice_in_dim(
        jnp.zeros((2, heads, head_dim), F32), own_sums, offset * mine, axis=1
    ).reshape(2, width)
    token_grad = grad_first + partial[0]
    for item in returned:
        token_grad = token_grad + item.astype(F32)
    ordered = jnp.concatenate([bias_grads, row_sums[5:6], row_sums[3:5], row_sums[2:3], row_sums[:2]], axis=0)
    small = jnp.concatenate(
        [
            ordered.reshape(8, devices, few).transpose(1, 0, 2).reshape(devices, 8 * few),
            expand_sums.reshape(devices, strips * few),
        ],
        axis=1,
    )
    small = jnp.pad(small, ((0, 0), (0, 1024 - small.shape[1]))).reshape(devices, 8, 128)
    project_in_grad, small = reduce_small(nt, ng, arranged_grad.reshape(devices, few, -1), small)
    project_in_grad = project_in_grad.astype(F32).reshape(span, few, mine, 4, head_dim)
    project_in_grad = jnp.concatenate(
        [
            project_in_grad[place, :, h, at[h]]
            for at in (query_at, key_at, value_at)
            for place in range(span)
            for h in range(mine)
        ],
        axis=1,
    )
    small = small.reshape(-1)
    each = [small[i * few : (i + 1) * few] for i in range(8)] + [small[8 * few : (8 + strips) * few]]
    return (
        result[None],
        token_grad[None],
        project_in_grad,
        each[0],
        each[1],
        project_out_grad,
        each[2],
        each[3],
        each[4],
        expand_grad,
        each[8],
        contract_grad,
        each[5],
        each[6],
        each[7],
    )


def solution(mesh):
    placed = (
        P("grp", "tok", None),
        P("grp", "tok", None),
        P("grp", None, "tok"),
        P(("tok", "grp"), None),
        P(("tok", "grp")),
        P(("tok", "grp")),
        P(("tok", "grp"), None),
        P(("tok", "grp")),
        P(("tok", "grp")),
        P(("tok", "grp")),
        P(("tok", "grp"), None),
        P(("tok", "grp")),
        P(("tok", "grp"), None),
        P(("tok", "grp")),
        P(("tok", "grp")),
        P(("tok", "grp")),
    )
    return jax.shard_map(
        shards,
        mesh=mesh,
        in_specs=placed,
        out_specs=(
            P("grp", "tok", None),
            P("grp", "tok", None),
            P(("tok", "grp"), None),
            P(("tok", "grp")),
            P(("tok", "grp")),
            P(("tok", "grp"), None),
            P(("tok", "grp")),
            P(("tok", "grp")),
            P(("tok", "grp")),
            P(("tok", "grp"), None),
            P(("tok", "grp")),
            P(("tok", "grp"), None),
            P(("tok", "grp")),
            P(("tok", "grp")),
            P(("tok", "grp")),
        ),
        check_vma=False,
    )
```

```python
import functools
import jax
import jax.numpy as jnp
from jax import lax
from jax.experimental import pallas as pl
from jax.experimental.pallas import tpu as pltpu
from jax.sharding import PartitionSpec as P

CL = 128
LONG = 4096
F32 = jnp.float32
BF = jnp.bfloat16
VMEM_ALL = 64 * 1024 * 1024 - 65536

epsilon = 1e-05
root_half = 0.7071067811865476
density_norm = 0.3989422804014327

def normalize(hidden, gain, shift):
    centred = hidden - jnp.mean(hidden, axis=1, keepdims=True)
    inverse_std = lax.rsqrt(jnp.mean(centred * centred, axis=1, keepdims=True) + epsilon)
    unit = centred * inverse_std
    return (unit * gain + shift, unit, inverse_std)


def normalize_back(grad_out, gain, unit, inverse_std):
    scaled = grad_out * gain
    return inverse_std * (
        scaled
        - jnp.mean(scaled, axis=1, keepdims=True)
        - unit * jnp.mean(scaled * unit, axis=1, keepdims=True)
    )


def nt(a,b): return lax.dot_general(a,b,(((1,),(1,)),((),())),preferred_element_type=F32)
def nn(a,b): return lax.dot_general(a,b,(((1,),(0,)),((),())),preferred_element_type=F32)
def tn(a,b): return lax.dot_general(a,b,(((0,),(0,)),((),())),preferred_element_type=F32)

def fwd_kernel(span, pos, tok, w, bias, *refs):
    leave = refs[:span]
    left, right, src, ord_, oc = refs[span:]
    h=pl.program_id(0)
    n=tok.shape[0]
    ch=512
    def proj(i,_):
        r=pl.multiple_of(i*ch,ch)
        acc=nn(tok[pl.ds(r,ch),:],w[...])+bias[0]
        src[pl.ds(2*r,ch,stride=2),:]=acc[:,:128]
        src[pl.ds(2*r+1,ch,stride=2),:]=acc[:,128:]
        return 0
    lax.fori_loop(0,n//ch,proj,0)
    U=64
    def scat(i,_):
        for u in range(U):
            t=i*U+u
            ord_[pl.ds(2*pos[h*n+t],2),:]=src[pl.ds(2*t,2),:]
        return 0
    lax.fori_loop(0,n//U,scat,0)
    CB=16
    def clus(i,_):
        at=[pl.multiple_of((i*CB+u)*CL,CL) for u in range(CB)]
        ls=[ord_[pl.ds(2*r,CL,stride=2),:].astype(BF) for r in at]
        rs=[ord_[pl.ds(2*r+1,CL,stride=2),:].astype(BF) for r in at]
        ss=[nt(rr,l) for rr,l in zip(rs,ls)]
        for r,l,rr in zip(at,ls,rs):
            left[0,pl.ds(r,CL),:]=l
            right[0,pl.ds(r,CL),:]=rr
        es=[jnp.exp((x-jnp.max(x,axis=0,keepdims=True))*0.125) for x in ss]
        ps=[(e*(1.0/jnp.sum(e,axis=0,keepdims=True))).astype(BF) for e in es]
        for r,p,rr in zip(at,ps,rs):
            oc[pl.ds(r,CL),:]=tn(p,rr)
        return 0
    lax.fori_loop(0,n//CL//CB,clus,0)
    def gath(i,_):
        for u in range(U):
            t=i*U+u
            src[pl.ds(t,1),:]=oc[pl.ds(pos[h*n+t],1),:]
        return 0
    lax.fori_loop(0,n//U,gath,0)
    count=n//span
    @pl.when(h==0)
    def _():
        for k in range(span):
            leave[k][:count,:64]=src[k*count:(k+1)*count,:64].astype(BF)
    @pl.when(h==1)
    def _():
        for k in range(span):
            leave[k][:count,64:]=src[k*count:(k+1)*count,64:].astype(BF)
    @pl.when(h==2)
    def _():
        for k in range(span):
            mid_row=k*count+count//2
            leave[k][count:,:64]=src[k*count:mid_row,64:].astype(BF)
            leave[k][count:,64:]=src[mid_row:(k+1)*count,64:].astype(BF)

def fwd(pos,tok,w,bias,span):
    rows=tok.shape[0]//span*3//2
    n=tok.shape[0]; H=pos.shape[0]//n
    return pl.pallas_call(functools.partial(fwd_kernel,span),grid=(H,),
      out_shape=(jax.ShapeDtypeStruct((rows,128),BF),)*span+(jax.ShapeDtypeStruct((H,n,128),BF),)*2,
      in_specs=[pl.BlockSpec(memory_space=pltpu.SMEM),
                pl.BlockSpec((n,tok.shape[1]),lambda h:(0,0)),
                pl.BlockSpec((tok.shape[1],256),lambda h:(0,h)),
                pl.BlockSpec((1,1,256),lambda h: (h, 0, 0))],
      out_specs=(pl.BlockSpec((rows,128),lambda h: (0, 0)),)*span+(pl.BlockSpec((1,n,128),lambda h: (h, 0, 0)),)*2,
      scratch_shapes=[pltpu.VMEM((2*n,128),F32),pltpu.VMEM((2*n,128),F32),pltpu.VMEM((n,128),F32)],
      compiler_params=pltpu.CompilerParams(vmem_limit_bytes=VMEM_ALL),name="att_fwd")(pos,tok,w,bias)

def bwd_kernel(span, pos, left, right, *refs):
    landed = refs[:span]
    gj, total, src, ord_, dc = refs[span:]
    h=pl.program_id(0)
    n=left.shape[1]
    U=64
    count=n//span
    @pl.when(h<2)
    def _():
        for k in range(span):
            src[k*count:(k+1)*count,:]=landed[k][:count,:].astype(F32)
    @pl.when(h==2)
    def _():
        for k in range(span):
            x=landed[k][count:,:].astype(F32)
            mid_row=k*count+count//2
            src[k*count:mid_row,:]=jnp.concatenate([x[:,64:],x[:,:64]],axis=1)
            src[mid_row:(k+1)*count,:]=x
    def scat(i,_):
        for u in range(U):
            t=i*U+u
            ord_[pl.ds(pos[h*n+t],1),:]=src[pl.ds(t,1),:]
        return 0
    lax.fori_loop(0,n//U,scat,0)
    lane=lax.broadcasted_iota(jnp.int32,(CL,128),1)
    mask=(lane<64)==(h==0)
    CB=16
    def clus(i,_):
        at=[pl.multiple_of((i*CB+u)*CL,CL) for u in range(CB)]
        ls=[left[0,pl.ds(r,CL),:] for r in at]
        rs=[right[0,pl.ds(r,CL),:] for r in at]
        gs=[jnp.where(mask,ord_[pl.ds(r,CL),:],0.0).astype(BF) for r in at]
        ss=[nt(rr,l) for rr,l in zip(rs,ls)]
        dps=[nt(rr,d) for rr,d in zip(rs,gs)]
        es=[jnp.exp((x-jnp.max(x,axis=0,keepdims=True))*0.125) for x in ss]
        ps=[e*(1.0/jnp.sum(e,axis=0,keepdims=True)) for e in es]
        dss=[(p*(dp-jnp.sum(dp*p,axis=0,keepdims=True))).astype(BF) for p,dp in zip(ps,dps)]
        for r,ds,p,l,rr,d in zip(at,dss,ps,ls,rs,gs):
            dc[pl.ds(2*r,CL,stride=2),:]=tn(ds,rr)*0.125
            dc[pl.ds(2*r+1,CL,stride=2),:]=nn(ds,l)*0.125+nn(p.astype(BF),d)
        return 0
    lax.fori_loop(0,n//CL//CB,clus,0)
    def gath(i,_):
        for u in range(U):
            t=i*U+u
            src[pl.ds(2*t,2),:]=dc[pl.ds(2*pos[h*n+t],2),:]
        return 0
    lax.fori_loop(0,n//U,gath,0)
    ch=512
    def out(i,sums):
        r=pl.multiple_of(i*ch,ch)
        one=src[pl.ds(2*r,ch,stride=2),:].astype(BF)
        two=src[pl.ds(2*r+1,ch,stride=2),:].astype(BF)
        gj[pl.ds(r,ch),:128]=one
        gj[pl.ds(r,ch),128:]=two
        fold=lambda x: jnp.sum(x.astype(F32).reshape(ch//8,8,128),axis=0)
        return (sums[0]+fold(one),sums[1]+fold(two))
    zero=jnp.zeros((8,128),F32)
    one,two=lax.fori_loop(0,n//ch,out,(zero,zero))
    total[:,:128]=one
    total[:,128:]=two

def bwd(pos,left,right,landed):
    H,n=left.shape[:2]
    span=len(landed)
    rows=landed[0].shape[0]
    blk=lambda: pl.BlockSpec((1,n,128),lambda h: (h, 0, 0))
    return pl.pallas_call(functools.partial(bwd_kernel,span),grid=(H,),
      out_shape=(jax.ShapeDtypeStruct((n,H*256),BF),jax.ShapeDtypeStruct((8,H*256),F32)),
      in_specs=[pl.BlockSpec(memory_space=pltpu.SMEM),blk(),blk()]+[pl.BlockSpec((rows,128),lambda h: (0, 0))]*span,
      out_specs=(pl.BlockSpec((n,256),lambda h: (0, h)),pl.BlockSpec((8,256),lambda h: (0, h))),
      scratch_shapes=[pltpu.VMEM((2*n,128),F32),pltpu.VMEM((n,128),F32),pltpu.VMEM((2*n,128),F32)],
      compiler_params=pltpu.CompilerParams(vmem_limit_bytes=VMEM_ALL),name="att_bwd")(pos,left,right,*landed)

def mid_kernel(span, *refs):
    came = refs[:span]
    at, tok, up, wo, we, wc, vec, ebias = refs[span:span + 8]
    result, gfirst = refs[span + 8:span + 10]
    leave = refs[span + 10:2 * span + 10]
    merged_o, gbranch_o, nlow_o, gmid_o, lifted_o, ginner_o, sums, esum = refs[2 * span + 10:2 * span + 18]
    wop, slope = refs[2 * span + 18:]
    i = pl.program_id(0)
    rows, width = tok.shape
    half = rows * pl.num_programs(0) // 2
    strips = we.shape[0]
    own = width // span
    pair = 128
    single = own - pair

    @pl.when(i == 0)
    def _():
        for k in range(span):
            p = pl.multiple_of((at[0] ^ k) * own, 64)
            wop[k * pair:(k + 1) * pair, :] = wo[pl.ds(p, pair), :]
            wop[span * pair + k * single:span * pair + (k + 1) * single, :] = wo[pl.ds(p + pair, single), :]
        sums[...] = jnp.zeros_like(sums)
        esum[...] = jnp.zeros_like(esum)

    def total(at_row, value):
        sums[at_row:at_row + 1, :] += jnp.sum(value, axis=0, keepdims=True)

    low = i * rows < half
    start = pl.multiple_of(2 * half + lax.rem(i * rows, half), rows)
    pairs = [c[pl.ds(pl.multiple_of(i * rows, rows), rows), :] for c in came]
    both = [c[pl.ds(start, rows), :] for c in came]
    singles = [jnp.where(low, x[:, :single], x[:, single:]) for x in both]
    merged = jnp.concatenate(pairs + singles, axis=1)
    merged_o[...] = merged
    hidden = tok[...].astype(F32) + nn(merged, wop[...]) + vec[0:1, :]
    normed_one, unit_one, inverse_one = normalize(hidden, vec[1:2, :], vec[2:3, :])
    normed_low = normed_one.astype(BF)
    nlow_o[...] = normed_low
    second = normed_one + vec[3:4, :]
    for k in range(strips):
        cols = slice(k * width, (k + 1) * width)
        inner = nn(normed_low, we[k]) + ebias[k:k + 1, :]
        cdf = 0.5 * (1.0 + lax.erf(inner * root_half))
        lifted = (inner * cdf).astype(BF)
        slope[:, cols] = cdf + inner * jnp.exp(-0.5 * inner * inner) * density_norm
        lifted_o[:, cols] = lifted
        second += nn(lifted, wc[cols, :])
    out, unit_two, inverse_two = normalize(second, vec[4:5, :], vec[5:6, :])
    result[...] = out.astype(BF)
    cotangent = up[...].astype(F32)
    total(0, cotangent * unit_two)
    total(1, cotangent)
    grad_second = normalize_back(cotangent, vec[4:5, :], unit_two, inverse_two)
    grad_mid = grad_second.astype(BF)
    gmid_o[...] = grad_mid
    total(2, grad_mid.astype(F32))
    grad_normed = grad_second
    for k in range(strips):
        cols = slice(k * width, (k + 1) * width)
        grad_inner = (nt(grad_mid, wc[cols, :]) * slope[:, cols]).astype(BF)
        ginner_o[:, cols] = grad_inner
        esum[k:k + 1, :] += jnp.sum(grad_inner.astype(F32), axis=0, keepdims=True)
        grad_normed += nt(grad_inner, we[k])
    total(3, grad_normed * unit_one)
    total(4, grad_normed)
    grad_first = normalize_back(grad_normed, vec[1:2, :], unit_one, inverse_one)
    gfirst[...] = grad_first
    grad_branch = grad_first.astype(BF)
    gbranch_o[...] = grad_branch
    total(5, grad_branch.astype(F32))
    grad_merged = nt(grad_branch, wop[...]).astype(BF)
    for k in range(span):
        leave[k][pl.ds(pl.multiple_of(i * rows, rows), rows), :] = grad_merged[:, k * pair:(k + 1) * pair]
        one = grad_merged[:, span * pair + k * single:span * pair + (k + 1) * single]

        @pl.when(low)
        def _():
            leave[k][pl.ds(start, rows), :single] = one

        @pl.when(jnp.logical_not(low))
        def _():
            leave[k][pl.ds(start, rows), single:] = one


def mid(came, at, tok, up, wo, we, wc, vec, ebias, rows=256):
    span = len(came)
    count, width = tok.shape
    strips = we.shape[0]
    S = jax.ShapeDtypeStruct
    vm = pl.BlockSpec(memory_space=pltpu.VMEM)
    tile = lambda w: pl.BlockSpec((rows, w), lambda i: (i, 0))
    fixed = lambda shape: pl.BlockSpec(shape, lambda i: (0, 0))
    deep = strips * width
    outs = (
        [(S((count, width), BF), tile(width)), (S((count, width), F32), tile(width))]
        + [(S(came[0].shape, BF), fixed(came[0].shape))] * span
        + [(S((count, width), BF), tile(width))] * 4
        + [(S((count, deep), BF), tile(deep))] * 2
        + [(S((8, width), F32), fixed((8, width))), (S((strips, width), F32), fixed((strips, width)))]
    )
    return pl.pallas_call(
        functools.partial(mid_kernel, span),
        grid=(count // rows,),
        out_shape=[o for o, _ in outs],
        in_specs=[vm] * span + [pl.BlockSpec(memory_space=pltpu.SMEM), tile(width), tile(width)] + [vm] * 5,
        out_specs=[b for _, b in outs],
        scratch_shapes=[pltpu.VMEM((width, width), BF), pltpu.VMEM((rows, deep), F32)],
        compiler_params=pltpu.CompilerParams(vmem_limit_bytes=VMEM_ALL),
        name="mid",
    )(*came, at, tok, up, wo, we, wc, vec, ebias)

MESH = pl.DeviceIdType.MESH


def bits_of(size):
    return size.bit_length() - 1


def steps_of(nt, ng):
    return [("tok", b) for b in reversed(range(bits_of(nt)))] + [
        ("grp", b) for b in reversed(range(bits_of(ng)))
    ]


def greet(peers):
    barrier = pltpu.get_barrier_semaphore()
    for peer in peers:
        pl.semaphore_signal(barrier, inc=1, device_id=peer, device_id_type=MESH)
    pl.semaphore_wait(barrier, len(peers))


def collect_kernel(nt, ng, parts, *refs):
    tok_in, pos_in, pin_in = refs[:3]
    nf = (len(refs) - 13) // 2
    full_in = refs[3:3 + nf]
    tok_out, pos_out, pin_out = refs[3 + nf:6 + nf]
    full_out = refs[6 + nf:6 + 2 * nf]
    lsem, tsend, trecv, psend, precv, wsend, wrecv = refs[6 + 2 * nf:]
    t = lax.axis_index("tok")
    g = lax.axis_index("grp")
    steps = steps_of(nt, ng)
    nb = len(steps)
    me = t * ng + g
    digits = [(me // (1 << (nb - 1 - j))) % 2 for j in range(nb)]

    def held_at(s):
        return (slice(None),) * s + tuple(digits[s:])

    def peer(axis, mask):
        return {"tok": t ^ mask, "grp": g} if axis == "tok" else {"tok": t, "grp": g ^ mask}

    count = tok_in.shape[0]
    own = [pltpu.make_async_copy(tok_in, tok_out.at[0], lsem.at[0]),
           pltpu.make_async_copy(pos_in.at[t % 4], pos_out.at[0], lsem.at[1])]
    for i, (a, b) in enumerate(zip(full_in, full_out)):
        own.append(pltpu.make_async_copy(a, b.at[held_at(0)], lsem.at[2 + i]))
    greet([peer(axis, 1 << b) for axis, b in steps] + [peer("tok", 3)])
    for copy in own:
        copy.start()

    flights = {}

    def send(name, src, dst, sems, to):
        copy = pltpu.make_async_remote_copy(
            src_ref=src, dst_ref=dst, send_sem=sems[0], recv_sem=sems[1],
            device_id=to, device_id_type=MESH)
        copy.start()
        flights[name] = copy

    arrived = set()

    def wait(name):
        if name not in arrived:
            arrived.add(name)
            flights[name].wait_recv()

    chunk = count // parts

    def rows(c):
        return pl.ds(c * chunk, chunk)

    def token(c, mask):
        i = (mask - 1) * parts + c
        send(("t", mask, c), tok_in.at[rows(c)], tok_out.at[mask, rows(c)],
             (tsend.at[i], trecv.at[i]), peer("tok", mask))

    def relay(c):
        i = 2 * parts + c
        mask = 2 if c >= parts // 2 else 1
        wait(("t", 3 - mask, c))
        send(("r", c), tok_out.at[3 - mask, rows(c)], tok_out.at[3, rows(c)],
             (tsend.at[i], trecv.at[i]), peer("tok", mask))

    def position(mask):
        i = mask - 1
        send(("p", mask), pos_in.at[(t ^ mask) % 4], pos_out.at[mask],
             (psend.at[i], precv.at[i]), peer("tok", mask))

    def full(w, s):
        axis, b = steps[s]
        i = w * nb + s
        to = peer(axis, 1 << b)
        out = full_out[w]
        if s == 0:
            src, dst = full_in[w], out.at[held_at(0)]
        else:
            wait(("w", w, s - 1))
            if s == 1:
                own[2 + w].wait()
            src = out.at[held_at(s)]
            dst = src
        send(("w", w, s), src, dst, (wsend.at[i], wrecv.at[i]), to)

    def slices(s):
        axis, b = steps[s]
        i = nf * nb + s
        to = peer(axis, 1 << b)
        tb = bits_of(nt)
        if s > 0:
            wait(("w", nf, s - 1))
        high = tb - 2
        theirs = (t ^ (1 << b)) if axis == "tok" else t
        if s < high:
            place = (slice(None), slice(None))
        elif s == high:
            place = ((theirs // 2) % 2, slice(None))
        else:
            place = ((theirs // 2) % 2, theirs % 2)
        src = pin_out.at[place + held_at(s)]
        send(("w", nf, s), src, src, (wsend.at[i], wrecv.at[i]), to)

    pin_own = pltpu.make_async_copy(pin_in, pin_out.at[(slice(None), slice(None)) + held_at(0)], lsem.at[2 + nf])
    pin_own.start()
    order = list(range(nf))
    half = parts // 2
    for c in range(half):
        token(c, 1)
    for w in order:
        full(w, 0)
    pin_own.wait()
    slices(0)
    for mask in (1, 2, 3):
        position(mask)
    token(0, 2)
    done_y, done_z = half, 1
    for s in range(1, nb):
        for w in order:
            full(w, s)
            if w >= 0:
                if done_z < parts:
                    token(done_z, 2)
                    done_z += 1
                if done_y < parts and s >= 2:
                    token(done_y, 1)
                    done_y += 1
        slices(s)
        if s == nb - 2:
            for c in range(done_z, parts):
                token(c, 2)
            for c in range(done_y, parts):
                token(c, 1)
            for c in range(parts):
                relay(c)
    own[0].wait()
    own[1].wait()
    if nb == 1:
        for w in range(nf):
            own[2 + w].wait()
    for name in flights:
        wait(name)
    for copy in flights.values():
        copy.wait_send()


def collect(nt, ng, tokens, pos, pin, fulls, parts=4):
    n = nt * ng
    nb = bits_of(nt) + bits_of(ng)
    hbm = pl.BlockSpec(memory_space=pl.ANY)
    vm = pl.BlockSpec(memory_space=pltpu.VMEM)
    S = jax.ShapeDtypeStruct
    block, at, own, *wide = pl.pallas_call(
        functools.partial(collect_kernel, nt, ng, parts),
        out_shape=[S((4,) + tokens.shape, tokens.dtype), S((4,) + pos.shape[1:], pos.dtype),
                   S((2, 2) + (2,) * nb + pin.shape[1:], pin.dtype)] + [S((2,) * nb + f.shape, f.dtype) for f in fulls],
        in_specs=[vm] * (3 + len(fulls)),
        out_specs=[hbm] * (3 + len(fulls)),
        scratch_shapes=[
            pltpu.SemaphoreType.DMA((3 + len(fulls),)),
            pltpu.SemaphoreType.DMA((3 * parts,)), pltpu.SemaphoreType.DMA((3 * parts,)),
            pltpu.SemaphoreType.DMA((3,)), pltpu.SemaphoreType.DMA((3,)),
            pltpu.SemaphoreType.DMA(((len(fulls) + 1) * nb,)), pltpu.SemaphoreType.DMA(((len(fulls) + 1) * nb,)),
        ],
        compiler_params=pltpu.CompilerParams(collective_id=0, has_side_effects=True),
        name="collect",
    )(tokens, pos, pin.reshape((2, 2) + pin.shape[1:]), *fulls)
    return [block, at, own.reshape((4, n) + pin.shape[1:])] + [
        w.reshape((n,) + f.shape) for w, f in zip(wide, fulls)]


def reduce_kernel(nt, ng, *refs):
    pin_in, small_in, pin_out, small_out = refs[:4]
    nb = bits_of(nt) + bits_of(ng)
    tb = bits_of(nt)
    pin_a, small_a, quad = refs[4:7]
    landing = refs[7:7 + 2 * nb]
    ssem, rsem = refs[7 + 2 * nb:]
    t = lax.axis_index("tok")
    g = lax.axis_index("grp")
    steps = steps_of(nt, ng)
    me = t * ng + g
    digits = [(me // (1 << (nb - 1 - j))) % 2 for j in range(nb)]

    def peer(s):
        axis, b = steps[s]
        mask = 1 << b
        return {"tok": t ^ mask, "grp": g} if axis == "tok" else {"tok": t, "grp": g ^ mask}

    greet([peer(s) for s in range(nb)])
    p1, p0 = (t // 2) % 2, t % 2
    flying = []

    def launch(i, src, dst, s):
        copy = pltpu.make_async_remote_copy(
            src_ref=src, dst_ref=dst, send_sem=ssem.at[i], recv_sem=rsem.at[i],
            device_id=peer(s), device_id_type=MESH)
        copy.start()
        flying.append(copy)
        return copy

    def away(s):
        return (slice(None),) * s + (1 - digits[s],) + tuple(digits[s + 1:])

    def kept(s):
        return (slice(None),) * s + tuple(digits[s:])

    def add(ref, at, other, dst, to):
        value = ref[at].astype(F32) + other[...].astype(F32)
        dst[to] = value.astype(dst.dtype)

    for s in reversed(range(nb)):
        first = s == nb - 1
        outer = s >= tb
        sources = [pin_in if first else pin_a, small_in if first else small_a]
        copies = []
        for w in range(2):
            land = landing[w * nb + s]
            i = w * nb + s
            if w == 0 and not outer:
                place = {tb - 1: (p1, p0), tb - 2: (p1, slice(None))}.get(s, (slice(None), slice(None)))
                cut = (slice(None),) * s + (1 - digits[s],) + tuple(digits[s + 1:tb])
                src = quad.at[place + cut]
                copies.append(launch(i, src, src if s >= tb - 2 else land, s))
            else:
                copies.append(launch(i, sources[w].at[away(s)], land, s))
        for w in range(2):
            copies[w].wait_recv()
            land = landing[w * nb + s]
            if w == 0 and not outer:
                if s < tb - 2:
                    at = (slice(None), slice(None)) + (slice(None),) * s + tuple(digits[s:tb])
                    add(quad, at, land, quad, at)
            elif w == 0 and s == tb:
                add(sources[0], kept(s), land, quad, (p1, p0))
            else:
                dst = (pin_a, small_a)[w]
                add(sources[w], kept(s), land, dst, kept(s))
    for copy in flying:
        copy.wait_send()
    pin_out[...] = quad[(slice(None), slice(None)) + tuple(digits[:tb])]
    small_out[...] = small_a[tuple(digits)]


def reduce_small(nt, ng, pin, small):
    nb = bits_of(nt) + bits_of(ng)
    tb = bits_of(nt)
    two = (2,) * nb
    r, c = pin.shape[1:]
    rs = small.shape[1:]
    S = jax.ShapeDtypeStruct
    vm = pl.BlockSpec(memory_space=pltpu.VMEM)
    landing = []
    for w, (shape, dt) in enumerate((((r, c), BF), (rs, F32))):
        for s in range(nb):
            lead = (2,) * s
            if w == 0 and s < tb:
                lead = ((2, 2) + lead) if s < tb - 2 else (1,)
                landing.append(pltpu.VMEM(lead + (shape if s < tb - 2 else (8, 128)), dt))
            else:
                landing.append(pltpu.VMEM(lead + shape, dt))
    return pl.pallas_call(
        functools.partial(reduce_kernel, nt, ng),
        out_shape=[S((2, 2, r, c), BF), S(rs, F32)],
        in_specs=[vm] * 2,
        out_specs=[vm] * 2,
        scratch_shapes=[
            pltpu.VMEM(two + (r, c), BF), pltpu.VMEM(two + rs, F32),
            pltpu.VMEM((2, 2) + (2,) * tb + (r, c), BF),
        ] + landing + [pltpu.SemaphoreType.DMA((2 * nb,)), pltpu.SemaphoreType.DMA((2 * nb,))],
        compiler_params=pltpu.CompilerParams(collective_id=1, has_side_effects=True, vmem_limit_bytes=VMEM_ALL),
        name="reduce_small",
    )(pin.reshape(two + (r, c)), small.reshape(two + rs))


def flip(block, mask):
    count = lax.axis_size("tok")
    return lax.ppermute(block, "tok", [(i, i ^ mask) for i in range(count)])


def gather_all(item):
    return lax.all_gather(item, ("tok", "grp"), axis=0, tiled=True)


def scatter_sum(item):
    return lax.psum_scatter(item, ("tok", "grp"), scatter_dimension=0, tiled=True)


def shards(
    tokens,
    upstream,
    cluster_pos,
    project_in,
    query_bias,
    value_bias,
    project_out,
    output_bias,
    first_gain,
    first_shift,
    expand,
    expand_bias,
    contract,
    contract_bias,
    second_gain,
    second_shift,
):
    inputs = tokens[0]
    count, width = inputs.shape
    positions = cluster_pos[0] % LONG
    heads = positions.shape[0]
    head_dim = width // heads
    span = LONG // count
    mine = heads // span
    offset = lax.axis_index("tok") % span
    total = span * count

    nt = lax.axis_size("tok")
    ng = lax.axis_size("grp")
    devices = nt * ng
    few = query_bias.shape[0]
    strips = expand.shape[1] // width

    pieces = project_in.reshape(few, 3, span, mine, head_dim)
    hollow = jnp.zeros((few, head_dim), BF)
    arranged = []
    for place in range(span):
        columns = []
        for h in range(mine):
            query, key, value = (pieces[:, i, place, h] for i in range(3))
            columns += [hollow, query, value, key] if h == 0 else [query, hollow, key, value]
        arranged.append(jnp.concatenate(columns, axis=1))
    packed = jnp.concatenate(
        [
            query_bias, value_bias, output_bias, first_gain, first_shift,
            contract_bias, second_gain, second_shift, expand_bias,
        ]
    ).astype(F32)
    packed = jnp.pad(packed, (0, 1024 - packed.shape[0])).reshape(8, 128)
    block, own_at, arranged, packed = collect(
        nt, ng, inputs, positions.reshape(span, mine, count), jnp.stack(arranged), [packed]
    )
    wide = jnp.concatenate(
        [project_out, expand.reshape(few, strips, width).transpose(1, 0, 2).reshape(-1, width), contract],
        axis=0,
    )
    wide, packed = lax.optimization_barrier((wide, packed))
    wide = gather_all(wide[None])
    project_out = wide[:, :few]
    expand = wide[:, few : (1 + strips) * few].reshape(devices, strips, few, width)
    expand = expand.transpose(1, 0, 2, 3).reshape(strips, width, width)
    contract = wide[:, (1 + strips) * few :].reshape(strips * width, width)
    block = block.reshape(total, width)
    own_at = own_at.transpose(1, 0, 2).reshape(-1)
    arranged = lax.dynamic_index_in_dim(arranged, offset, 0, False).reshape(width, -1)
    packed = packed.reshape(devices, -1)
    vectors = packed[:, : 8 * few].reshape(devices, 8, few).transpose(1, 0, 2).reshape(8, width)
    expand_bias = packed[:, 8 * few : (8 + strips) * few].reshape(strips, width)
    query_bias, value_bias = vectors[0], vectors[1]
    vectors = jnp.concatenate([vectors[2:], vectors[:2]], axis=0)

    own_query = lax.dynamic_slice_in_dim(query_bias.reshape(heads, head_dim), offset * mine, mine)
    own_value = lax.dynamic_slice_in_dim(value_bias.reshape(heads, head_dim), offset * mine, mine)
    blank = jnp.zeros((head_dim,), F32)
    rows = []
    for h in range(mine):
        parts = [blank, own_query[h], own_value[h], blank] if h == 0 else [own_query[h], blank, blank, own_value[h]]
        rows.append(jnp.concatenate(parts))
    bias_rows = jnp.stack(rows)[:, None]

    *leaving, left, right = fwd(own_at, block, arranged, bias_rows, span)
    came = [leaving[0]] + [flip(leaving[k], k) for k in range(1, span)]
    project_out = project_out.reshape(width, width)
    result, grad_first, *rest = mid(
        came, offset[None].astype(jnp.int32), inputs, upstream[0], project_out, expand, contract,
        vectors, expand_bias,
    )
    sending = rest[:span]
    merged, grad_branch, normed_low, grad_mid, lifted, grad_inner, row_sums, expand_sums = rest[span:]
    landed = [sending[0]] + [flip(sending[k], k) for k in range(1, span)]

    def turn(item):
        item = item.reshape(2, 2, mine * head_dim, width)
        item = jnp.where(offset % 2 == 1, item[:, ::-1], item)
        return jnp.where(offset // 2 == 1, item[::-1], item).reshape(width, width)

    contract_grad = jnp.einsum("rf,rd->fd", lifted, grad_mid, preferred_element_type=F32)
    expand_grad = jnp.einsum("rd,rf->df", normed_low, grad_inner, preferred_element_type=F32)
    turned_grad = jnp.einsum("rd,re->de", merged, grad_branch, preferred_element_type=F32).astype(BF)
    split = span * 2 * head_dim
    project_out_grad = turn(
        jnp.concatenate(
            [
                turned_grad[:split].reshape(span, 2 * head_dim, width),
                turned_grad[split:].reshape(span, head_dim, width),
            ],
            axis=1,
        )
    )
    expand_grad = expand_grad.astype(BF)
    contract_grad = contract_grad.astype(BF)
    wide_grad = jnp.concatenate(
        [project_out_grad.reshape(devices, few, width)]
        + [expand_grad[:, i * width : (i + 1) * width].reshape(devices, few, width) for i in range(strips)]
        + [contract_grad.reshape(devices, strips * few, width)],
        axis=1,
    )
    landed, held = lax.optimization_barrier((landed, wide_grad))
    wide_grad = scatter_sum(wide_grad)[0].astype(F32)
    project_out_grad = wide_grad[:few]
    expand_grad = wide_grad[few : (1 + strips) * few].reshape(strips, few, width).transpose(1, 0, 2).reshape(few, -1)
    contract_grad = wide_grad[(1 + strips) * few :]
    grad_rows, grad_sums = bwd(own_at, left, right, landed)
    partial = [
        jnp.einsum(
            "re,de->rd", grad_rows[k * count : (k + 1) * count], arranged, preferred_element_type=F32
        )
        for k in range(span)
    ]
    returned = [flip(partial[k].astype(BF), k) for k in range(1, span)]
    arranged_grad = jnp.einsum("rd,re->de", block, grad_rows, preferred_element_type=F32).astype(BF)
    sums = jnp.sum(grad_sums, axis=0).reshape(mine, 4, head_dim)
    query_at = [1] + [0] * (mine - 1)
    key_at = [3] + [2] * (mine - 1)
    value_at = [2] + [3] * (mine - 1)

    def spread(take, at):
        return jnp.stack([take(h, at[h]) for h in range(mine)], axis=-2)

    own_sums = jnp.stack([spread(lambda h, s: sums[h, s], at) for at in (query_at, value_at)])
    bias_grads = lax.dynamic_update_slice_in_dim(
        jnp.zeros((2, heads, head_dim), F32), own_sums, offset * mine, axis=1
    ).reshape(2, width)
    token_grad = grad_first + partial[0]
    for item in returned:
        token_grad = token_grad + item.astype(F32)
    ordered = jnp.concatenate([bias_grads, row_sums[5:6], row_sums[3:5], row_sums[2:3], row_sums[:2]], axis=0)
    small = jnp.concatenate(
        [
            ordered.reshape(8, devices, few).transpose(1, 0, 2).reshape(devices, 8 * few),
            expand_sums.reshape(devices, strips * few),
        ],
        axis=1,
    )
    small = jnp.pad(small, ((0, 0), (0, 1024 - small.shape[1]))).reshape(devices, 8, 128)
    project_in_grad, small = reduce_small(nt, ng, arranged_grad.reshape(devices, few, -1), small)
    project_in_grad = project_in_grad.astype(F32).reshape(span, few, mine, 4, head_dim)
    project_in_grad = jnp.concatenate(
        [
            project_in_grad[place, :, h, at[h]]
            for at in (query_at, key_at, value_at)
            for place in range(span)
            for h in range(mine)
        ],
        axis=1,
    )
    small = small.reshape(-1)
    each = [small[i * few : (i + 1) * few] for i in range(8)] + [small[8 * few : (8 + strips) * few]]
    return (
        result[None],
        token_grad[None],
        project_in_grad,
        each[0],
        each[1],
        project_out_grad,
        each[2],
        each[3],
        each[4],
        expand_grad,
        each[8],
        contract_grad,
        each[5],
        each[6],
        each[7],
    )


def solution(mesh):
    placed = (
        P("grp", "tok", None),
        P("grp", "tok", None),
        P("grp", None, "tok"),
        P(("tok", "grp"), None),
        P(("tok", "grp")),
        P(("tok", "grp")),
        P(("tok", "grp"), None),
        P(("tok", "grp")),
        P(("tok", "grp")),
        P(("tok", "grp")),
        P(("tok", "grp"), None),
        P(("tok", "grp")),
        P(("tok", "grp"), None),
        P(("tok", "grp")),
        P(("tok", "grp")),
        P(("tok", "grp")),
    )
    return jax.shard_map(
        shards,
        mesh=mesh,
        in_specs=placed,
        out_specs=(
            P("grp", "tok", None),
            P("grp", "tok", None),
            P(("tok", "grp"), None),
            P(("tok", "grp")),
            P(("tok", "grp")),
            P(("tok", "grp"), None),
            P(("tok", "grp")),
            P(("tok", "grp")),
            P(("tok", "grp")),
            P(("tok", "grp"), None),
            P(("tok", "grp")),
            P(("tok", "grp"), None),
            P(("tok", "grp")),
            P(("tok", "grp")),
            P(("tok", "grp")),
        ),
        check_vma=False,
    )
```

```python
import functools
import jax
import jax.numpy as jnp
from jax import lax
from jax.experimental import pallas as pl
from jax.experimental.pallas import tpu as pltpu
from jax.sharding import PartitionSpec as P

CL = 128
LONG = 4096
F32 = jnp.float32
BF = jnp.bfloat16
VMEM_ALL = 64 * 1024 * 1024 - 65536

epsilon = 1e-05
root_half = 0.7071067811865476
density_norm = 0.3989422804014327

def normalize(hidden, gain, shift):
    centred = hidden - jnp.mean(hidden, axis=1, keepdims=True)
    inverse_std = lax.rsqrt(jnp.mean(centred * centred, axis=1, keepdims=True) + epsilon)
    unit = centred * inverse_std
    return (unit * gain + shift, unit, inverse_std)


def normalize_back(grad_out, gain, unit, inverse_std):
    scaled = grad_out * gain
    return inverse_std * (
        scaled
        - jnp.mean(scaled, axis=1, keepdims=True)
        - unit * jnp.mean(scaled * unit, axis=1, keepdims=True)
    )


def nt(a,b): return lax.dot_general(a,b,(((1,),(1,)),((),())),preferred_element_type=F32)
def nn(a,b): return lax.dot_general(a,b,(((1,),(0,)),((),())),preferred_element_type=F32)
def tn(a,b): return lax.dot_general(a,b,(((0,),(0,)),((),())),preferred_element_type=F32)

def fwd_kernel(span, pos, tok, w, bias, *refs):
    leave = refs[:span]
    left, right, src, ord_, oc = refs[span:]
    h=pl.program_id(0)
    n=tok.shape[0]
    ch=512
    def proj(i,_):
        r=pl.multiple_of(i*ch,ch)
        acc=nn(tok[pl.ds(r,ch),:],w[...])+bias[0]
        src[pl.ds(2*r,ch,stride=2),:]=acc[:,:128]
        src[pl.ds(2*r+1,ch,stride=2),:]=acc[:,128:]
        return 0
    lax.fori_loop(0,n//ch,proj,0)
    U=64
    def scat(i,_):
        for u in range(U):
            t=i*U+u
            ord_[pl.ds(2*pos[h*n+t],2),:]=src[pl.ds(2*t,2),:]
        return 0
    lax.fori_loop(0,n//U,scat,0)
    CB=16
    def clus(i,_):
        at=[pl.multiple_of((i*CB+u)*CL,CL) for u in range(CB)]
        ls=[ord_[pl.ds(2*r,CL,stride=2),:].astype(BF) for r in at]
        rs=[ord_[pl.ds(2*r+1,CL,stride=2),:].astype(BF) for r in at]
        ss=[nt(rr,l) for rr,l in zip(rs,ls)]
        for r,l,rr in zip(at,ls,rs):
            left[0,pl.ds(r,CL),:]=l
            right[0,pl.ds(r,CL),:]=rr
        es=[jnp.exp((x-jnp.max(x,axis=0,keepdims=True))*0.125) for x in ss]
        ps=[(e*(1.0/jnp.sum(e,axis=0,keepdims=True))).astype(BF) for e in es]
        for r,p,rr in zip(at,ps,rs):
            oc[pl.ds(r,CL),:]=tn(p,rr)
        return 0
    lax.fori_loop(0,n//CL//CB,clus,0)
    def gath(i,_):
        for u in range(U):
            t=i*U+u
            src[pl.ds(t,1),:]=oc[pl.ds(pos[h*n+t],1),:]
        return 0
    lax.fori_loop(0,n//U,gath,0)
    count=n//span
    @pl.when(h==0)
    def _():
        for k in range(span):
            leave[k][:count,:64]=src[k*count:(k+1)*count,:64].astype(BF)
    @pl.when(h==1)
    def _():
        for k in range(span):
            leave[k][:count,64:]=src[k*count:(k+1)*count,64:].astype(BF)
    @pl.when(h==2)
    def _():
        for k in range(span):
            mid_row=k*count+count//2
            leave[k][count:,:64]=src[k*count:mid_row,64:].astype(BF)
            leave[k][count:,64:]=src[mid_row:(k+1)*count,64:].astype(BF)

def fwd(pos,tok,w,bias,span):
    rows=tok.shape[0]//span*3//2
    n=tok.shape[0]; H=pos.shape[0]//n
    return pl.pallas_call(functools.partial(fwd_kernel,span),grid=(H,),
      out_shape=(jax.ShapeDtypeStruct((rows,128),BF),)*span+(jax.ShapeDtypeStruct((H,n,128),BF),)*2,
      in_specs=[pl.BlockSpec(memory_space=pltpu.SMEM),
                pl.BlockSpec((n,tok.shape[1]),lambda h:(0,0)),
                pl.BlockSpec((tok.shape[1],256),lambda h:(0,h)),
                pl.BlockSpec((1,1,256),lambda h: (h, 0, 0))],
      out_specs=(pl.BlockSpec((rows,128),lambda h: (0, 0)),)*span+(pl.BlockSpec((1,n,128),lambda h: (h, 0, 0)),)*2,
      scratch_shapes=[pltpu.VMEM((2*n,128),F32),pltpu.VMEM((2*n,128),F32),pltpu.VMEM((n,128),F32)],
      compiler_params=pltpu.CompilerParams(vmem_limit_bytes=VMEM_ALL),name="att_fwd")(pos,tok,w,bias)

def bwd_kernel(span, pos, left, right, *refs):
    landed = refs[:span]
    gj, total, src, ord_, dc = refs[span:]
    h=pl.program_id(0)
    n=left.shape[1]
    U=64
    count=n//span
    @pl.when(h<2)
    def _():
        for k in range(span):
            src[k*count:(k+1)*count,:]=landed[k][:count,:].astype(F32)
    @pl.when(h==2)
    def _():
        for k in range(span):
            x=landed[k][count:,:].astype(F32)
            mid_row=k*count+count//2
            src[k*count:mid_row,:]=jnp.concatenate([x[:,64:],x[:,:64]],axis=1)
            src[mid_row:(k+1)*count,:]=x
    def scat(i,_):
        for u in range(U):
            t=i*U+u
            ord_[pl.ds(pos[h*n+t],1),:]=src[pl.ds(t,1),:]
        return 0
    lax.fori_loop(0,n//U,scat,0)
    lane=lax.broadcasted_iota(jnp.int32,(CL,128),1)
    mask=(lane<64)==(h==0)
    CB=16
    def clus(i,_):
        at=[pl.multiple_of((i*CB+u)*CL,CL) for u in range(CB)]
        ls=[left[0,pl.ds(r,CL),:] for r in at]
        rs=[right[0,pl.ds(r,CL),:] for r in at]
        gs=[jnp.where(mask,ord_[pl.ds(r,CL),:],0.0).astype(BF) for r in at]
        ss=[nt(rr,l) for rr,l in zip(rs,ls)]
        dps=[nt(rr,d) for rr,d in zip(rs,gs)]
        es=[jnp.exp((x-jnp.max(x,axis=0,keepdims=True))*0.125) for x in ss]
        ps=[e*(1.0/jnp.sum(e,axis=0,keepdims=True)) for e in es]
        dss=[(p*(dp-jnp.sum(dp*p,axis=0,keepdims=True))).astype(BF) for p,dp in zip(ps,dps)]
        for r,ds,p,l,rr,d in zip(at,dss,ps,ls,rs,gs):
            dc[pl.ds(2*r,CL,stride=2),:]=tn(ds,rr)*0.125
            dc[pl.ds(2*r+1,CL,stride=2),:]=nn(ds,l)*0.125+nn(p.astype(BF),d)
        return 0
    lax.fori_loop(0,n//CL//CB,clus,0)
    def gath(i,_):
        for u in range(U):
            t=i*U+u
            src[pl.ds(2*t,2),:]=dc[pl.ds(2*pos[h*n+t],2),:]
        return 0
    lax.fori_loop(0,n//U,gath,0)
    ch=512
    def out(i,sums):
        r=pl.multiple_of(i*ch,ch)
        one=src[pl.ds(2*r,ch,stride=2),:].astype(BF)
        two=src[pl.ds(2*r+1,ch,stride=2),:].astype(BF)
        gj[pl.ds(r,ch),:128]=one
        gj[pl.ds(r,ch),128:]=two
        fold=lambda x: jnp.sum(x.astype(F32).reshape(ch//8,8,128),axis=0)
        return (sums[0]+fold(one),sums[1]+fold(two))
    zero=jnp.zeros((8,128),F32)
    one,two=lax.fori_loop(0,n//ch,out,(zero,zero))
    total[:,:128]=one
    total[:,128:]=two

def bwd(pos,left,right,landed):
    H,n=left.shape[:2]
    span=len(landed)
    rows=landed[0].shape[0]
    blk=lambda: pl.BlockSpec((1,n,128),lambda h: (h, 0, 0))
    return pl.pallas_call(functools.partial(bwd_kernel,span),grid=(H,),
      out_shape=(jax.ShapeDtypeStruct((n,H*256),BF),jax.ShapeDtypeStruct((8,H*256),F32)),
      in_specs=[pl.BlockSpec(memory_space=pltpu.SMEM),blk(),blk()]+[pl.BlockSpec((rows,128),lambda h: (0, 0))]*span,
      out_specs=(pl.BlockSpec((n,256),lambda h: (0, h)),pl.BlockSpec((8,256),lambda h: (0, h))),
      scratch_shapes=[pltpu.VMEM((2*n,128),F32),pltpu.VMEM((n,128),F32),pltpu.VMEM((2*n,128),F32)],
      compiler_params=pltpu.CompilerParams(vmem_limit_bytes=VMEM_ALL),name="att_bwd")(pos,left,right,*landed)

def mid_kernel(span, *refs):
    came = refs[:span]
    at, tok, up, wo, we, wc, vec, ebias = refs[span:span + 8]
    result, gfirst = refs[span + 8:span + 10]
    leave = refs[span + 10:2 * span + 10]
    merged_o, gbranch_o, nlow_o, gmid_o, lifted_o, ginner_o, sums, esum = refs[2 * span + 10:2 * span + 18]
    wop, slope = refs[2 * span + 18:]
    i = pl.program_id(0)
    rows, width = tok.shape
    half = rows * pl.num_programs(0) // 2
    strips = we.shape[0]
    own = width // span
    pair = 128
    single = own - pair

    @pl.when(i == 0)
    def _():
        for k in range(span):
            p = pl.multiple_of((at[0] ^ k) * own, 64)
            wop[k * pair:(k + 1) * pair, :] = wo[pl.ds(p, pair), :]
            wop[span * pair + k * single:span * pair + (k + 1) * single, :] = wo[pl.ds(p + pair, single), :]
        sums[...] = jnp.zeros_like(sums)
        esum[...] = jnp.zeros_like(esum)

    def total(at_row, value):
        sums[at_row:at_row + 1, :] += jnp.sum(value, axis=0, keepdims=True)

    low = i * rows < half
    start = pl.multiple_of(2 * half + lax.rem(i * rows, half), rows)
    pairs = [c[pl.ds(pl.multiple_of(i * rows, rows), rows), :] for c in came]
    both = [c[pl.ds(start, rows), :] for c in came]
    singles = [jnp.where(low, x[:, :single], x[:, single:]) for x in both]
    merged = jnp.concatenate(pairs + singles, axis=1)
    merged_o[...] = merged
    hidden = tok[...].astype(F32) + nn(merged, wop[...]) + vec[0:1, :]
    normed_one, unit_one, inverse_one = normalize(hidden, vec[1:2, :], vec[2:3, :])
    normed_low = normed_one.astype(BF)
    nlow_o[...] = normed_low
    second = normed_one + vec[3:4, :]
    for k in range(strips):
        cols = slice(k * width, (k + 1) * width)
        inner = nn(normed_low, we[k]) + ebias[k:k + 1, :]
        cdf = 0.5 * (1.0 + lax.erf(inner * root_half))
        lifted = (inner * cdf).astype(BF)
        slope[:, cols] = cdf + inner * jnp.exp(-0.5 * inner * inner) * density_norm
        lifted_o[:, cols] = lifted
        second += nn(lifted, wc[cols, :])
    out, unit_two, inverse_two = normalize(second, vec[4:5, :], vec[5:6, :])
    result[...] = out.astype(BF)
    cotangent = up[...].astype(F32)
    total(0, cotangent * unit_two)
    total(1, cotangent)
    grad_second = normalize_back(cotangent, vec[4:5, :], unit_two, inverse_two)
    grad_mid = grad_second.astype(BF)
    gmid_o[...] = grad_mid
    total(2, grad_mid.astype(F32))
    grad_normed = grad_second
    for k in range(strips):
        cols = slice(k * width, (k + 1) * width)
        grad_inner = (nt(grad_mid, wc[cols, :]) * slope[:, cols]).astype(BF)
        ginner_o[:, cols] = grad_inner
        esum[k:k + 1, :] += jnp.sum(grad_inner.astype(F32), axis=0, keepdims=True)
        grad_normed += nt(grad_inner, we[k])
    total(3, grad_normed * unit_one)
    total(4, grad_normed)
    grad_first = normalize_back(grad_normed, vec[1:2, :], unit_one, inverse_one)
    gfirst[...] = grad_first
    grad_branch = grad_first.astype(BF)
    gbranch_o[...] = grad_branch
    total(5, grad_branch.astype(F32))
    grad_merged = nt(grad_branch, wop[...]).astype(BF)
    for k in range(span):
        leave[k][pl.ds(pl.multiple_of(i * rows, rows), rows), :] = grad_merged[:, k * pair:(k + 1) * pair]
        one = grad_merged[:, span * pair + k * single:span * pair + (k + 1) * single]

        @pl.when(low)
        def _():
            leave[k][pl.ds(start, rows), :single] = one

        @pl.when(jnp.logical_not(low))
        def _():
            leave[k][pl.ds(start, rows), single:] = one


def mid(came, at, tok, up, wo, we, wc, vec, ebias, rows=256):
    span = len(came)
    count, width = tok.shape
    strips = we.shape[0]
    S = jax.ShapeDtypeStruct
    vm = pl.BlockSpec(memory_space=pltpu.VMEM)
    tile = lambda w: pl.BlockSpec((rows, w), lambda i: (i, 0))
    fixed = lambda shape: pl.BlockSpec(shape, lambda i: (0, 0))
    deep = strips * width
    outs = (
        [(S((count, width), BF), tile(width)), (S((count, width), F32), tile(width))]
        + [(S(came[0].shape, BF), fixed(came[0].shape))] * span
        + [(S((count, width), BF), tile(width))] * 4
        + [(S((count, deep), BF), tile(deep))] * 2
        + [(S((8, width), F32), fixed((8, width))), (S((strips, width), F32), fixed((strips, width)))]
    )
    return pl.pallas_call(
        functools.partial(mid_kernel, span),
        grid=(count // rows,),
        out_shape=[o for o, _ in outs],
        in_specs=[vm] * span + [pl.BlockSpec(memory_space=pltpu.SMEM), tile(width), tile(width)] + [vm] * 5,
        out_specs=[b for _, b in outs],
        scratch_shapes=[pltpu.VMEM((width, width), BF), pltpu.VMEM((rows, deep), F32)],
        compiler_params=pltpu.CompilerParams(vmem_limit_bytes=VMEM_ALL),
        name="mid",
    )(*came, at, tok, up, wo, we, wc, vec, ebias)

MESH = pl.DeviceIdType.MESH


def bits_of(size):
    return size.bit_length() - 1


def steps_of(nt, ng):
    return [("tok", b) for b in reversed(range(bits_of(nt)))] + [
        ("grp", b) for b in reversed(range(bits_of(ng)))
    ]


def greet(peers):
    barrier = pltpu.get_barrier_semaphore()
    for peer in peers:
        pl.semaphore_signal(barrier, inc=1, device_id=peer, device_id_type=MESH)
    pl.semaphore_wait(barrier, len(peers))


def collect_kernel(nt, ng, parts, *refs):
    tok_in, pos_in, pin_in = refs[:3]
    nf = (len(refs) - 13) // 2
    full_in = refs[3:3 + nf]
    tok_out, pos_out, pin_out = refs[3 + nf:6 + nf]
    full_out = refs[6 + nf:6 + 2 * nf]
    lsem, tsend, trecv, psend, precv, wsend, wrecv = refs[6 + 2 * nf:]
    t = lax.axis_index("tok")
    g = lax.axis_index("grp")
    steps = steps_of(nt, ng)
    nb = len(steps)
    me = t * ng + g
    digits = [(me // (1 << (nb - 1 - j))) % 2 for j in range(nb)]

    def held_at(s):
        return (slice(None),) * s + tuple(digits[s:])

    def peer(axis, mask):
        return {"tok": t ^ mask, "grp": g} if axis == "tok" else {"tok": t, "grp": g ^ mask}

    count = tok_in.shape[0]
    own = [pltpu.make_async_copy(tok_in, tok_out.at[0], lsem.at[0]),
           pltpu.make_async_copy(pos_in.at[t % 4], pos_out.at[0], lsem.at[1])]
    for i, (a, b) in enumerate(zip(full_in, full_out)):
        own.append(pltpu.make_async_copy(a, b.at[held_at(0)], lsem.at[2 + i]))
    greet([peer(axis, 1 << b) for axis, b in steps] + [peer("tok", 3)])
    for copy in own:
        copy.start()

    flights = {}

    def send(name, src, dst, sems, to):
        copy = pltpu.make_async_remote_copy(
            src_ref=src, dst_ref=dst, send_sem=sems[0], recv_sem=sems[1],
            device_id=to, device_id_type=MESH)
        copy.start()
        flights[name] = copy

    arrived = set()

    def wait(name):
        if name not in arrived:
            arrived.add(name)
            flights[name].wait_recv()

    chunk = count // parts

    def rows(c):
        return pl.ds(c * chunk, chunk)

    def token(c, mask):
        i = (mask - 1) * parts + c
        send(("t", mask, c), tok_in.at[rows(c)], tok_out.at[mask, rows(c)],
             (tsend.at[i], trecv.at[i]), peer("tok", mask))

    def relay(c):
        i = 2 * parts + c
        mask = 2 if c >= parts // 2 else 1
        wait(("t", 3 - mask, c))
        send(("r", c), tok_out.at[3 - mask, rows(c)], tok_out.at[3, rows(c)],
             (tsend.at[i], trecv.at[i]), peer("tok", mask))

    def position(mask):
        i = mask - 1
        send(("p", mask), pos_in.at[(t ^ mask) % 4], pos_out.at[mask],
             (psend.at[i], precv.at[i]), peer("tok", mask))

    def full(w, s):
        axis, b = steps[s]
        i = w * nb + s
        to = peer(axis, 1 << b)
        out = full_out[w]
        if s == 0:
            src, dst = full_in[w], out.at[held_at(0)]
        else:
            wait(("w", w, s - 1))
            if s == 1:
                own[2 + w].wait()
            src = out.at[held_at(s)]
            dst = src
        send(("w", w, s), src, dst, (wsend.at[i], wrecv.at[i]), to)

    def slices(s):
        axis, b = steps[s]
        i = nf * nb + s
        to = peer(axis, 1 << b)
        tb = bits_of(nt)
        if s > 0:
            wait(("w", nf, s - 1))
        high = tb - 2
        theirs = (t ^ (1 << b)) if axis == "tok" else t
        if s < high:
            place = (slice(None), slice(None))
        elif s == high:
            place = ((theirs // 2) % 2, slice(None))
        else:
            place = ((theirs // 2) % 2, theirs % 2)
        src = pin_out.at[place + held_at(s)]
        send(("w", nf, s), src, src, (wsend.at[i], wrecv.at[i]), to)

    pin_own = pltpu.make_async_copy(pin_in, pin_out.at[(slice(None), slice(None)) + held_at(0)], lsem.at[2 + nf])
    pin_own.start()
    order = list(range(nf))
    half = parts // 2
    for c in range(half):
        token(c, 1)
    for w in order:
        full(w, 0)
    pin_own.wait()
    slices(0)
    for mask in (1, 2, 3):
        position(mask)
    token(0, 2)
    done_y, done_z = half, 1
    for s in range(1, nb):
        for w in order:
            full(w, s)
            if w >= 0:
                if done_z < parts:
                    token(done_z, 2)
                    done_z += 1
                if done_y < parts and s >= 2:
                    token(done_y, 1)
                    done_y += 1
        slices(s)
        if s == nb - 2:
            for c in range(done_z, parts):
                token(c, 2)
            for c in range(done_y, parts):
                token(c, 1)
            for c in range(parts):
                relay(c)
    own[0].wait()
    own[1].wait()
    if nb == 1:
        for w in range(nf):
            own[2 + w].wait()
    for name in flights:
        wait(name)
    for copy in flights.values():
        copy.wait_send()


def collect(nt, ng, tokens, pos, pin, fulls, parts=4):
    n = nt * ng
    nb = bits_of(nt) + bits_of(ng)
    hbm = pl.BlockSpec(memory_space=pl.ANY)
    vm = pl.BlockSpec(memory_space=pltpu.VMEM)
    S = jax.ShapeDtypeStruct
    block, at, own, *wide = pl.pallas_call(
        functools.partial(collect_kernel, nt, ng, parts),
        out_shape=[S((4,) + tokens.shape, tokens.dtype), S((4,) + pos.shape[1:], pos.dtype),
                   S((2, 2) + (2,) * nb + pin.shape[1:], pin.dtype)] + [S((2,) * nb + f.shape, f.dtype) for f in fulls],
        in_specs=[vm] * (3 + len(fulls)),
        out_specs=[hbm] * (3 + len(fulls)),
        scratch_shapes=[
            pltpu.SemaphoreType.DMA((3 + len(fulls),)),
            pltpu.SemaphoreType.DMA((3 * parts,)), pltpu.SemaphoreType.DMA((3 * parts,)),
            pltpu.SemaphoreType.DMA((3,)), pltpu.SemaphoreType.DMA((3,)),
            pltpu.SemaphoreType.DMA(((len(fulls) + 1) * nb,)), pltpu.SemaphoreType.DMA(((len(fulls) + 1) * nb,)),
        ],
        compiler_params=pltpu.CompilerParams(collective_id=0, has_side_effects=True),
        name="collect",
    )(tokens, pos, pin.reshape((2, 2) + pin.shape[1:]), *fulls)
    return [block, at, own.reshape((4, n) + pin.shape[1:])] + [
        w.reshape((n,) + f.shape) for w, f in zip(wide, fulls)]


def reduce_kernel(nt, ng, chunks, *refs):
    pin_in, small_in, own_in, p1, p2, p3 = refs[:6]
    pin_out, small_out, token_out = refs[6:9]
    nb = bits_of(nt) + bits_of(ng)
    tb = bits_of(nt)
    pin_a, small_a, quad = refs[9:12]
    landing = refs[12:12 + 2 * nb]
    near_a, far_a, near_b, far_b, pass_a, pass_b, end_a, end_b = refs[12 + 2 * nb:20 + 2 * nb]
    ssem, rsem, tsend, trecv = refs[20 + 2 * nb:]
    t = lax.axis_index("tok")
    g = lax.axis_index("grp")
    steps = steps_of(nt, ng)
    me = t * ng + g
    digits = [(me // (1 << (nb - 1 - j))) % 2 for j in range(nb)]

    def peer(s):
        axis, b = steps[s]
        mask = 1 << b
        return {"tok": t ^ mask, "grp": g} if axis == "tok" else {"tok": t, "grp": g ^ mask}

    greet([peer(s) for s in range(nb)])
    place_1, place_0 = (t // 2) % 2, t % 2
    flying = []

    def launch(i, src, dst, s):
        copy = pltpu.make_async_remote_copy(
            src_ref=src, dst_ref=dst, send_sem=ssem.at[i], recv_sem=rsem.at[i],
            device_id=peer(s), device_id_type=MESH)
        copy.start()
        flying.append(copy)
        return copy

    count, width = own_in.shape
    half = width // 2
    left_cols, right_cols = pl.ds(0, half), pl.ds(half, half)
    step = count // chunks

    def rows(c):
        return pl.ds(c * step, step)

    token = {}

    def ship(name, c, src, dst, mask):
        i = len(token)
        copy = pltpu.make_async_remote_copy(
            src_ref=src, dst_ref=dst, send_sem=tsend.at[i], recv_sem=trecv.at[i],
            device_id={"tok": t ^ mask, "grp": g}, device_id_type=MESH)
        copy.start()
        token[name, c] = copy

    def first(c):
        ship("far_a", c, p3.at[rows(c), left_cols], far_a.at[rows(c)], 1)
        ship("far_b", c, p3.at[rows(c), right_cols], far_b.at[rows(c)], 2)

    def second(c):
        ship("near_a", c, p1.at[rows(c), left_cols], near_a.at[rows(c)], 1)
        ship("near_b", c, p2.at[rows(c), right_cols], near_b.at[rows(c)], 2)

    def relay(c):
        token["far_a", c].wait_recv()
        value = p2[rows(c), left_cols].astype(F32) + far_a[rows(c), :].astype(F32)
        pass_a[rows(c), :] = value.astype(BF)
        ship("end_a", c, pass_a.at[rows(c)], end_a.at[rows(c)], 2)
        token["far_b", c].wait_recv()
        value = p1[rows(c), right_cols].astype(F32) + far_b[rows(c), :].astype(F32)
        pass_b[rows(c), :] = value.astype(BF)
        ship("end_b", c, pass_b.at[rows(c)], end_b.at[rows(c)], 1)

    def finish(c):
        for near, end in (("near_a", "end_a"), ("near_b", "end_b")):
            token[near, c].wait_recv()
            token[end, c].wait_recv()
        token_out[rows(c), left_cols] = (
            own_in[rows(c), left_cols] + near_a[rows(c), :].astype(F32) + end_a[rows(c), :].astype(F32)
        )
        token_out[rows(c), right_cols] = (
            own_in[rows(c), right_cols] + near_b[rows(c), :].astype(F32) + end_b[rows(c), :].astype(F32)
        )

    def away(s):
        return (slice(None),) * s + (1 - digits[s],) + tuple(digits[s + 1:])

    def kept(s):
        return (slice(None),) * s + tuple(digits[s:])

    def add(ref, at, other, dst, to):
        value = ref[at].astype(F32) + other[...].astype(F32)
        dst[to] = value.astype(dst.dtype)

    low = chunks // 2
    for s in reversed(range(nb)):
        head = s == nb - 1
        outer = s >= tb
        sources = [pin_in if head else pin_a, small_in if head else small_a]
        copies = []
        for w in range(2):
            land = landing[w * nb + s]
            i = w * nb + s
            if w == 0 and not outer:
                place = {tb - 1: (place_1, place_0), tb - 2: (place_1, slice(None))}.get(
                    s, (slice(None), slice(None)))
                cut = (slice(None),) * s + (1 - digits[s],) + tuple(digits[s + 1:tb])
                src = quad.at[place + cut]
                copies.append(launch(i, src, src if s >= tb - 2 else land, s))
            else:
                copies.append(launch(i, sources[w].at[away(s)], land, s))
        turn = nb - 1 - s
        if turn == 0:
            for c in range(chunks):
                first(c)
        elif turn == 1:
            for c in range(low):
                relay(c)
                second(c)
        elif turn == 2:
            for c in range(low, chunks):
                relay(c)
        elif turn == 3:
            for c in range(low, chunks):
                second(c)
        for w in range(2):
            copies[w].wait_recv()
            land = landing[w * nb + s]
            if w == 0 and not outer:
                if s < tb - 2:
                    at = (slice(None), slice(None)) + (slice(None),) * s + tuple(digits[s:tb])
                    add(quad, at, land, quad, at)
            elif w == 0 and s == tb:
                add(sources[0], kept(s), land, quad, (place_1, place_0))
            else:
                dst = (pin_a, small_a)[w]
                add(sources[w], kept(s), land, dst, kept(s))
    pin_out[...] = quad[(slice(None), slice(None)) + tuple(digits[:tb])]
    small_out[...] = small_a[tuple(digits)]
    for c in range(chunks):
        finish(c)
    for copy in flying:
        copy.wait_send()
    for copy in token.values():
        copy.wait_send()


def reduce_small(nt, ng, pin, small, own, parts, chunks=4):
    nb = bits_of(nt) + bits_of(ng)
    tb = bits_of(nt)
    two = (2,) * nb
    r, c = pin.shape[1:]
    rs = small.shape[1:]
    count, width = own.shape
    S = jax.ShapeDtypeStruct
    vm = pl.BlockSpec(memory_space=pltpu.VMEM)
    landing = []
    for w, (shape, dt) in enumerate((((r, c), BF), (rs, F32))):
        for s in range(nb):
            lead = (2,) * s
            if w == 0 and s < tb:
                lead = ((2, 2) + lead) if s < tb - 2 else (1,)
                landing.append(pltpu.VMEM(lead + (shape if s < tb - 2 else (8, 128)), dt))
            else:
                landing.append(pltpu.VMEM(lead + shape, dt))
    return pl.pallas_call(
        functools.partial(reduce_kernel, nt, ng, chunks),
        out_shape=[S((2, 2, r, c), BF), S(rs, F32), S((count, width), F32)],
        in_specs=[vm] * 6,
        out_specs=[vm] * 3,
        scratch_shapes=[
            pltpu.VMEM(two + (r, c), BF), pltpu.VMEM(two + rs, F32),
            pltpu.VMEM((2, 2) + (2,) * tb + (r, c), BF),
        ] + landing + [pltpu.VMEM((count, width // 2), BF)] * 8 + [
            pltpu.SemaphoreType.DMA((2 * nb,)), pltpu.SemaphoreType.DMA((2 * nb,)),
            pltpu.SemaphoreType.DMA((6 * chunks,)), pltpu.SemaphoreType.DMA((6 * chunks,)),
        ],
        compiler_params=pltpu.CompilerParams(collective_id=1, has_side_effects=True, vmem_limit_bytes=VMEM_ALL),
        name="reduce_small",
    )(pin.reshape(two + (r, c)), small.reshape(two + rs), own, *parts)


def flip(block, mask):
    count = lax.axis_size("tok")
    return lax.ppermute(block, "tok", [(i, i ^ mask) for i in range(count)])


def gather_all(item):
    return lax.all_gather(item, ("tok", "grp"), axis=0, tiled=True)


def scatter_sum(item):
    return lax.psum_scatter(item, ("tok", "grp"), scatter_dimension=0, tiled=True)


def shards(
    tokens,
    upstream,
    cluster_pos,
    project_in,
    query_bias,
    value_bias,
    project_out,
    output_bias,
    first_gain,
    first_shift,
    expand,
    expand_bias,
    contract,
    contract_bias,
    second_gain,
    second_shift,
):
    inputs = tokens[0]
    count, width = inputs.shape
    positions = cluster_pos[0] % LONG
    heads = positions.shape[0]
    head_dim = width // heads
    span = LONG // count
    mine = heads // span
    offset = lax.axis_index("tok") % span
    total = span * count

    nt = lax.axis_size("tok")
    ng = lax.axis_size("grp")
    devices = nt * ng
    few = query_bias.shape[0]
    strips = expand.shape[1] // width

    pieces = project_in.reshape(few, 3, span, mine, head_dim)
    hollow = jnp.zeros((few, head_dim), BF)
    arranged = []
    for place in range(span):
        columns = []
        for h in range(mine):
            query, key, value = (pieces[:, i, place, h] for i in range(3))
            columns += [hollow, query, value, key] if h == 0 else [query, hollow, key, value]
        arranged.append(jnp.concatenate(columns, axis=1))
    packed = jnp.concatenate(
        [
            query_bias, value_bias, output_bias, first_gain, first_shift,
            contract_bias, second_gain, second_shift, expand_bias,
        ]
    ).astype(F32)
    packed = jnp.pad(packed, (0, 1024 - packed.shape[0])).reshape(8, 128)
    block, own_at, arranged, packed = collect(
        nt, ng, inputs, positions.reshape(span, mine, count), jnp.stack(arranged), [packed]
    )
    wide = jnp.concatenate(
        [project_out, expand.reshape(few, strips, width).transpose(1, 0, 2).reshape(-1, width), contract],
        axis=0,
    )
    wide, packed = lax.optimization_barrier((wide, packed))
    wide = gather_all(wide[None])
    project_out = wide[:, :few]
    expand = wide[:, few : (1 + strips) * few].reshape(devices, strips, few, width)
    expand = expand.transpose(1, 0, 2, 3).reshape(strips, width, width)
    contract = wide[:, (1 + strips) * few :].reshape(strips * width, width)
    block = block.reshape(total, width)
    own_at = own_at.transpose(1, 0, 2).reshape(-1)
    arranged = lax.dynamic_index_in_dim(arranged, offset, 0, False).reshape(width, -1)
    packed = packed.reshape(devices, -1)
    vectors = packed[:, : 8 * few].reshape(devices, 8, few).transpose(1, 0, 2).reshape(8, width)
    expand_bias = packed[:, 8 * few : (8 + strips) * few].reshape(strips, width)
    query_bias, value_bias = vectors[0], vectors[1]
    vectors = jnp.concatenate([vectors[2:], vectors[:2]], axis=0)

    own_query = lax.dynamic_slice_in_dim(query_bias.reshape(heads, head_dim), offset * mine, mine)
    own_value = lax.dynamic_slice_in_dim(value_bias.reshape(heads, head_dim), offset * mine, mine)
    blank = jnp.zeros((head_dim,), F32)
    rows = []
    for h in range(mine):
        parts = [blank, own_query[h], own_value[h], blank] if h == 0 else [own_query[h], blank, blank, own_value[h]]
        rows.append(jnp.concatenate(parts))
    bias_rows = jnp.stack(rows)[:, None]

    *leaving, left, right = fwd(own_at, block, arranged, bias_rows, span)
    came = [leaving[0]] + [flip(leaving[k], k) for k in range(1, span)]
    project_out = project_out.reshape(width, width)
    result, grad_first, *rest = mid(
        came, offset[None].astype(jnp.int32), inputs, upstream[0], project_out, expand, contract,
        vectors, expand_bias,
    )
    sending = rest[:span]
    merged, grad_branch, normed_low, grad_mid, lifted, grad_inner, row_sums, expand_sums = rest[span:]
    landed = [sending[0]] + [flip(sending[k], k) for k in range(1, span)]

    def turn(item):
        item = item.reshape(2, 2, mine * head_dim, width)
        item = jnp.where(offset % 2 == 1, item[:, ::-1], item)
        return jnp.where(offset // 2 == 1, item[::-1], item).reshape(width, width)

    landed, lifted = lax.optimization_barrier((landed, lifted))
    contract_grad = jnp.einsum("rf,rd->fd", lifted, grad_mid, preferred_element_type=F32)
    expand_grad = jnp.einsum("rd,rf->df", normed_low, grad_inner, preferred_element_type=F32)
    turned_grad = jnp.einsum("rd,re->de", merged, grad_branch, preferred_element_type=F32).astype(BF)
    split = span * 2 * head_dim
    project_out_grad = turn(
        jnp.concatenate(
            [
                turned_grad[:split].reshape(span, 2 * head_dim, width),
                turned_grad[split:].reshape(span, head_dim, width),
            ],
            axis=1,
        )
    )
    expand_grad = expand_grad.astype(BF)
    contract_grad = contract_grad.astype(BF)
    wide_grad = jnp.concatenate(
        [project_out_grad.reshape(devices, few, width)]
        + [expand_grad[:, i * width : (i + 1) * width].reshape(devices, few, width) for i in range(strips)]
        + [contract_grad.reshape(devices, strips * few, width)],
        axis=1,
    )
    landed, held = lax.optimization_barrier((landed, wide_grad))
    wide_grad = scatter_sum(wide_grad)[0].astype(F32)
    project_out_grad = wide_grad[:few]
    expand_grad = wide_grad[few : (1 + strips) * few].reshape(strips, few, width).transpose(1, 0, 2).reshape(few, -1)
    contract_grad = wide_grad[(1 + strips) * few :]
    grad_rows, grad_sums = bwd(own_at, left, right, landed)
    partial = [
        jnp.einsum(
            "re,de->rd", grad_rows[k * count : (k + 1) * count], arranged, preferred_element_type=F32
        )
        for k in range(span)
    ]
    parts = [partial[k].astype(BF) for k in range(1, span)]
    arranged_grad = jnp.einsum("rd,re->de", block, grad_rows, preferred_element_type=F32).astype(BF)
    sums = jnp.sum(grad_sums, axis=0).reshape(mine, 4, head_dim)
    query_at = [1] + [0] * (mine - 1)
    key_at = [3] + [2] * (mine - 1)
    value_at = [2] + [3] * (mine - 1)

    def spread(take, at):
        return jnp.stack([take(h, at[h]) for h in range(mine)], axis=-2)

    own_sums = jnp.stack([spread(lambda h, s: sums[h, s], at) for at in (query_at, value_at)])
    bias_grads = lax.dynamic_update_slice_in_dim(
        jnp.zeros((2, heads, head_dim), F32), own_sums, offset * mine, axis=1
    ).reshape(2, width)
    ordered = jnp.concatenate([bias_grads, row_sums[5:6], row_sums[3:5], row_sums[2:3], row_sums[:2]], axis=0)
    small = jnp.concatenate(
        [
            ordered.reshape(8, devices, few).transpose(1, 0, 2).reshape(devices, 8 * few),
            expand_sums.reshape(devices, strips * few),
        ],
        axis=1,
    )
    small = jnp.pad(small, ((0, 0), (0, 1024 - small.shape[1]))).reshape(devices, 8, 128)
    project_in_grad, small, token_grad = reduce_small(
        nt, ng, arranged_grad.reshape(devices, few, -1), small, grad_first + partial[0], parts
    )
    project_in_grad = project_in_grad.astype(F32).reshape(span, few, mine, 4, head_dim)
    project_in_grad = jnp.concatenate(
        [
            project_in_grad[place, :, h, at[h]]
            for at in (query_at, key_at, value_at)
            for place in range(span)
            for h in range(mine)
        ],
        axis=1,
    )
    small = small.reshape(-1)
    each = [small[i * few : (i + 1) * few] for i in range(8)] + [small[8 * few : (8 + strips) * few]]
    return (
        result[None],
        token_grad[None],
        project_in_grad,
        each[0],
        each[1],
        project_out_grad,
        each[2],
        each[3],
        each[4],
        expand_grad,
        each[8],
        contract_grad,
        each[5],
        each[6],
        each[7],
    )


def solution(mesh):
    placed = (
        P("grp", "tok", None),
        P("grp", "tok", None),
        P("grp", None, "tok"),
        P(("tok", "grp"), None),
        P(("tok", "grp")),
        P(("tok", "grp")),
        P(("tok", "grp"), None),
        P(("tok", "grp")),
        P(("tok", "grp")),
        P(("tok", "grp")),
        P(("tok", "grp"), None),
        P(("tok", "grp")),
        P(("tok", "grp"), None),
        P(("tok", "grp")),
        P(("tok", "grp")),
        P(("tok", "grp")),
    )
    return jax.shard_map(
        shards,
        mesh=mesh,
        in_specs=placed,
        out_specs=(
            P("grp", "tok", None),
            P("grp", "tok", None),
            P(("tok", "grp"), None),
            P(("tok", "grp")),
            P(("tok", "grp")),
            P(("tok", "grp"), None),
            P(("tok", "grp")),
            P(("tok", "grp")),
            P(("tok", "grp")),
            P(("tok", "grp"), None),
            P(("tok", "grp")),
            P(("tok", "grp"), None),
            P(("tok", "grp")),
            P(("tok", "grp")),
            P(("tok", "grp")),
        ),
        check_vma=False,
    )
```

```python
import functools
import jax
import jax.numpy as jnp
from jax import lax
from jax.experimental import pallas as pl
from jax.experimental.pallas import tpu as pltpu
from jax.sharding import PartitionSpec as P

CL = 128
LONG = 4096
F32 = jnp.float32
BF = jnp.bfloat16
VMEM_ALL = 64 * 1024 * 1024 - 65536

epsilon = 1e-05
root_half = 0.7071067811865476
density_norm = 0.3989422804014327

def normalize(hidden, gain, shift):
    centred = hidden - jnp.mean(hidden, axis=1, keepdims=True)
    inverse_std = lax.rsqrt(jnp.mean(centred * centred, axis=1, keepdims=True) + epsilon)
    unit = centred * inverse_std
    return (unit * gain + shift, unit, inverse_std)


def normalize_back(grad_out, gain, unit, inverse_std):
    scaled = grad_out * gain
    return inverse_std * (
        scaled
        - jnp.mean(scaled, axis=1, keepdims=True)
        - unit * jnp.mean(scaled * unit, axis=1, keepdims=True)
    )


def nt(a,b): return lax.dot_general(a,b,(((1,),(1,)),((),())),preferred_element_type=F32)
def nn(a,b): return lax.dot_general(a,b,(((1,),(0,)),((),())),preferred_element_type=F32)
def tn(a,b): return lax.dot_general(a,b,(((0,),(0,)),((),())),preferred_element_type=F32)

def fwd_kernel(span, pos, tok, w, bias, *refs):
    leave = refs[:span]
    left, right, src, ord_, oc = refs[span:]
    h=pl.program_id(0)
    n=tok.shape[0]
    ch=512
    def proj(i,_):
        r=pl.multiple_of(i*ch,ch)
        acc=nn(tok[pl.ds(r,ch),:],w[...])+bias[0]
        src[pl.ds(2*r,ch,stride=2),:]=acc[:,:128]
        src[pl.ds(2*r+1,ch,stride=2),:]=acc[:,128:]
        return 0
    lax.fori_loop(0,n//ch,proj,0)
    U=64
    def scat(i,_):
        for u in range(U):
            t=i*U+u
            ord_[pl.ds(2*pos[h*n+t],2),:]=src[pl.ds(2*t,2),:]
        return 0
    lax.fori_loop(0,n//U,scat,0)
    CB=16
    def clus(i,_):
        at=[pl.multiple_of((i*CB+u)*CL,CL) for u in range(CB)]
        ls=[ord_[pl.ds(2*r,CL,stride=2),:].astype(BF) for r in at]
        rs=[ord_[pl.ds(2*r+1,CL,stride=2),:].astype(BF) for r in at]
        ss=[nt(rr,l) for rr,l in zip(rs,ls)]
        for r,l,rr in zip(at,ls,rs):
            left[0,pl.ds(r,CL),:]=l
            right[0,pl.ds(r,CL),:]=rr
        es=[jnp.exp((x-jnp.max(x,axis=0,keepdims=True))*0.125) for x in ss]
        ps=[(e*(1.0/jnp.sum(e,axis=0,keepdims=True))).astype(BF) for e in es]
        for r,p,rr in zip(at,ps,rs):
            oc[pl.ds(r,CL),:]=tn(p,rr)
        return 0
    lax.fori_loop(0,n//CL//CB,clus,0)
    def gath(i,_):
        for u in range(U):
            t=i*U+u
            src[pl.ds(t,1),:]=oc[pl.ds(pos[h*n+t],1),:]
        return 0
    lax.fori_loop(0,n//U,gath,0)
    count=n//span
    @pl.when(h==0)
    def _():
        for k in range(span):
            leave[k][:count,:64]=src[k*count:(k+1)*count,:64].astype(BF)
    @pl.when(h==1)
    def _():
        for k in range(span):
            leave[k][:count,64:]=src[k*count:(k+1)*count,64:].astype(BF)
    @pl.when(h==2)
    def _():
        for k in range(span):
            mid_row=k*count+count//2
            leave[k][count:,:64]=src[k*count:mid_row,64:].astype(BF)
            leave[k][count:,64:]=src[mid_row:(k+1)*count,64:].astype(BF)

def fwd(pos,tok,w,bias,span):
    rows=tok.shape[0]//span*3//2
    n=tok.shape[0]; H=pos.shape[0]//n
    return pl.pallas_call(functools.partial(fwd_kernel,span),grid=(H,),
      out_shape=(jax.ShapeDtypeStruct((rows,128),BF),)*span+(jax.ShapeDtypeStruct((H,n,128),BF),)*2,
      in_specs=[pl.BlockSpec(memory_space=pltpu.SMEM),
                pl.BlockSpec((n,tok.shape[1]),lambda h:(0,0)),
                pl.BlockSpec((tok.shape[1],256),lambda h:(0,h)),
                pl.BlockSpec((1,1,256),lambda h: (h, 0, 0))],
      out_specs=(pl.BlockSpec((rows,128),lambda h: (0, 0)),)*span+(pl.BlockSpec((1,n,128),lambda h: (h, 0, 0)),)*2,
      scratch_shapes=[pltpu.VMEM((2*n,128),F32),pltpu.VMEM((2*n,128),F32),pltpu.VMEM((n,128),F32)],
      compiler_params=pltpu.CompilerParams(vmem_limit_bytes=VMEM_ALL),name="att_fwd")(pos,tok,w,bias)

def bwd_kernel(span, pos, left, right, *refs):
    landed = refs[:span]
    gj, total, src, ord_, dc = refs[span:]
    h=pl.program_id(0)
    n=left.shape[1]
    U=64
    count=n//span
    @pl.when(h<2)
    def _():
        for k in range(span):
            src[k*count:(k+1)*count,:]=landed[k][:count,:].astype(F32)
    @pl.when(h==2)
    def _():
        for k in range(span):
            x=landed[k][count:,:].astype(F32)
            mid_row=k*count+count//2
            src[k*count:mid_row,:]=jnp.concatenate([x[:,64:],x[:,:64]],axis=1)
            src[mid_row:(k+1)*count,:]=x
    def scat(i,_):
        for u in range(U):
            t=i*U+u
            ord_[pl.ds(pos[h*n+t],1),:]=src[pl.ds(t,1),:]
        return 0
    lax.fori_loop(0,n//U,scat,0)
    lane=lax.broadcasted_iota(jnp.int32,(CL,128),1)
    mask=(lane<64)==(h==0)
    CB=16
    def clus(i,_):
        at=[pl.multiple_of((i*CB+u)*CL,CL) for u in range(CB)]
        ls=[left[0,pl.ds(r,CL),:] for r in at]
        rs=[right[0,pl.ds(r,CL),:] for r in at]
        gs=[jnp.where(mask,ord_[pl.ds(r,CL),:],0.0).astype(BF) for r in at]
        ss=[nt(rr,l) for rr,l in zip(rs,ls)]
        dps=[nt(rr,d) for rr,d in zip(rs,gs)]
        es=[jnp.exp((x-jnp.max(x,axis=0,keepdims=True))*0.125) for x in ss]
        ps=[e*(1.0/jnp.sum(e,axis=0,keepdims=True)) for e in es]
        dss=[(p*(dp-jnp.sum(dp*p,axis=0,keepdims=True))).astype(BF) for p,dp in zip(ps,dps)]
        for r,ds,p,l,rr,d in zip(at,dss,ps,ls,rs,gs):
            dc[pl.ds(2*r,CL,stride=2),:]=tn(ds,rr)*0.125
            dc[pl.ds(2*r+1,CL,stride=2),:]=nn(ds,l)*0.125+nn(p.astype(BF),d)
        return 0
    lax.fori_loop(0,n//CL//CB,clus,0)
    def gath(i,_):
        for u in range(U):
            t=i*U+u
            src[pl.ds(2*t,2),:]=dc[pl.ds(2*pos[h*n+t],2),:]
        return 0
    lax.fori_loop(0,n//U,gath,0)
    ch=512
    def out(i,sums):
        r=pl.multiple_of(i*ch,ch)
        one=src[pl.ds(2*r,ch,stride=2),:].astype(BF)
        two=src[pl.ds(2*r+1,ch,stride=2),:].astype(BF)
        gj[pl.ds(r,ch),:128]=one
        gj[pl.ds(r,ch),128:]=two
        fold=lambda x: jnp.sum(x.astype(F32).reshape(ch//8,8,128),axis=0)
        return (sums[0]+fold(one),sums[1]+fold(two))
    zero=jnp.zeros((8,128),F32)
    one,two=lax.fori_loop(0,n//ch,out,(zero,zero))
    total[:,:128]=one
    total[:,128:]=two

def bwd(pos,left,right,landed):
    H,n=left.shape[:2]
    span=len(landed)
    rows=landed[0].shape[0]
    blk=lambda: pl.BlockSpec((1,n,128),lambda h: (h, 0, 0))
    return pl.pallas_call(functools.partial(bwd_kernel,span),grid=(H,),
      out_shape=(jax.ShapeDtypeStruct((n,H*256),BF),jax.ShapeDtypeStruct((8,H*256),F32)),
      in_specs=[pl.BlockSpec(memory_space=pltpu.SMEM),blk(),blk()]+[pl.BlockSpec((rows,128),lambda h: (0, 0))]*span,
      out_specs=(pl.BlockSpec((n,256),lambda h: (0, h)),pl.BlockSpec((8,256),lambda h: (0, h))),
      scratch_shapes=[pltpu.VMEM((2*n,128),F32),pltpu.VMEM((n,128),F32),pltpu.VMEM((2*n,128),F32)],
      compiler_params=pltpu.CompilerParams(vmem_limit_bytes=VMEM_ALL),name="att_bwd")(pos,left,right,*landed)

def mid_kernel(span, *refs):
    came = refs[:span]
    at, tok, up, wo, we, wc, vec, ebias = refs[span:span + 8]
    result, gfirst = refs[span + 8:span + 10]
    leave = refs[span + 10:2 * span + 10]
    merged_o, gbranch_o, nlow_o, gmid_o, lifted_o, ginner_o, sums, esum = refs[2 * span + 10:2 * span + 18]
    wop, slope = refs[2 * span + 18:]
    i = pl.program_id(0)
    rows, width = tok.shape
    half = rows * pl.num_programs(0) // 2
    strips = we.shape[0]
    own = width // span
    pair = 128
    single = own - pair

    @pl.when(i == 0)
    def _():
        for k in range(span):
            p = pl.multiple_of((at[0] ^ k) * own, 64)
            wop[k * pair:(k + 1) * pair, :] = wo[pl.ds(p, pair), :]
            wop[span * pair + k * single:span * pair + (k + 1) * single, :] = wo[pl.ds(p + pair, single), :]
        sums[...] = jnp.zeros_like(sums)
        esum[...] = jnp.zeros_like(esum)

    def total(at_row, value):
        sums[at_row:at_row + 1, :] += jnp.sum(value, axis=0, keepdims=True)

    low = i * rows < half
    start = pl.multiple_of(2 * half + lax.rem(i * rows, half), rows)
    pairs = [c[pl.ds(pl.multiple_of(i * rows, rows), rows), :] for c in came]
    both = [c[pl.ds(start, rows), :] for c in came]
    singles = [jnp.where(low, x[:, :single], x[:, single:]) for x in both]
    merged = jnp.concatenate(pairs + singles, axis=1)
    merged_o[...] = merged
    hidden = tok[...].astype(F32) + nn(merged, wop[...]) + vec[0:1, :]
    normed_one, unit_one, inverse_one = normalize(hidden, vec[1:2, :], vec[2:3, :])
    normed_low = normed_one.astype(BF)
    nlow_o[...] = normed_low
    second = normed_one + vec[3:4, :]
    for k in range(strips):
        cols = slice(k * width, (k + 1) * width)
        inner = nn(normed_low, we[k]) + ebias[k:k + 1, :]
        cdf = 0.5 * (1.0 + lax.erf(inner * root_half))
        lifted = (inner * cdf).astype(BF)
        slope[:, cols] = cdf + inner * jnp.exp(-0.5 * inner * inner) * density_norm
        lifted_o[:, cols] = lifted
        second += nn(lifted, wc[cols, :])
    out, unit_two, inverse_two = normalize(second, vec[4:5, :], vec[5:6, :])
    result[...] = out.astype(BF)
    cotangent = up[...].astype(F32)
    total(0, cotangent * unit_two)
    total(1, cotangent)
    grad_second = normalize_back(cotangent, vec[4:5, :], unit_two, inverse_two)
    grad_mid = grad_second.astype(BF)
    gmid_o[...] = grad_mid
    total(2, grad_mid.astype(F32))
    grad_normed = grad_second
    for k in range(strips):
        cols = slice(k * width, (k + 1) * width)
        grad_inner = (nt(grad_mid, wc[cols, :]) * slope[:, cols]).astype(BF)
        ginner_o[:, cols] = grad_inner
        esum[k:k + 1, :] += jnp.sum(grad_inner.astype(F32), axis=0, keepdims=True)
        grad_normed += nt(grad_inner, we[k])
    total(3, grad_normed * unit_one)
    total(4, grad_normed)
    grad_first = normalize_back(grad_normed, vec[1:2, :], unit_one, inverse_one)
    gfirst[...] = grad_first
    grad_branch = grad_first.astype(BF)
    gbranch_o[...] = grad_branch
    total(5, grad_branch.astype(F32))
    grad_merged = nt(grad_branch, wop[...]).astype(BF)
    for k in range(span):
        leave[k][pl.ds(pl.multiple_of(i * rows, rows), rows), :] = grad_merged[:, k * pair:(k + 1) * pair]
        one = grad_merged[:, span * pair + k * single:span * pair + (k + 1) * single]

        @pl.when(low)
        def _():
            leave[k][pl.ds(start, rows), :single] = one

        @pl.when(jnp.logical_not(low))
        def _():
            leave[k][pl.ds(start, rows), single:] = one


def mid(came, at, tok, up, wo, we, wc, vec, ebias, rows=256):
    span = len(came)
    count, width = tok.shape
    strips = we.shape[0]
    S = jax.ShapeDtypeStruct
    vm = pl.BlockSpec(memory_space=pltpu.VMEM)
    tile = lambda w: pl.BlockSpec((rows, w), lambda i: (i, 0))
    fixed = lambda shape: pl.BlockSpec(shape, lambda i: (0, 0))
    deep = strips * width
    outs = (
        [(S((count, width), BF), tile(width)), (S((count, width), F32), tile(width))]
        + [(S(came[0].shape, BF), fixed(came[0].shape))] * span
        + [(S((count, width), BF), tile(width))] * 4
        + [(S((count, deep), BF), tile(deep))] * 2
        + [(S((8, width), F32), fixed((8, width))), (S((strips, width), F32), fixed((strips, width)))]
    )
    return pl.pallas_call(
        functools.partial(mid_kernel, span),
        grid=(count // rows,),
        out_shape=[o for o, _ in outs],
        in_specs=[vm] * span + [pl.BlockSpec(memory_space=pltpu.SMEM), tile(width), tile(width)] + [vm] * 5,
        out_specs=[b for _, b in outs],
        scratch_shapes=[pltpu.VMEM((width, width), BF), pltpu.VMEM((rows, deep), F32)],
        compiler_params=pltpu.CompilerParams(vmem_limit_bytes=VMEM_ALL),
        name="mid",
    )(*came, at, tok, up, wo, we, wc, vec, ebias)

MESH = pl.DeviceIdType.MESH


def bits_of(size):
    return size.bit_length() - 1


def steps_of(nt, ng):
    return [("tok", b) for b in reversed(range(bits_of(nt)))] + [
        ("grp", b) for b in reversed(range(bits_of(ng)))
    ]


def greet(peers):
    barrier = pltpu.get_barrier_semaphore()
    for peer in peers:
        pl.semaphore_signal(barrier, inc=1, device_id=peer, device_id_type=MESH)
    pl.semaphore_wait(barrier, len(peers))


def collect_kernel(nt, ng, parts, *refs):
    tok_in, pos_in, pin_in = refs[:3]
    nf = (len(refs) - 13) // 2
    full_in = refs[3:3 + nf]
    tok_out, pos_out, pin_out = refs[3 + nf:6 + nf]
    full_out = refs[6 + nf:6 + 2 * nf]
    lsem, tsend, trecv, psend, precv, wsend, wrecv = refs[6 + 2 * nf:]
    t = lax.axis_index("tok")
    g = lax.axis_index("grp")
    steps = steps_of(nt, ng)
    nb = len(steps)
    me = t * ng + g
    digits = [(me // (1 << (nb - 1 - j))) % 2 for j in range(nb)]

    def held_at(s):
        return (slice(None),) * s + tuple(digits[s:])

    def peer(axis, mask):
        return {"tok": t ^ mask, "grp": g} if axis == "tok" else {"tok": t, "grp": g ^ mask}

    count = tok_in.shape[0]
    own = [pltpu.make_async_copy(tok_in, tok_out.at[0], lsem.at[0]),
           pltpu.make_async_copy(pos_in.at[t % 4], pos_out.at[0], lsem.at[1])]
    for i, (a, b) in enumerate(zip(full_in, full_out)):
        own.append(pltpu.make_async_copy(a, b.at[held_at(0)], lsem.at[2 + i]))
    greet([peer(axis, 1 << b) for axis, b in steps] + [peer("tok", 3)])
    for copy in own:
        copy.start()

    flights = {}

    def send(name, src, dst, sems, to):
        copy = pltpu.make_async_remote_copy(
            src_ref=src, dst_ref=dst, send_sem=sems[0], recv_sem=sems[1],
            device_id=to, device_id_type=MESH)
        copy.start()
        flights[name] = copy

    arrived = set()

    def wait(name):
        if name not in arrived:
            arrived.add(name)
            flights[name].wait_recv()

    chunk = count // parts

    def rows(c):
        return pl.ds(c * chunk, chunk)

    def token(c, mask):
        i = (mask - 1) * parts + c
        send(("t", mask, c), tok_in.at[rows(c)], tok_out.at[mask, rows(c)],
             (tsend.at[i], trecv.at[i]), peer("tok", mask))

    def relay(c):
        i = 2 * parts + c
        mask = 2 if c >= parts // 2 else 1
        wait(("t", 3 - mask, c))
        send(("r", c), tok_out.at[3 - mask, rows(c)], tok_out.at[3, rows(c)],
             (tsend.at[i], trecv.at[i]), peer("tok", mask))

    def position(mask):
        i = mask - 1
        send(("p", mask), pos_in.at[(t ^ mask) % 4], pos_out.at[mask],
             (psend.at[i], precv.at[i]), peer("tok", mask))

    def full(w, s):
        axis, b = steps[s]
        i = w * nb + s
        to = peer(axis, 1 << b)
        out = full_out[w]
        if s == 0:
            src, dst = full_in[w], out.at[held_at(0)]
        else:
            wait(("w", w, s - 1))
            if s == 1:
                own[2 + w].wait()
            src = out.at[held_at(s)]
            dst = src
        send(("w", w, s), src, dst, (wsend.at[i], wrecv.at[i]), to)

    def slices(s):
        axis, b = steps[s]
        i = nf * nb + s
        to = peer(axis, 1 << b)
        tb = bits_of(nt)
        if s > 0:
            wait(("w", nf, s - 1))
        high = tb - 2
        theirs = (t ^ (1 << b)) if axis == "tok" else t
        if s < high:
            place = (slice(None), slice(None))
        elif s == high:
            place = ((theirs // 2) % 2, slice(None))
        else:
            place = ((theirs // 2) % 2, theirs % 2)
        src = pin_out.at[place + held_at(s)]
        send(("w", nf, s), src, src, (wsend.at[i], wrecv.at[i]), to)

    pin_own = pltpu.make_async_copy(pin_in, pin_out.at[(slice(None), slice(None)) + held_at(0)], lsem.at[2 + nf])
    pin_own.start()
    order = list(range(nf))
    half = parts // 2
    for c in range(half):
        token(c, 1)
    for w in order:
        full(w, 0)
    pin_own.wait()
    slices(0)
    for mask in (1, 2, 3):
        position(mask)
    token(0, 2)
    done_y, done_z = half, 1
    for s in range(1, nb):
        for w in order:
            full(w, s)
            if w >= 0:
                if done_z < parts:
                    token(done_z, 2)
                    done_z += 1
                if done_y < parts and s >= 2:
                    token(done_y, 1)
                    done_y += 1
        slices(s)
        if s == nb - 2:
            for c in range(done_z, parts):
                token(c, 2)
            for c in range(done_y, parts):
                token(c, 1)
            for c in range(parts):
                relay(c)
    own[0].wait()
    own[1].wait()
    if nb == 1:
        for w in range(nf):
            own[2 + w].wait()
    for name in flights:
        wait(name)
    for copy in flights.values():
        copy.wait_send()


def collect(nt, ng, tokens, pos, pin, fulls, parts=4):
    n = nt * ng
    nb = bits_of(nt) + bits_of(ng)
    hbm = pl.BlockSpec(memory_space=pl.ANY)
    vm = pl.BlockSpec(memory_space=pltpu.VMEM)
    S = jax.ShapeDtypeStruct
    block, at, own, *wide = pl.pallas_call(
        functools.partial(collect_kernel, nt, ng, parts),
        out_shape=[S((4,) + tokens.shape, tokens.dtype), S((4,) + pos.shape[1:], pos.dtype),
                   S((2, 2) + (2,) * nb + pin.shape[1:], pin.dtype)] + [S((2,) * nb + f.shape, f.dtype) for f in fulls],
        in_specs=[vm] * (3 + len(fulls)),
        out_specs=[hbm] * (3 + len(fulls)),
        scratch_shapes=[
            pltpu.SemaphoreType.DMA((3 + len(fulls),)),
            pltpu.SemaphoreType.DMA((3 * parts,)), pltpu.SemaphoreType.DMA((3 * parts,)),
            pltpu.SemaphoreType.DMA((3,)), pltpu.SemaphoreType.DMA((3,)),
            pltpu.SemaphoreType.DMA(((len(fulls) + 1) * nb,)), pltpu.SemaphoreType.DMA(((len(fulls) + 1) * nb,)),
        ],
        compiler_params=pltpu.CompilerParams(collective_id=0, has_side_effects=True),
        name="collect",
    )(tokens, pos, pin.reshape((2, 2) + pin.shape[1:]), *fulls)
    return [block, at, own.reshape((4, n) + pin.shape[1:])] + [
        w.reshape((n,) + f.shape) for w, f in zip(wide, fulls)]


nt_dot = nt


def reduce_kernel(nt, ng, chunks, *refs):
    pin_in, small_in, own_in, grads, spread = refs[:5]
    pin_out, small_out, token_out = refs[5:8]
    nb = bits_of(nt) + bits_of(ng)
    tb = bits_of(nt)
    pin_a, small_a, quad = refs[8:11]
    landing = refs[11:11 + 2 * nb]
    near_a, far_a, near_b, far_b, pass_a, pass_b, end_a, end_b = refs[11 + 2 * nb:19 + 2 * nb]
    p1, p2, p3 = refs[19 + 2 * nb:22 + 2 * nb]
    ssem, rsem, tsend, trecv = refs[22 + 2 * nb:]
    t = lax.axis_index("tok")
    g = lax.axis_index("grp")
    steps = steps_of(nt, ng)
    me = t * ng + g
    digits = [(me // (1 << (nb - 1 - j))) % 2 for j in range(nb)]

    def peer(s):
        axis, b = steps[s]
        mask = 1 << b
        return {"tok": t ^ mask, "grp": g} if axis == "tok" else {"tok": t, "grp": g ^ mask}

    greet([peer(s) for s in range(nb)])
    place_1, place_0 = (t // 2) % 2, t % 2
    flying = []

    def launch(i, src, dst, s):
        copy = pltpu.make_async_remote_copy(
            src_ref=src, dst_ref=dst, send_sem=ssem.at[i], recv_sem=rsem.at[i],
            device_id=peer(s), device_id_type=MESH)
        copy.start()
        flying.append(copy)
        return copy

    count, width = own_in.shape
    half = width // 2
    left_cols, right_cols = pl.ds(0, half), pl.ds(half, half)
    step = count // chunks

    def rows(c):
        return pl.ds(c * step, step)

    token = {}

    def part(k, c):
        return nt_dot(grads[pl.ds(k * count + c * step, step), :], spread[...])

    def ship(name, c, src, dst, mask):
        i = len(token)
        copy = pltpu.make_async_remote_copy(
            src_ref=src, dst_ref=dst, send_sem=tsend.at[i], recv_sem=trecv.at[i],
            device_id={"tok": t ^ mask, "grp": g}, device_id_type=MESH)
        copy.start()
        token[name, c] = copy

    def first(c):
        ship("far_a", c, p3.at[rows(c), left_cols], far_a.at[rows(c)], 1)
        ship("far_b", c, p3.at[rows(c), right_cols], far_b.at[rows(c)], 2)

    def second(c):
        ship("near_a", c, p1.at[rows(c), left_cols], near_a.at[rows(c)], 1)
        ship("near_b", c, p2.at[rows(c), right_cols], near_b.at[rows(c)], 2)

    def relay(c):
        token["far_a", c].wait_recv()
        value = p2[rows(c), left_cols].astype(F32) + far_a[rows(c), :].astype(F32)
        pass_a[rows(c), :] = value.astype(BF)
        ship("end_a", c, pass_a.at[rows(c)], end_a.at[rows(c)], 2)
        token["far_b", c].wait_recv()
        value = p1[rows(c), right_cols].astype(F32) + far_b[rows(c), :].astype(F32)
        pass_b[rows(c), :] = value.astype(BF)
        ship("end_b", c, pass_b.at[rows(c)], end_b.at[rows(c)], 1)

    def finish(c):
        for near, end in (("near_a", "end_a"), ("near_b", "end_b")):
            token[near, c].wait_recv()
            token[end, c].wait_recv()
        mine = own_in[rows(c), :] + part(0, c)
        token_out[rows(c), left_cols] = (
            mine[:, :half] + near_a[rows(c), :].astype(F32) + end_a[rows(c), :].astype(F32)
        )
        token_out[rows(c), right_cols] = (
            mine[:, half:] + near_b[rows(c), :].astype(F32) + end_b[rows(c), :].astype(F32)
        )

    def away(s):
        return (slice(None),) * s + (1 - digits[s],) + tuple(digits[s + 1:])

    def kept(s):
        return (slice(None),) * s + tuple(digits[s:])

    def add(ref, at, other, dst, to):
        value = ref[at].astype(F32) + other[...].astype(F32)
        dst[to] = value.astype(dst.dtype)

    low = chunks // 2
    for s in reversed(range(nb)):
        head = s == nb - 1
        outer = s >= tb
        sources = [pin_in if head else pin_a, small_in if head else small_a]
        copies = []
        for w in range(2):
            land = landing[w * nb + s]
            i = w * nb + s
            if w == 0 and not outer:
                place = {tb - 1: (place_1, place_0), tb - 2: (place_1, slice(None))}.get(
                    s, (slice(None), slice(None)))
                cut = (slice(None),) * s + (1 - digits[s],) + tuple(digits[s + 1:tb])
                src = quad.at[place + cut]
                copies.append(launch(i, src, src if s >= tb - 2 else land, s))
            else:
                copies.append(launch(i, sources[w].at[away(s)], land, s))
        turn = nb - 1 - s
        if turn == 0:
            for c in range(chunks):
                p3[rows(c), :] = part(3, c).astype(BF)
                if c > 0:
                    first(c - 1)
            for c in range(chunks):
                p2[rows(c), :] = part(2, c).astype(BF)
                if c == 0:
                    first(chunks - 1)
                p1[rows(c), :] = part(1, c).astype(BF)
        elif turn == 1:
            for c in range(low):
                relay(c)
                second(c)
        elif turn == 2:
            for c in range(low, chunks):
                relay(c)
        elif turn == 3:
            for c in range(low, chunks):
                second(c)
        for w in range(2):
            copies[w].wait_recv()
            land = landing[w * nb + s]
            if w == 0 and not outer:
                if s < tb - 2:
                    at = (slice(None), slice(None)) + (slice(None),) * s + tuple(digits[s:tb])
                    add(quad, at, land, quad, at)
            elif w == 0 and s == tb:
                add(sources[0], kept(s), land, quad, (place_1, place_0))
            else:
                dst = (pin_a, small_a)[w]
                add(sources[w], kept(s), land, dst, kept(s))
    pin_out[...] = quad[(slice(None), slice(None)) + tuple(digits[:tb])]
    small_out[...] = small_a[tuple(digits)]
    for c in range(chunks):
        finish(c)
    for copy in flying:
        copy.wait_send()
    for copy in token.values():
        copy.wait_send()


def reduce_small(nt, ng, pin, small, own, grads, spread, chunks=4):
    nb = bits_of(nt) + bits_of(ng)
    tb = bits_of(nt)
    two = (2,) * nb
    r, c = pin.shape[1:]
    rs = small.shape[1:]
    count, width = own.shape
    S = jax.ShapeDtypeStruct
    vm = pl.BlockSpec(memory_space=pltpu.VMEM)
    landing = []
    for w, (shape, dt) in enumerate((((r, c), BF), (rs, F32))):
        for s in range(nb):
            lead = (2,) * s
            if w == 0 and s < tb:
                lead = ((2, 2) + lead) if s < tb - 2 else (1,)
                landing.append(pltpu.VMEM(lead + (shape if s < tb - 2 else (8, 128)), dt))
            else:
                landing.append(pltpu.VMEM(lead + shape, dt))
    return pl.pallas_call(
        functools.partial(reduce_kernel, nt, ng, chunks),
        out_shape=[S((2, 2, r, c), BF), S(rs, F32), S((count, width), F32)],
        in_specs=[vm] * 5,
        out_specs=[vm] * 3,
        scratch_shapes=[
            pltpu.VMEM(two + (r, c), BF), pltpu.VMEM(two + rs, F32),
            pltpu.VMEM((2, 2) + (2,) * tb + (r, c), BF),
        ] + landing + [pltpu.VMEM((count, width // 2), BF)] * 8 + [pltpu.VMEM((count, width), BF)] * 3 + [
            pltpu.SemaphoreType.DMA((2 * nb,)), pltpu.SemaphoreType.DMA((2 * nb,)),
            pltpu.SemaphoreType.DMA((6 * chunks,)), pltpu.SemaphoreType.DMA((6 * chunks,)),
        ],
        compiler_params=pltpu.CompilerParams(collective_id=1, has_side_effects=True, vmem_limit_bytes=VMEM_ALL),
        name="reduce_small",
    )(pin.reshape(two + (r, c)), small.reshape(two + rs), own, grads, spread)


def flip(block, mask):
    count = lax.axis_size("tok")
    return lax.ppermute(block, "tok", [(i, i ^ mask) for i in range(count)])


def gather_all(item):
    return lax.all_gather(item, ("tok", "grp"), axis=0, tiled=True)


def scatter_sum(item):
    return lax.psum_scatter(item, ("tok", "grp"), scatter_dimension=0, tiled=True)


def shards(
    tokens,
    upstream,
    cluster_pos,
    project_in,
    query_bias,
    value_bias,
    project_out,
    output_bias,
    first_gain,
    first_shift,
    expand,
    expand_bias,
    contract,
    contract_bias,
    second_gain,
    second_shift,
):
    inputs = tokens[0]
    count, width = inputs.shape
    positions = cluster_pos[0] % LONG
    heads = positions.shape[0]
    head_dim = width // heads
    span = LONG // count
    mine = heads // span
    offset = lax.axis_index("tok") % span
    total = span * count

    nt = lax.axis_size("tok")
    ng = lax.axis_size("grp")
    devices = nt * ng
    few = query_bias.shape[0]
    strips = expand.shape[1] // width

    pieces = project_in.reshape(few, 3, span, mine, head_dim)
    hollow = jnp.zeros((few, head_dim), BF)
    arranged = []
    for place in range(span):
        columns = []
        for h in range(mine):
            query, key, value = (pieces[:, i, place, h] for i in range(3))
            columns += [hollow, query, value, key] if h == 0 else [query, hollow, key, value]
        arranged.append(jnp.concatenate(columns, axis=1))
    packed = jnp.concatenate(
        [
            query_bias, value_bias, output_bias, first_gain, first_shift,
            contract_bias, second_gain, second_shift, expand_bias,
        ]
    ).astype(F32)
    packed = jnp.pad(packed, (0, 1024 - packed.shape[0])).reshape(8, 128)
    block, own_at, arranged, packed, project_out = collect(
        nt, ng, inputs, positions.reshape(span, mine, count), jnp.stack(arranged), [packed, project_out]
    )
    wide = jnp.concatenate(
        [expand.reshape(few, strips, width).transpose(1, 0, 2).reshape(-1, width), contract], axis=0
    )
    wide, packed = lax.optimization_barrier((wide, packed))
    wide = gather_all(wide[None])
    expand = wide[:, : strips * few].reshape(devices, strips, few, width)
    expand = expand.transpose(1, 0, 2, 3).reshape(strips, width, width)
    contract = wide[:, strips * few :].reshape(strips * width, width)
    block = block.reshape(total, width)
    own_at = own_at.transpose(1, 0, 2).reshape(-1)
    arranged = lax.dynamic_index_in_dim(arranged, offset, 0, False).reshape(width, -1)
    packed = packed.reshape(devices, -1)
    vectors = packed[:, : 8 * few].reshape(devices, 8, few).transpose(1, 0, 2).reshape(8, width)
    expand_bias = packed[:, 8 * few : (8 + strips) * few].reshape(strips, width)
    query_bias, value_bias = vectors[0], vectors[1]
    vectors = jnp.concatenate([vectors[2:], vectors[:2]], axis=0)

    own_query = lax.dynamic_slice_in_dim(query_bias.reshape(heads, head_dim), offset * mine, mine)
    own_value = lax.dynamic_slice_in_dim(value_bias.reshape(heads, head_dim), offset * mine, mine)
    blank = jnp.zeros((head_dim,), F32)
    rows = []
    for h in range(mine):
        parts = [blank, own_query[h], own_value[h], blank] if h == 0 else [own_query[h], blank, blank, own_value[h]]
        rows.append(jnp.concatenate(parts))
    bias_rows = jnp.stack(rows)[:, None]

    *leaving, left, right = fwd(own_at, block, arranged, bias_rows, span)
    came = [leaving[0]] + [flip(leaving[k], k) for k in range(1, span)]
    project_out = project_out.reshape(width, width)
    result, grad_first, *rest = mid(
        came, offset[None].astype(jnp.int32), inputs, upstream[0], project_out, expand, contract,
        vectors, expand_bias,
    )
    sending = rest[:span]
    merged, grad_branch, normed_low, grad_mid, lifted, grad_inner, row_sums, expand_sums = rest[span:]
    landed = [sending[0]] + [flip(sending[k], k) for k in range(1, span)]

    def turn(item):
        item = item.reshape(2, 2, mine * head_dim, width)
        item = jnp.where(offset % 2 == 1, item[:, ::-1], item)
        return jnp.where(offset // 2 == 1, item[::-1], item).reshape(width, width)

    landed, lifted = lax.optimization_barrier((landed, lifted))
    contract_grad = jnp.einsum("rf,rd->fd", lifted, grad_mid, preferred_element_type=F32)
    expand_grad = jnp.einsum("rd,rf->df", normed_low, grad_inner, preferred_element_type=F32)
    turned_grad = jnp.einsum("rd,re->de", merged, grad_branch, preferred_element_type=F32).astype(BF)
    split = span * 2 * head_dim
    project_out_grad = turn(
        jnp.concatenate(
            [
                turned_grad[:split].reshape(span, 2 * head_dim, width),
                turned_grad[split:].reshape(span, head_dim, width),
            ],
            axis=1,
        )
    )
    expand_grad = expand_grad.astype(BF)
    contract_grad = contract_grad.astype(BF)
    wide_grad = jnp.concatenate(
        [project_out_grad.reshape(devices, few, width)]
        + [expand_grad[:, i * width : (i + 1) * width].reshape(devices, few, width) for i in range(strips)]
        + [contract_grad.reshape(devices, strips * few, width)],
        axis=1,
    )
    landed, held = lax.optimization_barrier((landed, wide_grad))
    wide_grad = scatter_sum(wide_grad)[0].astype(F32)
    project_out_grad = wide_grad[:few]
    expand_grad = wide_grad[few : (1 + strips) * few].reshape(strips, few, width).transpose(1, 0, 2).reshape(few, -1)
    contract_grad = wide_grad[(1 + strips) * few :]
    grad_rows, grad_sums = bwd(own_at, left, right, landed)
    arranged_grad = jnp.einsum("rd,re->de", block, grad_rows, preferred_element_type=F32).astype(BF)
    sums = jnp.sum(grad_sums, axis=0).reshape(mine, 4, head_dim)
    query_at = [1] + [0] * (mine - 1)
    key_at = [3] + [2] * (mine - 1)
    value_at = [2] + [3] * (mine - 1)

    def spread(take, at):
        return jnp.stack([take(h, at[h]) for h in range(mine)], axis=-2)

    own_sums = jnp.stack([spread(lambda h, s: sums[h, s], at) for at in (query_at, value_at)])
    bias_grads = lax.dynamic_update_slice_in_dim(
        jnp.zeros((2, heads, head_dim), F32), own_sums, offset * mine, axis=1
    ).reshape(2, width)
    ordered = jnp.concatenate([bias_grads, row_sums[5:6], row_sums[3:5], row_sums[2:3], row_sums[:2]], axis=0)
    small = jnp.concatenate(
        [
            ordered.reshape(8, devices, few).transpose(1, 0, 2).reshape(devices, 8 * few),
            expand_sums.reshape(devices, strips * few),
        ],
        axis=1,
    )
    small = jnp.pad(small, ((0, 0), (0, 1024 - small.shape[1]))).reshape(devices, 8, 128)
    project_in_grad, small, token_grad = reduce_small(
        nt, ng, arranged_grad.reshape(devices, few, -1), small, grad_first, grad_rows, arranged
    )
    project_in_grad = project_in_grad.astype(F32).reshape(span, few, mine, 4, head_dim)
    project_in_grad = jnp.concatenate(
        [
            project_in_grad[place, :, h, at[h]]
            for at in (query_at, key_at, value_at)
            for place in range(span)
            for h in range(mine)
        ],
        axis=1,
    )
    small = small.reshape(-1)
    each = [small[i * few : (i + 1) * few] for i in range(8)] + [small[8 * few : (8 + strips) * few]]
    return (
        result[None],
        token_grad[None],
        project_in_grad,
        each[0],
        each[1],
        project_out_grad,
        each[2],
        each[3],
        each[4],
        expand_grad,
        each[8],
        contract_grad,
        each[5],
        each[6],
        each[7],
    )


def solution(mesh):
    placed = (
        P("grp", "tok", None),
        P("grp", "tok", None),
        P("grp", None, "tok"),
        P(("tok", "grp"), None),
        P(("tok", "grp")),
        P(("tok", "grp")),
        P(("tok", "grp"), None),
        P(("tok", "grp")),
        P(("tok", "grp")),
        P(("tok", "grp")),
        P(("tok", "grp"), None),
        P(("tok", "grp")),
        P(("tok", "grp"), None),
        P(("tok", "grp")),
        P(("tok", "grp")),
        P(("tok", "grp")),
    )
    return jax.shard_map(
        shards,
        mesh=mesh,
        in_specs=placed,
        out_specs=(
            P("grp", "tok", None),
            P("grp", "tok", None),
            P(("tok", "grp"), None),
            P(("tok", "grp")),
            P(("tok", "grp")),
            P(("tok", "grp"), None),
            P(("tok", "grp")),
            P(("tok", "grp")),
            P(("tok", "grp")),
            P(("tok", "grp"), None),
            P(("tok", "grp")),
            P(("tok", "grp"), None),
            P(("tok", "grp")),
            P(("tok", "grp")),
            P(("tok", "grp")),
        ),
        check_vma=False,
    )
```
